32 devices in a mesh: clips: 2 (over y), space: 4 (over z), tm: 2 (over x), chan: 2 (over core).
Axes of the slice: x: 2, y: 2, z: 4, core: 2. Of those that a mesh axis runs over, the one named last changes fastest.
Arguments:
- frames_in: bfloat16 [4, 16, 160, 384], P(('clips', 'tm'), 'space', None, 'chan'), parts along dimension 0, may hold values from -6 to 6
- cache: bfloat16 [4, 16, 160, 384], P('clips', 'space'), parts along dimension 0, may hold values from -6 to 6
- gain_one: bfloat16 [384], replicated, may hold values from 0.099609375 to 1.8984375
- gain_two: bfloat16 [384], replicated, may hold values from 0.099609375 to 1.8984375
- w_query: bfloat16 [384, 384], replicated, may hold values from -10 to 10
- w_key: bfloat16 [384, 384], replicated, may hold values from -10 to 10
- w_value: bfloat16 [384, 384], replicated, may hold values from -0.3125 to 0.3125
- w_out: bfloat16 [384, 384], replicated, may hold values from -0.3125 to 0.3125
- conv_weight: bfloat16 [3, 3, 3, 384, 384], P(None, None, None, None, 'chan'), may hold values from -0.0625 to 0.0625
Outputs:
- decoded: bfloat16 [4, 16, 160, 384], P(('clips', 'tm'), 'space', None, 'chan'), parts along dimension 0
The draws below stay inside these ranges and needn't reach their ends.
There are 2 independent parts, one for each index of `clips`. The reference program is written for one: setup_inputs(seed, part) draws one part's arguments, and reference() takes and returns one part's arrays. A program takes and returns all parts, laid end to end along the dimension named above; an argument that names none is the same for every part. Nothing has to cross between parts.
All inputs are finite; a program needn't handle non-finite values.
Results may differ from the reference program's by a relative error of at most 0.0062.
Values may be sent and summed in bfloat16 or wider, within the bound.
A program may use at most 128 MiB of HBM per device.

```python
import math
import jax
import jax.numpy as jnp
from jax import lax

C = 384
W = 160
F = 2
H = 16


def projection_draw(key, salt):
    scatter = jax.random.truncated_normal(jax.random.fold_in(key, salt), -4.0, 4.0, (C, C), jnp.float32) / math.sqrt(C)
    return (1.75 * scatter).astype(jnp.bfloat16)


def draw_w_query(key, part):
    return projection_draw(key, 11)


def draw_w_key(key, part):
    return projection_draw(key, 13)


def draw_frames_in(key, part):
    return jax.random.truncated_normal(jax.random.fold_in(key, 25), -6.0, 6.0, (F, H, W, C), jnp.float32).astype(jnp.bfloat16)


def steps_of(stream_key, shape, pieces, smallest, high):
    level, own = 1.0, jax.random.fold_in(stream_key, 6)
    for dim, shards_of in pieces:
        draws = jnp.exp(jax.random.uniform(jax.random.fold_in(own, dim), (shards_of,), jnp.float32, smallest / len(pieces), high / len(pieces)))
        level = level * jnp.repeat(draws, shape[dim] // shards_of).reshape([-1 if axis == dim else 1 for axis in range(len(shape))])
    return level


def scatter_about(stream_key, extent, spread, most, cuts=(), held_as=jnp.bfloat16):
    entries = jax.random.normal(stream_key, extent, jnp.float32) * spread
    if len(cuts) > 0:
        entries = steps_of(stream_key, extent, cuts, -0.22, 0.18) * entries
    return jnp.clip(entries, min=-most, max=most).astype(held_as)


def setup_inputs(seed: int = 0, part: int = 0) -> dict:
    key_of = jax.random.split(jax.random.key(seed), 10)
    own_keys = jax.random.split(jax.random.fold_in(key_of[9], part), 10)
    frames_in = draw_frames_in(jax.random.fold_in(jax.random.fold_in(key_of[9], part), 71), part)
    cache = scatter_about(own_keys[1], (2, H, W, C), 1.0, 6.0, ((1, 4),))
    gain_one = jnp.clip(1.0 + 0.18 * jax.random.normal(key_of[2], (C,), jnp.float32), 0.099609375, 1.8984375).astype(jnp.bfloat16)
    gain_two = jnp.clip(1.0 + 0.18 * jax.random.normal(key_of[3], (C,), jnp.float32), 0.099609375, 1.8984375).astype(jnp.bfloat16)
    w_query = draw_w_query(jax.random.fold_in(key_of[9], 71), part)
    w_key = draw_w_key(jax.random.fold_in(key_of[9], 71), part)
    w_value = scatter_about(key_of[6], (C, C), C ** -0.5, 0.3125)
    w_out = scatter_about(key_of[7], (C, C), C ** -0.5, 0.3125)
    conv_weight = scatter_about(key_of[8], (3, 3, 3, C, C), (27 * C) ** -0.5, 0.0625, ((4, 2),))
    return dict(frames_in=frames_in, cache=cache, gain_one=gain_one, gain_two=gain_two, w_query=w_query, w_key=w_key, w_value=w_value, w_out=w_out, conv_weight=conv_weight)


def rms_scaled(values, gain):
    wide = values.astype(jnp.float32)
    factor = lax.rsqrt(lax.optimization_barrier(jnp.mean(wide * wide, axis=-1, keepdims=True)) + 1e-06)
    return wide * factor * gain.astype(jnp.float32)

def frame_attention(frame, gain_one, w_query, w_key, w_value, w_out):
    tokens = frame.reshape(-1, C)
    normed = rms_scaled(tokens, gain_one).astype(jnp.bfloat16)
    query = jnp.dot(normed, w_query, preferred_element_type=jnp.float32).astype(jnp.bfloat16)
    keys = jnp.dot(normed, w_key, preferred_element_type=jnp.float32).astype(jnp.bfloat16)
    values = jnp.dot(normed, w_value, preferred_element_type=jnp.float32).astype(jnp.bfloat16)
    block = math.gcd(tokens.shape[0], 512)
    blocks = query.reshape(-1, block, C)

    def one_block(rows):
        scores = jnp.einsum('qc,kc->qk', rows.astype(jnp.float32), keys.astype(jnp.float32)) * C ** (-0.5)
        top = lax.optimization_barrier(jnp.max(scores, axis=-1, keepdims=True))
        weights = jnp.exp(scores - top)
        total = lax.optimization_barrier(jnp.sum(weights, axis=-1, keepdims=True))
        mixed = jnp.dot(weights.astype(jnp.bfloat16), values, preferred_element_type=jnp.float32) / total
        return mixed.astype(jnp.bfloat16)
    attended = lax.map(one_block, blocks).reshape(-1, C)
    joined = tokens.astype(jnp.float32) + jnp.dot(attended, w_out, preferred_element_type=jnp.float32)
    return joined.astype(jnp.bfloat16).reshape(frame.shape)

def reference(frames_in, cache, gain_one, gain_two, w_query, w_key, w_value, w_out, conv_weight):
    joined = lax.map(lambda frame: frame_attention(frame, gain_one, w_query, w_key, w_value, w_out), frames_in)
    act = jax.nn.silu(rms_scaled(joined, gain_two)).astype(jnp.bfloat16)
    extended = jnp.concatenate([cache, act], axis=0).astype(jnp.float32)
    extended = jnp.pad(extended, ((0, 0), (1, 1), (1, 1), (0, 0)))
    conv = lax.conv_general_dilated(extended[None], conv_weight.astype(jnp.float32), (1, 1, 1), 'VALID', dimension_numbers=('NDHWC', 'DHWIO', 'NDHWC'), precision=lax.Precision.HIGHEST)[0]
    return (joined.astype(jnp.float32) + conv).astype(jnp.bfloat16)
```

```python
import functools
import math

import jax
import jax.numpy as jnp
from jax import lax
from jax.experimental import pallas as pl
from jax.experimental.pallas import tpu as pltpu
from jax.sharding import PartitionSpec as P

F32 = jnp.float32
BF16 = jnp.bfloat16
MESH = pl.DeviceIdType.MESH


def normalized(wide, gain):
    factor = lax.rsqrt(jnp.mean(wide * wide, axis=-1, keepdims=True) + 1e-06)
    return wide * factor * gain


def kernel(
    Z, N,
    x_hbm, cache_hbm, g1_hbm, g2_hbm, wq_hbm, wk_hbm, wv_hbm, wo_hbm, cw_hbm,
    out_ref,
    xo, xg, xn, qk, top, total, acc, cb, hb, jt, jo, parts, g1_ref, g2_ref, ws, wvo, cw,
    s_loc, s_pair, r_pair, s_right, s_left, s_sib, r_z, r_sib,
    s_cache, r_halo, s_edge, s_rest, r_edge, r_rest, s_tm, r_tm, s_half, r_half,
):
    z = lax.axis_index("space")
    c = lax.axis_index("chan")
    tm = lax.axis_index("tm")
    o = 1 - c
    R, W, S = out_ref.shape[1:]
    C = 2 * S
    hr = R // 2
    T = R * W
    hw = W // 2
    L = 128
    E = S - L
    blocks = ((0, 0, L), (S, L, L), (L, 2 * L, E), (S + L, 2 * L + E, E))

    def dev(dz=None, core=None, frame=None):
        return {
            "space": z if dz is None else dz,
            "chan": c if core is None else core,
            "tm": tm if frame is None else frame,
        }

    def send(src, dst, ssem, rsem, to):
        return pltpu.make_async_remote_copy(
            src_ref=src, dst_ref=dst, send_sem=ssem, recv_sem=rsem,
            device_id=to, device_id_type=MESH,
        )

    near = z + 2 * c - 1
    has_near = jnp.logical_and(near >= 0, near < Z)

    barrier = pltpu.get_barrier_semaphore()

    def greet(to):
        pl.semaphore_signal(barrier, inc=1, device_id=to, device_id_type=MESH)

    greet(dev(core=o))
    pl.when(z > 0)(lambda: greet(dev(dz=z - 1)))
    pl.when(z < Z - 1)(lambda: greet(dev(dz=z + 1)))
    pl.when(has_near)(lambda: greet(dev(dz=near, core=o)))
    for hop in (1, 2):
        if N > hop:
            pl.when(tm >= hop)(functools.partial(lambda h: greet(dev(frame=tm - h)), hop))

    x_own = pltpu.make_async_copy(x_hbm.at[0], xo, s_loc.at[0])
    x_own.start()
    gains = [
        pltpu.make_async_copy(a, b, s_loc.at[1 + i])
        for i, (a, b) in enumerate(((g1_hbm, g1_ref), (g2_hbm, g2_ref)))
    ]
    for g in gains:
        g.start()
    for i, w_hbm in enumerate((wq_hbm, wk_hbm, wv_hbm)):
        for src, dst, count in blocks:
            pltpu.make_async_copy(w_hbm.at[pl.ds(src, count)], ws.at[i, pl.ds(dst, count)], s_loc.at[3]).start()
    pltpu.make_async_copy(wo_hbm, ws.at[3], s_loc.at[3]).start()
    taps_own = pltpu.make_async_copy(cw_hbm, cw, s_loc.at[4])
    taps_own.start()
    first = jnp.minimum(tm, 1)
    cache_two = pltpu.make_async_copy(cache_hbm.at[first], cb.at[0, pl.ds(1, R)], s_loc.at[5])
    cache_one = pltpu.make_async_copy(cache_hbm.at[1], cb.at[1, pl.ds(1, R)], s_loc.at[6])
    pl.when(tm <= 1)(cache_two.start)
    pl.when(tm == 0)(cache_one.start)

    blank = jnp.zeros((W, C), BF16)
    for f in range(3):
        cb[f, 0] = blank
        cb[f, R + 1] = blank

    x_own.wait()
    for k in range(hr):
        a, b = xo[2 * k], xo[2 * k + 1]
        xg[z, k, c] = jnp.concatenate([a[:, :L], b[:, :L], a[:, L:], b[:, L:]], axis=-1)

    want = 1 + jnp.where(z > 0, 1, 0) + jnp.where(z < Z - 1, 1, 0) + jnp.where(has_near, 1, 0)
    for hop in (1, 2):
        if N > hop:
            want = want + jnp.where(tm + hop < N, 1, 0)
    pl.semaphore_wait(barrier, want)

    def rightward(j, k):
        return send(xg.at[j, k, c], xg.at[j, k, c], s_right.at[k], r_z.at[j, k], dev(dz=z + 1))

    def leftward(j, k):
        return send(xg.at[j, k, c], xg.at[j, k, c], s_left.at[k], r_z.at[j, k], dev(dz=z - 1))

    def sideward(j, k, flow):
        return send(xg.at[j, k, c], xg.at[j, k, c], s_sib.at[flow, k], r_sib.at[j, k], dev(core=o))

    for k in range(hr):
        pl.when(z < Z - 1)(rightward(z, k).start)
        pl.when(z > 0)(leftward(z, k).start)
        sideward(z, k, 0).start()

    gains[0].wait()
    gain_one = g1_ref[...].astype(F32).reshape(1, C)
    gain_one = jnp.concatenate([gain_one[:, at : at + count] for at, _, count in blocks], axis=-1)
    low_lanes = lax.broadcasted_iota(jnp.int32, (W, L), 1) < E

    def tokens(j, k):
        p, q = xg[j, k, 0].astype(F32), xg[j, k, 1].astype(F32)
        pt, qt = p[:, 2 * L :], q[:, 2 * L :]
        even = jnp.where(low_lanes, pt, pltpu.roll(qt, E, 1))
        odd = jnp.where(low_lanes, pltpu.roll(pt, E, 1), qt)
        return jnp.concatenate([
            jnp.concatenate([p[:, :L], q[:, :L], even], axis=-1),
            jnp.concatenate([p[:, L : 2 * L], q[:, L : 2 * L], odd], axis=-1),
        ], axis=0)

    def normed(wide):
        return normalized(wide, gain_one).astype(BF16)

    top[...] = jnp.full(top.shape, -1e30, F32)
    total[...] = jnp.zeros(total.shape, F32)
    acc[...] = jnp.zeros(acc.shape, F32)

    def attend(keys):
        scores = lax.dot_general(qk[...], keys, (((1,), (1,)), ((), ())), preferred_element_type=F32)
        old = top[...]
        new = jnp.maximum(old, jnp.max(scores, axis=-1, keepdims=True))
        weight = jnp.exp2(scores - new)
        fade = jnp.exp2(old - new)
        top[...] = new
        total[...] = total[...] * fade + jnp.sum(weight, axis=-1, keepdims=True)
        acc[...] = acc[...] * fade + jnp.dot(weight.astype(BF16), keys, preferred_element_type=F32)

    for k in range(hr):
        sideward(z, k, 0).wait_recv()
    pltpu.make_async_copy(ws, ws, s_loc.at[3]).wait()
    mine = tokens(z, c)
    xn[...] = jnp.concatenate(
        [mine[:, :L], mine[:, 2 * L : 2 * L + E], mine[:, L : 2 * L], mine[:, 2 * L + E :]], axis=-1
    ).astype(BF16)
    keys = normed(mine)
    query = jnp.dot(keys, ws[0], preferred_element_type=F32).astype(BF16)
    folded = lax.dot_general(query, ws[1], (((1,), (1,)), ((), ())), preferred_element_type=F32)
    qk[...] = (folded * (C ** (-0.5) * math.log2(math.e))).astype(BF16)
    attend(keys)
    attend(normed(tokens(z, o)))
    wvo[...] = jnp.dot(ws[2], ws[3], preferred_element_type=F32).astype(BF16)

    def piece(f, dw, start):
        rows = jnp.concatenate([cb[f, dh : dh + R].reshape(T, C) for dh in range(3)], axis=-1)
        kernel_rows = jnp.concatenate([cw[f, dh, dw] for dh in range(3)], axis=-1)
        value = lax.dot_general(rows, kernel_rows, (((1,), (1,)), ((), ())), preferred_element_type=F32)
        if start:
            parts[dw, pl.ds(8, T)] = value
        else:
            parts[dw, pl.ds(8, T)] += value

    def early(i):
        f, dw = divmod(i, 3)
        pl.when(tm <= 1 - f)(lambda: piece(f, dw, f == 0))

    taps_own.wait()
    pl.when(tm <= 1)(cache_two.wait)
    pl.when(tm == 0)(cache_one.wait)
    early(0)

    def cache_edge(f, side):
        row = R - 1 if side == 0 else 0
        cells = pl.ds(pl.multiple_of(c * hw, hw), hw)
        source = cache_hbm.at[first if f == 0 else 1, row, cells]
        to = dev(dz=z + 1) if side == 0 else dev(dz=z - 1)
        return send(source, hb.at[f, side, cells], s_cache.at[f, side], r_halo.at[f, side], to)

    def cache_edges(act):
        for side, there in ((0, z < Z - 1), (1, z > 0)):
            pl.when(jnp.logical_and(there, tm <= 1))(lambda s=side: act(cache_edge(0, s)))
            pl.when(jnp.logical_and(there, tm == 0))(lambda s=side: act(cache_edge(1, s)))

    slots = 5
    def step(d, carry):
        lo, hi = z - d, z + d
        has_lo, has_hi = lo >= 0, hi < Z

        for k in range(hr):

            @pl.when(has_lo)
            def _():
                rightward(lo, k).wait_recv()

                @pl.when(z < Z - 1)
                def _():
                    rightward(lo, k).wait_send()
                    rightward(lo, k).start()

                sideward(lo, k, 0).wait_send()
                sideward(lo, k, 0).start()

            @pl.when(has_hi)
            def _():
                leftward(hi, k).wait_recv()

                @pl.when(z > 0)
                def _():
                    leftward(hi, k).wait_send()
                    leftward(hi, k).start()

                pl.when(d > 1)(sideward(hi, k, 1).wait_send)
                sideward(hi, k, 1).start()

            if k == hr - 1:
                pl.when(d == Z - 1)(lambda: cache_edges(lambda copy: copy.start()))

            @pl.when(has_lo)
            def _():
                sideward(lo, k, 0).wait_recv()
                attend(normed(tokens(lo, k)))

            @pl.when(has_hi)
            def _():
                sideward(hi, k, 1).wait_recv()
                attend(normed(tokens(hi, k)))

            for i in range(slots):
                if i % hr == k and i // hr + 1 < Z:
                    pl.when(d == i // hr + 1)(functools.partial(early, i + 1))

        return carry

    lax.fori_loop(1, Z, step, 0)
    for i in range(slots):
        if i // hr + 1 >= Z:
            early(i + 1)

    gains[1].wait()
    gain_two = g2_ref[...].astype(F32).reshape(1, C)

    def finish_rows(row, count):
        at = pl.ds(pl.multiple_of(row * W, W), count * W)
        mixed = (acc[at, :] * (1.0 / total[at, :])).astype(BF16)
        joined = xn[at, :].astype(F32) + jnp.dot(mixed, wvo[...], preferred_element_type=F32)
        joined = joined.astype(BF16).astype(F32)
        scaled = normalized(joined, gain_two)
        act = (scaled / (1.0 + jnp.exp(-scaled))).astype(BF16)
        cb[2, pl.ds(1 + c * hr + row, count)] = act.reshape(count, W, C)
        low, high = joined[:, :S].astype(BF16), joined[:, S:].astype(BF16)
        jo[pl.ds(c * hr + row, count)] = jnp.where(c == 0, low, high).reshape(count, W, S)
        jt[pl.ds(row, count)] = jnp.where(c == 0, high, low).reshape(count, W, S)

    edge = jnp.where(c == 0, 1, R)
    rest = jnp.where(c == 0, 2, 1 + hr)
    far = jnp.where(c == 0, 1, 0)

    def along_tm(hop, part):
        row = cb.at[2, edge] if part == 0 else cb.at[2, pl.ds(rest, hr - 1)]
        there = cb.at[2 - hop, edge] if part == 0 else cb.at[2 - hop, pl.ds(rest, hr - 1)]
        return send(row, there, s_tm.at[hop - 1, part], r_tm.at[hop - 1, part], dev(frame=tm + hop))

    def edge_copy(f, k):
        src = cb.at[f, edge]
        if k == 0:
            return send(src, src, s_edge.at[2 - f, 0], r_edge.at[2 - f], dev(core=o))
        cells = pl.ds((k - 1) * hw, hw)
        return send(
            cb.at[f, edge, cells], hb.at[f, far, cells], s_edge.at[2 - f, k], r_halo.at[f, o],
            dev(dz=near, core=k - 1),
        )

    def rest_copy(f):
        src = cb.at[f, pl.ds(rest, hr - 1)]
        return send(src, src, s_rest.at[2 - f], r_rest.at[2 - f], dev(core=o))

    def from_sibling(f):
        there = jnp.where(c == 0, R, 1)
        others = jnp.where(c == 0, 1 + hr, 2)
        row = cb.at[f, there]
        send(row, row, s_edge.at[2 - f, 0], r_edge.at[2 - f], dev(core=o)).wait_recv()
        rows = cb.at[f, pl.ds(others, hr - 1)]
        send(rows, rows, s_rest.at[2 - f], r_rest.at[2 - f], dev(core=o)).wait_recv()

    def halo_half(f, side, core):
        half_row = hb.at[f, side, pl.ds(pl.multiple_of(core * hw, hw), hw)]
        return send(half_row, half_row, s_half.at[f, side], r_half.at[f, side], dev(core=o))

    def both_sides(visit):
        pl.when(z > 0)(lambda: visit(0))
        pl.when(z < Z - 1)(lambda: visit(1))

    def relay_halo(f):
        def visit(side):
            half_row = hb.at[f, side, pl.ds(pl.multiple_of(c * hw, hw), hw)]
            send(half_row, half_row, s_half.at[f, side], r_halo.at[f, side], dev(core=o)).wait_recv()
            halo_half(f, side, c).start()

        both_sides(visit)

    def spread_edge(f):
        edge_copy(f, 0).start()

        @pl.when(has_near)
        def _():
            edge_copy(f, 1).start()
            edge_copy(f, 2).start()

    for part in (0, 1):
        if part == 0:
            finish_rows(edge - 1 - c * hr, 1)
        else:
            finish_rows(rest - 1 - c * hr, hr - 1)
        for hop in (1, 2):
            if N > hop:
                pl.when(tm + hop < N)(along_tm(hop, part).start)
        if part == 0:
            spread_edge(2)
        else:
            rest_copy(2).start()

    joined_copy = send(jt, jo.at[pl.ds(c * hr, hr)], s_pair, r_pair, dev(core=o))
    joined_copy.start()

    def taps(f, start):
        for dw in range(3):
            piece(f, dw, start)

    def forwarded(f, part):
        along_tm(2 - f, part).wait_recv()
        if part == 0:
            spread_edge(f)
        else:
            rest_copy(f).start()

    pl.when(tm <= 1)(lambda: relay_halo(0))
    pl.when(tm == 0)(lambda: relay_halo(1))
    from_sibling(2)
    if N > 2:
        pl.when(tm <= 1)(lambda: taps(2, False))
        pl.when(tm >= 2)(lambda: taps(2, True))
    else:
        taps(2, False)

    if N > 1:

        @pl.when(tm >= 1)
        def _():
            forwarded(1, 0)
            forwarded(1, 1)
            relay_halo(2)
            from_sibling(1)
            taps(1, False)
            relay_halo(1)

        pl.when(tm == 0)(lambda: relay_halo(2))
    else:
        relay_halo(2)
    if N > 2:

        @pl.when(tm >= 2)
        def _():
            forwarded(0, 0)
            forwarded(0, 1)
            from_sibling(0)
            taps(0, False)
            relay_halo(0)

    def from_halo(side):
        for f in range(3):
            halo_half(f, side, o).wait_recv()
        rows = jnp.concatenate([hb[f, side] for f in range(3)], axis=-1)
        for dw in range(3):
            kernel_rows = jnp.concatenate([cw[f, 2 * side, dw] for f in range(3)], axis=-1)
            parts[dw, pl.ds(8 + side * (T - W), W)] += lax.dot_general(
                rows, kernel_rows, (((1,), (1,)), ((), ())), preferred_element_type=F32
            )

    both_sides(from_halo)

    there = jo.at[pl.ds(o * hr, hr)]
    send(jt, there, s_pair, r_pair, dev(core=o)).wait_recv()
    cell = lax.rem(lax.broadcasted_iota(jnp.int32, (T, S), 0), W)
    before = jnp.where(cell == 0, 0.0, parts[0, pl.ds(7, T)])
    after = jnp.where(cell == W - 1, 0.0, parts[2, pl.ds(9, T)])
    conv = before + parts[1, pl.ds(8, T)] + after
    out_ref[0] = (jo[...].reshape(T, S).astype(F32) + conv).astype(BF16).reshape(R, W, S)

    joined_copy.wait_send()
    for k in range(hr):
        pl.when(z < Z - 1)(rightward(z, k).wait_send)
        pl.when(z > 0)(leftward(z, k).wait_send)
        sideward(z, k, 0).wait_send()
        pl.when(z < Z - 1)(sideward(z, k, 1).wait_send)
    cache_edges(lambda copy: copy.wait_send())
    for f in range(3):
        both_sides(lambda side: halo_half(f, side, c).wait_send())
    for part in (0, 1):
        for hop in (1, 2):
            if N > hop:
                pl.when(tm + hop < N)(along_tm(hop, part).wait_send)

    def spread_done(f):
        edge_copy(f, 0).wait_send()
        rest_copy(f).wait_send()

        @pl.when(has_near)
        def _():
            edge_copy(f, 1).wait_send()
            edge_copy(f, 2).wait_send()

    spread_done(2)
    if N > 1:
        pl.when(tm >= 1)(lambda: spread_done(1))
    if N > 2:
        pl.when(tm >= 2)(lambda: spread_done(0))


def solution(mesh):
    Z, N = mesh.shape["space"], mesh.shape["tm"]

    def body(frames_in, cache, gain_one, gain_two, w_query, w_key, w_value, w_out, conv_weight):
        _, R, W, S = frames_in.shape
        C = 2 * S
        hr, half, T = R // 2, R // 2 * W, R * W
        hops, sets = max(1, min(2, N - 1)), min(3, N)
        dma = pltpu.SemaphoreType.DMA
        hbm = pl.BlockSpec(memory_space=pltpu.HBM)
        vmem = pl.BlockSpec(memory_space=pltpu.VMEM)
        return pl.pallas_call(
            functools.partial(kernel, Z, N),
            out_shape=jax.ShapeDtypeStruct(frames_in.shape, BF16),
            in_specs=[hbm] * 9,
            out_specs=vmem,
            scratch_shapes=[
                pltpu.VMEM((R, W, S), BF16),
                pltpu.VMEM((Z, hr, 2, W, C), BF16),
                pltpu.VMEM((half, C), BF16),
                pltpu.VMEM((half, C), BF16),
                pltpu.VMEM((half, 1), F32),
                pltpu.VMEM((half, 1), F32),
                pltpu.VMEM((half, C), F32),
                pltpu.VMEM((3, R + 2, W, C), BF16),
                pltpu.VMEM((3, 2, W, C), BF16),
                pltpu.VMEM((hr, W, S), BF16),
                pltpu.VMEM((R, W, S), BF16),
                pltpu.VMEM((3, T + 16, S), F32),
                pltpu.VMEM((C,), BF16),
                pltpu.VMEM((C,), BF16),
                pltpu.VMEM((4, C, C), BF16),
                pltpu.VMEM((C, C), BF16),
                pltpu.VMEM((3, 3, 3, S, C), BF16),
                dma((7,)),
                dma,
                dma,
                dma((hr,)),
                dma((hr,)),
                dma((2, hr)),
                dma((Z, hr)),
                dma((Z, hr)),
                dma((2, 2)),
                dma((3, 2)),
                dma((sets, 3)),
                dma((sets,)),
                dma((sets,)),
                dma((sets,)),
                dma((hops, 2)),
                dma((hops, 2)),
                dma((3, 2)),
                dma((3, 2)),
            ],
            compiler_params=pltpu.CompilerParams(
                collective_id=0, has_side_effects=True, vmem_limit_bytes=50 << 20
            ),
        )(*(pltpu.with_memory_space_constraint(a, pltpu.HBM) for a in (
            frames_in, cache, gain_one, gain_two,
            w_query, w_key, w_value, w_out, jnp.swapaxes(conv_weight, 3, 4),
        )))

    return jax.shard_map(
        body,
        mesh=mesh,
        in_specs=(
            P(("clips", "tm"), "space", None, "chan"),
            P("clips", "space", None, None),
            P(),
            P(),
            P(),
            P(),
            P(),
            P(),
            P(None, None, None, None, "chan"),
        ),
        out_specs=P(("clips", "tm"), "space", None, "chan"),
        check_vma=False,
    )
```

```python
import functools
import math

import jax
import jax.numpy as jnp
from jax import lax
from jax.experimental import pallas as pl
from jax.experimental.pallas import tpu as pltpu
from jax.sharding import PartitionSpec as P

F32 = jnp.float32
BF16 = jnp.bfloat16
MESH = pl.DeviceIdType.MESH


def normalized(wide, gain):
    factor = lax.rsqrt(jnp.mean(wide * wide, axis=-1, keepdims=True) + 1e-06)
    return wide * factor * gain


def kernel(
    Z, N,
    x_hbm, cache_hbm, g1_hbm, g2_hbm, wq_hbm, wk_hbm, wv_hbm, wo_hbm, cw_hbm,
    out_ref,
    xo, xg, xn, qk, top, total, acc, cb, hb, jt, jo, parts, g1_ref, g2_ref, ws, wvo, cw,
    s_loc, s_pair, r_pair, s_right, s_left, s_sib, r_z, r_sib,
    s_cache, r_halo, s_near, s_edge, s_rest, r_edge, r_rest, s_tm, r_tm, s_half,
):
    z = lax.axis_index("space")
    c = lax.axis_index("chan")
    tm = lax.axis_index("tm")
    o = 1 - c
    R, W, S = out_ref.shape[1:]
    C = 2 * S
    hr = R // 2
    T = R * W
    L = 128
    E = S - L
    blocks = ((0, 0, L), (S, L, L), (L, 2 * L, E), (S + L, 2 * L + E, E))

    def dev(dz=None, core=None, frame=None):
        return {
            "space": z if dz is None else dz,
            "chan": c if core is None else core,
            "tm": tm if frame is None else frame,
        }

    def send(src, dst, ssem, rsem, to):
        return pltpu.make_async_remote_copy(
            src_ref=src, dst_ref=dst, send_sem=ssem, recv_sem=rsem,
            device_id=to, device_id_type=MESH,
        )

    near, back = z + 2 * c - 1, z + 1 - 2 * c
    has_near = jnp.logical_and(near >= 0, near < Z)
    has_back = jnp.logical_and(back >= 0, back < Z)

    barrier = pltpu.get_barrier_semaphore()

    def greet(to):
        pl.semaphore_signal(barrier, inc=1, device_id=to, device_id_type=MESH)

    greet(dev(core=o))
    pl.when(z > 0)(lambda: greet(dev(dz=z - 1)))
    pl.when(z < Z - 1)(lambda: greet(dev(dz=z + 1)))
    for hop in (1, 2):
        if N > hop:
            pl.when(tm >= hop)(functools.partial(lambda h: greet(dev(frame=tm - h)), hop))

    x_own = pltpu.make_async_copy(x_hbm.at[0], xo, s_loc.at[0])
    x_own.start()
    gains = [
        pltpu.make_async_copy(a, b, s_loc.at[1 + i])
        for i, (a, b) in enumerate(((g1_hbm, g1_ref), (g2_hbm, g2_ref)))
    ]
    for g in gains:
        g.start()
    for i, w_hbm in enumerate((wq_hbm, wk_hbm, wv_hbm)):
        for src, dst, count in blocks:
            pltpu.make_async_copy(w_hbm.at[pl.ds(src, count)], ws.at[i, pl.ds(dst, count)], s_loc.at[3]).start()
    pltpu.make_async_copy(wo_hbm, ws.at[3], s_loc.at[3]).start()
    taps_own = pltpu.make_async_copy(cw_hbm, cw, s_loc.at[4])
    taps_own.start()
    first = jnp.minimum(tm, 1)
    cache_two = pltpu.make_async_copy(cache_hbm.at[first], cb.at[0, pl.ds(1, R)], s_loc.at[5])
    cache_one = pltpu.make_async_copy(cache_hbm.at[1], cb.at[1, pl.ds(1, R)], s_loc.at[6])
    pl.when(tm <= 1)(cache_two.start)
    pl.when(tm == 0)(cache_one.start)

    blank = jnp.zeros((W, C), BF16)
    for f in range(3):
        cb[f, 0] = blank
        cb[f, R + 1] = blank

    x_own.wait()
    for k in range(hr):
        a, b = xo[2 * k], xo[2 * k + 1]
        xg[z, k, c] = jnp.concatenate([a[:, :L], b[:, :L], a[:, L:], b[:, L:]], axis=-1)

    want = 1 + jnp.where(z > 0, 1, 0) + jnp.where(z < Z - 1, 1, 0)
    for hop in (1, 2):
        if N > hop:
            want = want + jnp.where(tm + hop < N, 1, 0)
    pl.semaphore_wait(barrier, want)

    def rightward(j, k):
        return send(xg.at[j, k, c], xg.at[j, k, c], s_right.at[k], r_z.at[j, k], dev(dz=z + 1))

    def leftward(j, k):
        return send(xg.at[j, k, c], xg.at[j, k, c], s_left.at[k], r_z.at[j, k], dev(dz=z - 1))

    def sideward(j, k, flow):
        return send(xg.at[j, k, c], xg.at[j, k, c], s_sib.at[flow, k], r_sib.at[j, k], dev(core=o))

    for k in range(hr):
        pl.when(z < Z - 1)(rightward(z, k).start)
        pl.when(z > 0)(leftward(z, k).start)
        sideward(z, k, 0).start()

    gains[0].wait()
    gain_one = g1_ref[...].astype(F32).reshape(1, C)
    gain_one = jnp.concatenate([gain_one[:, at : at + count] for at, _, count in blocks], axis=-1)
    low_lanes = lax.broadcasted_iota(jnp.int32, (W, L), 1) < E

    def tokens(j, k):
        p, q = xg[j, k, 0].astype(F32), xg[j, k, 1].astype(F32)
        pt, qt = p[:, 2 * L :], q[:, 2 * L :]
        even = jnp.where(low_lanes, pt, pltpu.roll(qt, E, 1))
        odd = jnp.where(low_lanes, pltpu.roll(pt, E, 1), qt)
        return jnp.concatenate([
            jnp.concatenate([p[:, :L], q[:, :L], even], axis=-1),
            jnp.concatenate([p[:, L : 2 * L], q[:, L : 2 * L], odd], axis=-1),
        ], axis=0)

    def normed(wide):
        return normalized(wide, gain_one).astype(BF16)

    top[...] = jnp.full(top.shape, -1e30, F32)
    total[...] = jnp.zeros(total.shape, F32)
    acc[...] = jnp.zeros(acc.shape, F32)

    def attend(keys):
        scores = lax.dot_general(qk[...], keys, (((1,), (1,)), ((), ())), preferred_element_type=F32)
        old = top[...]
        new = jnp.maximum(old, jnp.max(scores, axis=-1, keepdims=True))
        weight = jnp.exp2(scores - new)
        fade = jnp.exp2(old - new)
        top[...] = new
        total[...] = total[...] * fade + jnp.sum(weight, axis=-1, keepdims=True)
        acc[...] = acc[...] * fade + jnp.dot(weight.astype(BF16), keys, preferred_element_type=F32)

    for k in range(hr):
        sideward(z, k, 0).wait_recv()
    pltpu.make_async_copy(ws, ws, s_loc.at[3]).wait()
    mine = tokens(z, c)
    xn[...] = jnp.concatenate(
        [mine[:, :L], mine[:, 2 * L : 2 * L + E], mine[:, L : 2 * L], mine[:, 2 * L + E :]], axis=-1
    ).astype(BF16)
    keys = normed(mine)
    query = jnp.dot(keys, ws[0], preferred_element_type=F32).astype(BF16)
    folded = lax.dot_general(query, ws[1], (((1,), (1,)), ((), ())), preferred_element_type=F32)
    qk[...] = (folded * (C ** (-0.5) * math.log2(math.e))).astype(BF16)
    attend(keys)
    attend(normed(tokens(z, o)))
    wvo[...] = jnp.dot(ws[2], ws[3], preferred_element_type=F32).astype(BF16)

    def piece(f, dw, start):
        rows = jnp.concatenate([cb[f, dh : dh + R].reshape(T, C) for dh in range(3)], axis=-1)
        kernel_rows = jnp.concatenate([cw[f, dh, dw] for dh in range(3)], axis=-1)
        value = lax.dot_general(rows, kernel_rows, (((1,), (1,)), ((), ())), preferred_element_type=F32)
        if start:
            parts[dw, pl.ds(8, T)] = value
        else:
            parts[dw, pl.ds(8, T)] += value

    def early(i):
        f, dw = divmod(i, 3)
        pl.when(tm <= 1 - f)(lambda: piece(f, dw, f == 0))

    taps_own.wait()
    pl.when(tm <= 1)(cache_two.wait)
    pl.when(tm == 0)(cache_one.wait)
    early(0)

    def cache_edge(f):
        row = jnp.where(c == 0, 0, R - 1)
        source = cache_hbm.at[first if f == 0 else 1, row]
        return send(source, hb.at[f, o], s_cache.at[f], r_halo.at[f, o], dev(dz=near))

    def cache_edges(act):
        pl.when(jnp.logical_and(has_near, tm <= 1))(lambda: act(cache_edge(0)))
        pl.when(jnp.logical_and(has_near, tm == 0))(lambda: act(cache_edge(1)))

    ahead = Z - 1 - z
    longer = jnp.maximum(z, ahead)
    sign = jnp.where(ahead >= z, 1, -1)
    edges_at = jnp.minimum(jnp.where(c == 0, ahead, z) + 1, Z - 1)
    slots = 5
    def step(d, carry):
        lo, hi = z - d, z + d
        has_lo, has_hi = lo >= 0, hi < Z

        for k in range(hr):

            @pl.when(has_lo)
            def _():
                rightward(lo, k).wait_recv()

                @pl.when(z < Z - 1)
                def _():
                    rightward(lo, k).wait_send()
                    rightward(lo, k).start()

                sideward(lo, k, 0).wait_send()
                sideward(lo, k, 0).start()

            @pl.when(has_hi)
            def _():
                leftward(hi, k).wait_recv()

                @pl.when(z > 0)
                def _():
                    leftward(hi, k).wait_send()
                    leftward(hi, k).start()

                pl.when(d > 1)(sideward(hi, k, 1).wait_send)
                sideward(hi, k, 1).start()

            if k == hr - 1:
                pl.when(d == edges_at)(lambda: cache_edges(lambda copy: copy.start()))

            for i in range(slots):
                if i % hr == k and i // hr + 1 < Z:
                    pl.when(d == i // hr + 1)(functools.partial(early, i + 1))

            j = z + jnp.where(d <= longer, sign * d, sign * (longer - d))
            sideward(j, k, 0).wait_recv()
            attend(normed(tokens(j, k)))

        return carry

    lax.fori_loop(1, Z, step, 0)
    for i in range(slots):
        if i // hr + 1 >= Z:
            early(i + 1)

    gains[1].wait()
    gain_two = g2_ref[...].astype(F32).reshape(1, C)

    def finish_rows(row, count):
        at = pl.ds(pl.multiple_of(row * W, W), count * W)
        mixed = (acc[at, :] * (1.0 / total[at, :])).astype(BF16)
        joined = xn[at, :].astype(F32) + jnp.dot(mixed, wvo[...], preferred_element_type=F32)
        joined = joined.astype(BF16).astype(F32)
        scaled = normalized(joined, gain_two)
        act = (scaled / (1.0 + jnp.exp(-scaled))).astype(BF16)
        cb[2, pl.ds(1 + c * hr + row, count)] = act.reshape(count, W, C)
        low, high = joined[:, :S].astype(BF16), joined[:, S:].astype(BF16)
        jo[pl.ds(c * hr + row, count)] = jnp.where(c == 0, low, high).reshape(count, W, S)
        jt[pl.ds(row, count)] = jnp.where(c == 0, high, low).reshape(count, W, S)

    edge = jnp.where(c == 0, 1, R)
    rest = jnp.where(c == 0, 2, 1 + hr)
    def along_tm(hop, part):
        row = cb.at[2, edge] if part == 0 else cb.at[2, pl.ds(rest, hr - 1)]
        there = cb.at[2 - hop, edge] if part == 0 else cb.at[2 - hop, pl.ds(rest, hr - 1)]
        return send(row, there, s_tm.at[hop - 1, part], r_tm.at[hop - 1, part], dev(frame=tm + hop))

    def edge_copy(f):
        src = cb.at[f, edge]
        return send(src, src, s_edge.at[2 - f], r_edge.at[2 - f], dev(core=o))

    def near_copy(hop):
        return send(
            cb.at[2, edge], hb.at[2 - hop, o], s_near.at[hop], r_halo.at[2 - hop, o],
            dev(dz=near, frame=tm + hop),
        )

    def near_copies(act):
        for hop in range(min(3, N)):
            pl.when(jnp.logical_and(has_near, tm + hop < N))(functools.partial(lambda h: act(near_copy(h)), hop))

    def rest_copy(f):
        src = cb.at[f, pl.ds(rest, hr - 1)]
        return send(src, src, s_rest.at[2 - f], r_rest.at[2 - f], dev(core=o))

    def from_sibling(f):
        there = jnp.where(c == 0, R, 1)
        others = jnp.where(c == 0, 1 + hr, 2)
        row = cb.at[f, there]
        send(row, row, s_edge.at[2 - f], r_edge.at[2 - f], dev(core=o)).wait_recv()
        rows = cb.at[f, pl.ds(others, hr - 1)]
        send(rows, rows, s_rest.at[2 - f], r_rest.at[2 - f], dev(core=o)).wait_recv()

    def relay(f):
        row = hb.at[f, o]
        return send(row, row, s_half.at[f], r_halo.at[f, o], dev(core=o))

    def relay_halo(f):
        @pl.when(has_back)
        def _():
            relay(f).wait_recv()
            relay(f).start()

    def both_sides(visit):
        pl.when(z > 0)(lambda: visit(0))
        pl.when(z < Z - 1)(lambda: visit(1))

    for part in (0, 1):
        if part == 0:
            finish_rows(edge - 1 - c * hr, 1)
        else:
            finish_rows(rest - 1 - c * hr, hr - 1)
        for hop in (1, 2):
            if N > hop:
                pl.when(tm + hop < N)(along_tm(hop, part).start)
        if part == 0:
            edge_copy(2).start()
            near_copies(lambda copy: copy.start())
        else:
            rest_copy(2).start()

    joined_copy = send(jt, jo.at[pl.ds(c * hr, hr)], s_pair, r_pair, dev(core=o))
    joined_copy.start()

    def taps(f, start):
        for dw in range(3):
            piece(f, dw, start)

    def forwarded(f, part):
        along_tm(2 - f, part).wait_recv()
        if part == 0:
            edge_copy(f).start()
        else:
            rest_copy(f).start()

    from_sibling(2)
    if N > 2:
        pl.when(tm <= 1)(lambda: taps(2, False))
        pl.when(tm >= 2)(lambda: taps(2, True))
    else:
        taps(2, False)

    if N > 1:

        @pl.when(tm >= 1)
        def _():
            forwarded(1, 0)
            forwarded(1, 1)
            from_sibling(1)
            taps(1, False)

    if N > 2:

        @pl.when(tm >= 2)
        def _():
            forwarded(0, 0)
            forwarded(0, 1)
            from_sibling(0)
            taps(0, False)

    for f in range(3):
        relay_halo(f)
    for f in range(3):
        row = hb.at[f, c]
        pl.when(has_near)(send(row, row, s_half.at[f], r_halo.at[f, c], dev(core=o)).wait_recv)

    def from_halo(side):
        rows = jnp.concatenate([hb[f, side] for f in range(3)], axis=-1)
        for dw in range(3):
            kernel_rows = jnp.concatenate([cw[f, 2 * side, dw] for f in range(3)], axis=-1)
            parts[dw, pl.ds(8 + side * (T - W), W)] += lax.dot_general(
                rows, kernel_rows, (((1,), (1,)), ((), ())), preferred_element_type=F32
            )

    both_sides(from_halo)

    there = jo.at[pl.ds(o * hr, hr)]
    send(jt, there, s_pair, r_pair, dev(core=o)).wait_recv()
    cell = lax.rem(lax.broadcasted_iota(jnp.int32, (T, S), 0), W)
    before = jnp.where(cell == 0, 0.0, parts[0, pl.ds(7, T)])
    after = jnp.where(cell == W - 1, 0.0, parts[2, pl.ds(9, T)])
    conv = before + parts[1, pl.ds(8, T)] + after
    out_ref[0] = (jo[...].reshape(T, S).astype(F32) + conv).astype(BF16).reshape(R, W, S)

    joined_copy.wait_send()
    for k in range(hr):
        pl.when(z < Z - 1)(rightward(z, k).wait_send)
        pl.when(z > 0)(leftward(z, k).wait_send)
        sideward(z, k, 0).wait_send()
        pl.when(z < Z - 1)(sideward(z, k, 1).wait_send)
    cache_edges(lambda copy: copy.wait_send())
    for f in range(3):
        pl.when(has_back)(relay(f).wait_send)
    near_copies(lambda copy: copy.wait_send())
    for part in (0, 1):
        for hop in (1, 2):
            if N > hop:
                pl.when(tm + hop < N)(along_tm(hop, part).wait_send)

    def spread_done(f):
        edge_copy(f).wait_send()
        rest_copy(f).wait_send()

    spread_done(2)
    if N > 1:
        pl.when(tm >= 1)(lambda: spread_done(1))
    if N > 2:
        pl.when(tm >= 2)(lambda: spread_done(0))


def solution(mesh):
    Z, N = mesh.shape["space"], mesh.shape["tm"]

    def body(frames_in, cache, gain_one, gain_two, w_query, w_key, w_value, w_out, conv_weight):
        _, R, W, S = frames_in.shape
        C = 2 * S
        hr, half, T = R // 2, R // 2 * W, R * W
        hops, sets = max(1, min(2, N - 1)), min(3, N)
        dma = pltpu.SemaphoreType.DMA
        hbm = pl.BlockSpec(memory_space=pltpu.HBM)
        vmem = pl.BlockSpec(memory_space=pltpu.VMEM)
        return pl.pallas_call(
            functools.partial(kernel, Z, N),
            out_shape=jax.ShapeDtypeStruct(frames_in.shape, BF16),
            in_specs=[hbm] * 9,
            out_specs=vmem,
            scratch_shapes=[
                pltpu.VMEM((R, W, S), BF16),
                pltpu.VMEM((Z, hr, 2, W, C), BF16),
                pltpu.VMEM((half, C), BF16),
                pltpu.VMEM((half, C), BF16),
                pltpu.VMEM((half, 1), F32),
                pltpu.VMEM((half, 1), F32),
                pltpu.VMEM((half, C), F32),
                pltpu.VMEM((3, R + 2, W, C), BF16),
                pltpu.VMEM((3, 2, W, C), BF16),
                pltpu.VMEM((hr, W, S), BF16),
                pltpu.VMEM((R, W, S), BF16),
                pltpu.VMEM((3, T + 16, S), F32),
                pltpu.VMEM((C,), BF16),
                pltpu.VMEM((C,), BF16),
                pltpu.VMEM((4, C, C), BF16),
                pltpu.VMEM((C, C), BF16),
                pltpu.VMEM((3, 3, 3, S, C), BF16),
                dma((7,)),
                dma,
                dma,
                dma((hr,)),
                dma((hr,)),
                dma((2, hr)),
                dma((Z, hr)),
                dma((Z, hr)),
                dma((2,)),
                dma((3, 2)),
                dma((sets,)),
                dma((sets,)),
                dma((sets,)),
                dma((sets,)),
                dma((sets,)),
                dma((hops, 2)),
                dma((hops, 2)),
                dma((3,)),
            ],
            compiler_params=pltpu.CompilerParams(
                collective_id=0, has_side_effects=True, vmem_limit_bytes=50 << 20
            ),
        )(*(pltpu.with_memory_space_constraint(a, pltpu.HBM) for a in (
            frames_in, cache, gain_one, gain_two,
            w_query, w_key, w_value, w_out, jnp.swapaxes(conv_weight, 3, 4),
        )))

    return jax.shard_map(
        body,
        mesh=mesh,
        in_specs=(
            P(("clips", "tm"), "space", None, "chan"),
            P("clips", "space", None, None),
            P(),
            P(),
            P(),
            P(),
            P(),
            P(),
            P(None, None, None, None, "chan"),
        ),
        out_specs=P(("clips", "tm"), "space", None, "chan"),
        check_vma=False,
    )
```

```python
import functools
import math

import jax
import jax.numpy as jnp
from jax import lax
from jax.experimental import pallas as pl
from jax.experimental.pallas import tpu as pltpu
from jax.sharding import PartitionSpec as P

F32 = jnp.float32
BF16 = jnp.bfloat16
MESH = pl.DeviceIdType.MESH


def normalized(wide, gain):
    factor = lax.rsqrt(jnp.mean(wide * wide, axis=-1, keepdims=True) + 1e-06)
    return wide * factor * gain


def kernel(
    Z, N,
    x_hbm, cache_hbm, g1_hbm, g2_hbm, wq_hbm, wk_hbm, wv_hbm, wo_hbm, cw_hbm,
    out_ref,
    xo, xg, xn, qk, top, total, acc, cb, hb, jt, jo, parts, g1_ref, g2_ref, ws, wvo, cw,
    s_loc, s_pair, r_pair, s_right, s_left, s_sib, r_z, r_sib,
    s_cache, r_halo, s_near, s_edge, s_rest, r_edge, r_rest, s_tm, r_tm, s_half,
):
    z = lax.axis_index("space")
    c = lax.axis_index("chan")
    tm = lax.axis_index("tm")
    o = 1 - c
    R, W, S = out_ref.shape[1:]
    C = 2 * S
    hr = R // 2
    T = R * W
    L = 128
    E = S - L
    blocks = ((0, 0, L), (S, L, L), (L, 2 * L, E), (S + L, 2 * L + E, E))

    def dev(dz=None, core=None, frame=None):
        return {
            "space": z if dz is None else dz,
            "chan": c if core is None else core,
            "tm": tm if frame is None else frame,
        }

    def send(src, dst, ssem, rsem, to):
        return pltpu.make_async_remote_copy(
            src_ref=src, dst_ref=dst, send_sem=ssem, recv_sem=rsem,
            device_id=to, device_id_type=MESH,
        )

    near, back = z + 2 * c - 1, z + 1 - 2 * c
    has_near = jnp.logical_and(near >= 0, near < Z)
    has_back = jnp.logical_and(back >= 0, back < Z)
    is_end = jnp.logical_or(z == 0, z == Z - 1)
    inner = jnp.logical_not(is_end)

    barrier = pltpu.get_barrier_semaphore()

    def greet(to):
        pl.semaphore_signal(barrier, inc=1, device_id=to, device_id_type=MESH)

    greet(dev(core=o))
    pl.when(z > 0)(lambda: greet(dev(dz=z - 1)))
    pl.when(z < Z - 1)(lambda: greet(dev(dz=z + 1)))
    for hop in (1, 2):
        if N > hop:
            pl.when(tm >= hop)(functools.partial(lambda h: greet(dev(frame=tm - h)), hop))

    x_own = pltpu.make_async_copy(x_hbm.at[0], xo, s_loc.at[0])
    x_own.start()
    gains = [
        pltpu.make_async_copy(a, b, s_loc.at[1 + i])
        for i, (a, b) in enumerate(((g1_hbm, g1_ref), (g2_hbm, g2_ref)))
    ]
    for g in gains:
        g.start()
    for i, w_hbm in enumerate((wq_hbm, wk_hbm, wv_hbm)):
        for src, dst, count in blocks:
            pltpu.make_async_copy(w_hbm.at[pl.ds(src, count)], ws.at[i, pl.ds(dst, count)], s_loc.at[3]).start()
    pltpu.make_async_copy(wo_hbm, ws.at[3], s_loc.at[3]).start()
    taps_own = pltpu.make_async_copy(cw_hbm, cw, s_loc.at[4])
    taps_own.start()
    first = jnp.minimum(tm, 1)
    cache_two = pltpu.make_async_copy(cache_hbm.at[first], cb.at[0, pl.ds(1, R)], s_loc.at[5])
    cache_one = pltpu.make_async_copy(cache_hbm.at[1], cb.at[1, pl.ds(1, R)], s_loc.at[6])
    pl.when(tm <= 1)(cache_two.start)
    pl.when(tm == 0)(cache_one.start)

    blank = jnp.zeros((W, C), BF16)
    for f in range(3):
        cb[f, 0] = blank
        cb[f, R + 1] = blank

    x_own.wait()
    for k in range(hr):
        a, b = xo[2 * k], xo[2 * k + 1]
        xg[z, k, c] = jnp.concatenate([a[:, :L], b[:, :L], a[:, L:], b[:, L:]], axis=-1)

    want = 1 + jnp.where(z > 0, 1, 0) + jnp.where(z < Z - 1, 1, 0)
    for hop in (1, 2):
        if N > hop:
            want = want + jnp.where(tm + hop < N, 1, 0)
    pl.semaphore_wait(barrier, want)

    def rightward(j, k):
        return send(xg.at[j, k, c], xg.at[j, k, c], s_right.at[k], r_z.at[j, k], dev(dz=z + 1))

    def leftward(j, k):
        return send(xg.at[j, k, c], xg.at[j, k, c], s_left.at[k], r_z.at[j, k], dev(dz=z - 1))

    def sideward(j, k, flow):
        return send(xg.at[j, k, c], xg.at[j, k, c], s_sib.at[flow, k], r_sib.at[j, k], dev(core=o))

    for k in range(hr):
        pl.when(z < Z - 1)(rightward(z, k).start)
        pl.when(z > 0)(leftward(z, k).start)
        sideward(z, k, 0).start()

    gains[0].wait()
    gain_one = g1_ref[...].astype(F32).reshape(1, C)
    gain_one = jnp.concatenate([gain_one[:, at : at + count] for at, _, count in blocks], axis=-1)
    low_lanes = lax.broadcasted_iota(jnp.int32, (W, L), 1) < E

    def tokens(j, k):
        p, q = xg[j, k, 0].astype(F32), xg[j, k, 1].astype(F32)
        pt, qt = p[:, 2 * L :], q[:, 2 * L :]
        even = jnp.where(low_lanes, pt, pltpu.roll(qt, E, 1))
        odd = jnp.where(low_lanes, pltpu.roll(pt, E, 1), qt)
        return jnp.concatenate([
            jnp.concatenate([p[:, :L], q[:, :L], even], axis=-1),
            jnp.concatenate([p[:, L : 2 * L], q[:, L : 2 * L], odd], axis=-1),
        ], axis=0)

    def normed(wide):
        return normalized(wide, gain_one).astype(BF16)

    top[...] = jnp.full(top.shape, -1e30, F32)
    total[...] = jnp.zeros(total.shape, F32)
    acc[...] = jnp.zeros(acc.shape, F32)

    def attend(keys):
        scores = lax.dot_general(qk[...], keys, (((1,), (1,)), ((), ())), preferred_element_type=F32)
        old = top[...]
        new = jnp.maximum(old, jnp.max(scores, axis=-1, keepdims=True))
        weight = jnp.exp2(scores - new)
        fade = jnp.exp2(old - new)
        top[...] = new
        total[...] = total[...] * fade + jnp.sum(weight, axis=-1, keepdims=True)
        acc[...] = acc[...] * fade + jnp.dot(weight.astype(BF16), keys, preferred_element_type=F32)

    for k in range(hr):
        sideward(z, k, 0).wait_recv()
    pltpu.make_async_copy(ws, ws, s_loc.at[3]).wait()
    mine = tokens(z, c)
    xn[...] = jnp.concatenate(
        [mine[:, :L], mine[:, 2 * L : 2 * L + E], mine[:, L : 2 * L], mine[:, 2 * L + E :]], axis=-1
    ).astype(BF16)
    keys = normed(mine)
    query = jnp.dot(keys, ws[0], preferred_element_type=F32).astype(BF16)
    folded = lax.dot_general(query, ws[1], (((1,), (1,)), ((), ())), preferred_element_type=F32)
    qk[...] = (folded * (C ** (-0.5) * math.log2(math.e))).astype(BF16)
    attend(keys)
    attend(normed(tokens(z, o)))
    wvo[...] = jnp.dot(ws[2], ws[3], preferred_element_type=F32).astype(BF16)

    def piece(f, dw, start):
        rows = jnp.concatenate([cb[f, dh : dh + R].reshape(T, C) for dh in range(3)], axis=-1)
        kernel_rows = jnp.concatenate([cw[f, dh, dw] for dh in range(3)], axis=-1)
        value = lax.dot_general(rows, kernel_rows, (((1,), (1,)), ((), ())), preferred_element_type=F32)
        if start:
            parts[dw, pl.ds(8, T)] = value
        else:
            parts[dw, pl.ds(8, T)] += value

    def early(i):
        f, dw = divmod(i, 3)
        pl.when(tm <= 1 - f)(lambda: piece(f, dw, f == 0))

    taps_own.wait()
    pl.when(tm <= 1)(cache_two.wait)
    pl.when(tm == 0)(cache_one.wait)
    early(0)

    def cache_edge(f):
        row = jnp.where(c == 0, 0, R - 1)
        source = cache_hbm.at[first if f == 0 else 1, row]
        return send(source, hb.at[f, o], s_cache.at[f], r_halo.at[f, o], dev(dz=near))

    def cache_edges(act):
        pl.when(jnp.logical_and(has_near, tm <= 1))(lambda: act(cache_edge(0)))
        pl.when(jnp.logical_and(has_near, tm == 0))(lambda: act(cache_edge(1)))

    ahead = Z - 1 - z
    longer = jnp.maximum(z, ahead)
    sign = jnp.where(ahead >= z, 1, -1)
    edges_at = jnp.minimum(jnp.where(c == 0, ahead, z) + 1, Z - 1)
    slots = 5
    def step(d, carry):
        lo, hi = z - d, z + d
        has_lo, has_hi = lo >= 0, hi < Z

        for k in range(hr):

            @pl.when(has_lo)
            def _():
                rightward(lo, k).wait_recv()

                @pl.when(z < Z - 1)
                def _():
                    rightward(lo, k).wait_send()
                    rightward(lo, k).start()

                sideward(lo, k, 0).wait_send()
                sideward(lo, k, 0).start()

            @pl.when(has_hi)
            def _():
                leftward(hi, k).wait_recv()

                @pl.when(z > 0)
                def _():
                    leftward(hi, k).wait_send()
                    leftward(hi, k).start()

                pl.when(d > 1)(sideward(hi, k, 1).wait_send)
                sideward(hi, k, 1).start()

            if k == hr - 1:
                pl.when(d == edges_at)(lambda: cache_edges(lambda copy: copy.start()))

            for i in range(slots):
                if i % hr == k and i // hr + 1 < Z:
                    pl.when(d == i // hr + 1)(functools.partial(early, i + 1))

            j = z + jnp.where(d <= longer, sign * d, sign * (longer - d))
            sideward(j, k, 0).wait_recv()
            attend(normed(tokens(j, k)))

        return carry

    lax.fori_loop(1, Z, step, 0)
    for i in range(slots):
        if i // hr + 1 >= Z:
            early(i + 1)

    gains[1].wait()
    gain_two = g2_ref[...].astype(F32).reshape(1, C)

    def finish_rows(row, count):
        at = pl.ds(pl.multiple_of(row * W, W), count * W)
        mixed = (acc[at, :] * (1.0 / total[at, :])).astype(BF16)
        joined = xn[at, :].astype(F32) + jnp.dot(mixed, wvo[...], preferred_element_type=F32)
        joined = joined.astype(BF16).astype(F32)
        scaled = normalized(joined, gain_two)
        act = (scaled / (1.0 + jnp.exp(-scaled))).astype(BF16)
        cb[2, pl.ds(1 + c * hr + row, count)] = act.reshape(count, W, C)
        low, high = joined[:, :S].astype(BF16), joined[:, S:].astype(BF16)
        jo[pl.ds(c * hr + row, count)] = jnp.where(c == 0, low, high).reshape(count, W, S)
        jt[pl.ds(row, count)] = jnp.where(c == 0, high, low).reshape(count, W, S)

    edge = jnp.where(c == 0, 1, R)
    rest = jnp.where(c == 0, 2, 1 + hr)
    def along_tm(hop, part):
        row = cb.at[2, edge] if part == 0 else cb.at[2, pl.ds(rest, hr - 1)]
        there = cb.at[2 - hop, edge] if part == 0 else cb.at[2 - hop, pl.ds(rest, hr - 1)]
        return send(row, there, s_tm.at[hop - 1, part], r_tm.at[hop - 1, part], dev(frame=tm + hop))

    def edge_copy(f):
        src = cb.at[f, edge]
        return send(src, src, s_edge.at[2 - f], r_edge.at[2 - f], dev(core=o))

    def near_copy(hop):
        return send(
            cb.at[2, edge], hb.at[2 - hop, o], s_near.at[hop], r_halo.at[2 - hop, o],
            dev(dz=near, frame=tm + hop),
        )

    def near_copies(act):
        pl.when(has_near)(lambda: act(near_copy(0)))
        for hop in range(1, min(3, N)):
            pl.when(jnp.logical_and(jnp.logical_and(has_near, is_end), tm + hop < N))(
                functools.partial(lambda h: act(near_copy(h)), hop)
            )

    def near_pass(f):
        return send(cb.at[f, edge], hb.at[f, o], s_near.at[2 - f], r_halo.at[f, o], dev(dz=near))

    def rest_copy(f):
        src = cb.at[f, pl.ds(rest, hr - 1)]
        return send(src, src, s_rest.at[2 - f], r_rest.at[2 - f], dev(core=o))

    def edge_row(f):
        row = cb.at[f, jnp.where(c == 0, R, 1)]
        send(row, row, s_edge.at[2 - f], r_edge.at[2 - f], dev(core=o)).wait_recv()

    def rest_rows(f):
        rows = cb.at[f, pl.ds(jnp.where(c == 0, 1 + hr, 2), hr - 1)]
        send(rows, rows, s_rest.at[2 - f], r_rest.at[2 - f], dev(core=o)).wait_recv()

    def from_sibling(f):
        edge_row(f)
        rest_rows(f)

    def relay(f):
        row = hb.at[f, o]
        return send(row, row, s_half.at[f], r_halo.at[f, o], dev(core=o))

    def relay_halo(f):
        @pl.when(has_back)
        def _():
            relay(f).wait_recv()
            relay(f).start()

    def both_sides(visit):
        pl.when(z > 0)(lambda: visit(0))
        pl.when(z < Z - 1)(lambda: visit(1))

    for part in (0, 1):
        if part == 0:
            finish_rows(edge - 1 - c * hr, 1)
        else:
            finish_rows(rest - 1 - c * hr, hr - 1)
        for hop in (1, 2):
            if N > hop:
                pl.when(tm + hop < N)(along_tm(hop, part).start)
        if part == 0:
            edge_copy(2).start()
            near_copies(lambda copy: copy.start())
        else:
            rest_copy(2).start()

    joined_copy = send(jt, jo.at[pl.ds(c * hr, hr)], s_pair, r_pair, dev(core=o))
    joined_copy.start()

    def taps(f, start):
        for dw in range(3):
            piece(f, dw, start)

    def forwarded(f, part):
        along_tm(2 - f, part).wait_recv()
        if part == 0:
            edge_copy(f).start()
            pl.when(jnp.logical_and(has_near, inner))(near_pass(f).start)
        else:
            rest_copy(f).start()

    def product(f, dh, dw, at, count):
        rows = jnp.concatenate([cb[f, at + i] for i in range(count)], axis=-1)
        kernel_rows = jnp.concatenate([cw[f, dh + i, dw] for i in range(count)], axis=-1)
        return lax.dot_general(rows, kernel_rows, (((1,), (1,)), ((), ())), preferred_element_type=F32)

    def outer_taps(f):
        for dw in range(3):
            rows = jnp.concatenate([cb[f, 1], cb[f, R]], axis=0)
            both = lax.dot_general(rows, cw[f, 1, dw], (((1,), (1,)), ((), ())), preferred_element_type=F32)
            parts[dw, pl.ds(8, W)] += both[:W]
            parts[dw, pl.ds(8 + (R - 1) * W, W)] += both[W:]
            parts[dw, pl.ds(8 + W, W)] += product(f, 0, dw, 1, 1)
            parts[dw, pl.ds(8 + (R - 2) * W, W)] += product(f, 2, dw, R, 1)

    def inner_taps(f):
        for dw in range(3):
            for r in range(R):
                lo, hi = max(r, 2), min(r + 2, R - 1)
                parts[dw, pl.ds(8 + r * W, W)] += product(f, lo - r, dw, lo, hi - lo + 1)

    def other_halo(f):
        row = hb.at[f, c]
        pl.when(has_near)(send(row, row, s_half.at[f], r_halo.at[f, c], dev(core=o)).wait_recv)

    def halo_taps(frames):
        for f in frames:
            other_halo(f)

        def visit(side):
            rows = jnp.concatenate([hb[f, side] for f in frames], axis=-1)
            for dw in range(3):
                kernel_rows = jnp.concatenate([cw[f, 2 * side, dw] for f in frames], axis=-1)
                parts[dw, pl.ds(8 + side * (T - W), W)] += lax.dot_general(
                    rows, kernel_rows, (((1,), (1,)), ((), ())), preferred_element_type=F32
                )

        both_sides(visit)

    def halos(frames):
        for f in frames:
            relay_halo(f)
        halo_taps(frames)

    from_sibling(2)
    if N > 2:
        pl.when(tm <= 1)(lambda: taps(2, False))
        pl.when(tm >= 2)(lambda: taps(2, True))
    else:
        taps(2, False)

    pl.when(tm == 0)(lambda: halos((0, 2, 1)))
    if N > 1:

        @pl.when(tm >= 1)
        def _():
            pl.when(is_end)(lambda: relay_halo(2))
            if N == 2:
                pl.when(is_end)(lambda: relay_halo(0))
            forwarded(1, 0)
            if N == 2:
                pl.when(is_end)(lambda: halo_taps((0, 2)))
            else:
                pl.when(is_end)(lambda: halo_taps((2,)))
            edge_row(1)
            outer_taps(1)
            pl.when(is_end)(lambda: halos((1,)))
            forwarded(1, 1)
            rest_rows(1)
            inner_taps(1)
            if N == 2:
                pl.when(inner)(lambda: halos((0, 2, 1)))
            else:
                pl.when(inner)(lambda: halos((2, 1)))
    if N > 2:

        @pl.when(tm >= 2)
        def _():
            forwarded(0, 0)
            forwarded(0, 1)
            from_sibling(0)
            taps(0, False)

        pl.when(tm >= 1)(lambda: halos((0,)))

    there = jo.at[pl.ds(o * hr, hr)]
    send(jt, there, s_pair, r_pair, dev(core=o)).wait_recv()
    cell = lax.rem(lax.broadcasted_iota(jnp.int32, (T, S), 0), W)
    before = jnp.where(cell == 0, 0.0, parts[0, pl.ds(7, T)])
    after = jnp.where(cell == W - 1, 0.0, parts[2, pl.ds(9, T)])
    conv = before + parts[1, pl.ds(8, T)] + after
    out_ref[0] = (jo[...].reshape(T, S).astype(F32) + conv).astype(BF16).reshape(R, W, S)

    joined_copy.wait_send()
    for k in range(hr):
        pl.when(z < Z - 1)(rightward(z, k).wait_send)
        pl.when(z > 0)(leftward(z, k).wait_send)
        sideward(z, k, 0).wait_send()
        pl.when(z < Z - 1)(sideward(z, k, 1).wait_send)
    cache_edges(lambda copy: copy.wait_send())
    for f in range(3):
        pl.when(has_back)(relay(f).wait_send)
    near_copies(lambda copy: copy.wait_send())
    for part in (0, 1):
        for hop in (1, 2):
            if N > hop:
                pl.when(tm + hop < N)(along_tm(hop, part).wait_send)

    def spread_done(f):
        edge_copy(f).wait_send()
        rest_copy(f).wait_send()
        if f < 2:
            pl.when(jnp.logical_and(has_near, inner))(near_pass(f).wait_send)

    spread_done(2)
    if N > 1:
        pl.when(tm >= 1)(lambda: spread_done(1))
    if N > 2:
        pl.when(tm >= 2)(lambda: spread_done(0))


def solution(mesh):
    Z, N = mesh.shape["space"], mesh.shape["tm"]

    def body(frames_in, cache, gain_one, gain_two, w_query, w_key, w_value, w_out, conv_weight):
        _, R, W, S = frames_in.shape
        C = 2 * S
        hr, half, T = R // 2, R // 2 * W, R * W
        hops, sets = max(1, min(2, N - 1)), min(3, N)
        dma = pltpu.SemaphoreType.DMA
        hbm = pl.BlockSpec(memory_space=pltpu.HBM)
        vmem = pl.BlockSpec(memory_space=pltpu.VMEM)
        return pl.pallas_call(
            functools.partial(kernel, Z, N),
            out_shape=jax.ShapeDtypeStruct(frames_in.shape, BF16),
            in_specs=[hbm] * 9,
            out_specs=vmem,
            scratch_shapes=[
                pltpu.VMEM((R, W, S), BF16),
                pltpu.VMEM((Z, hr, 2, W, C), BF16),
                pltpu.VMEM((half, C), BF16),
                pltpu.VMEM((half, C), BF16),
                pltpu.VMEM((half, 1), F32),
                pltpu.VMEM((half, 1), F32),
                pltpu.VMEM((half, C), F32),
                pltpu.VMEM((3, R + 2, W, C), BF16),
                pltpu.VMEM((3, 2, W, C), BF16),
                pltpu.VMEM((hr, W, S), BF16),
                pltpu.VMEM((R, W, S), BF16),
                pltpu.VMEM((3, T + 16, S), F32),
                pltpu.VMEM((C,), BF16),
                pltpu.VMEM((C,), BF16),
                pltpu.VMEM((4, C, C), BF16),
                pltpu.VMEM((C, C), BF16),
                pltpu.VMEM((3, 3, 3, S, C), BF16),
                dma((7,)),
                dma,
                dma,
                dma((hr,)),
                dma((hr,)),
                dma((2, hr)),
                dma((Z, hr)),
                dma((Z, hr)),
                dma((2,)),
                dma((3, 2)),
                dma((sets,)),
                dma((sets,)),
                dma((sets,)),
                dma((sets,)),
                dma((sets,)),
                dma((hops, 2)),
                dma((hops, 2)),
                dma((3,)),
            ],
            compiler_params=pltpu.CompilerParams(
                collective_id=0, has_side_effects=True, vmem_limit_bytes=50 << 20
            ),
        )(*(pltpu.with_memory_space_constraint(a, pltpu.HBM) for a in (
            frames_in, cache, gain_one, gain_two,
            w_query, w_key, w_value, w_out, jnp.swapaxes(conv_weight, 3, 4),
        )))

    return jax.shard_map(
        body,
        mesh=mesh,
        in_specs=(
            P(("clips", "tm"), "space", None, "chan"),
            P("clips", "space", None, None),
            P(),
            P(),
            P(),
            P(),
            P(),
            P(),
            P(None, None, None, None, "chan"),
        ),
        out_specs=P(("clips", "tm"), "space", None, "chan"),
        check_vma=False,
    )
```

```python
import functools
import math

import jax
import jax.numpy as jnp
from jax import lax
from jax.experimental import pallas as pl
from jax.experimental.pallas import tpu as pltpu
from jax.sharding import PartitionSpec as P

F32 = jnp.float32
BF16 = jnp.bfloat16
MESH = pl.DeviceIdType.MESH


def normalized(wide, gain):
    factor = lax.rsqrt(jnp.mean(wide * wide, axis=-1, keepdims=True) + 1e-06)
    return wide * factor * gain


def kernel(
    Z, N,
    x_hbm, cache_hbm, g1_hbm, g2_hbm, wq_hbm, wk_hbm, wv_hbm, wo_hbm, cw_hbm,
    out_ref,
    xo, xg, xn, qk, top, total, acc, cb, hb, jt, jo, parts, g1_ref, g2_ref, ws, wvo, cw,
    s_loc, s_pair, r_pair, s_right, s_left, s_sib, r_z, r_sib,
    s_cache, r_halo, s_near, s_edge, s_rest, r_edge, r_rest, s_tm, r_tm, s_half,
):
    z = lax.axis_index("space")
    c = lax.axis_index("chan")
    tm = lax.axis_index("tm")
    o = 1 - c
    R, W, S = out_ref.shape[1:]
    C = 2 * S
    hr = R // 2
    T = R * W
    L = 128
    E = S - L
    blocks = ((0, 0, L), (S, L, L), (L, 2 * L, E), (S + L, 2 * L + E, E))

    def dev(dz=None, core=None, frame=None):
        return {
            "space": z if dz is None else dz,
            "chan": c if core is None else core,
            "tm": tm if frame is None else frame,
        }

    def send(src, dst, ssem, rsem, to):
        return pltpu.make_async_remote_copy(
            src_ref=src, dst_ref=dst, send_sem=ssem, recv_sem=rsem,
            device_id=to, device_id_type=MESH,
        )

    near, back = z + 2 * c - 1, z + 1 - 2 * c
    has_near = jnp.logical_and(near >= 0, near < Z)
    has_back = jnp.logical_and(back >= 0, back < Z)
    is_end = jnp.logical_or(z == 0, z == Z - 1)
    inner = jnp.logical_not(is_end)

    barrier = pltpu.get_barrier_semaphore()

    def greet(to):
        pl.semaphore_signal(barrier, inc=1, device_id=to, device_id_type=MESH)

    greet(dev(core=o))
    pl.when(z > 0)(lambda: greet(dev(dz=z - 1)))
    pl.when(z < Z - 1)(lambda: greet(dev(dz=z + 1)))
    for hop in (1, 2):
        if N > hop:
            pl.when(tm >= hop)(functools.partial(lambda h: greet(dev(frame=tm - h)), hop))

    x_own = pltpu.make_async_copy(x_hbm.at[0], xo, s_loc.at[0])
    x_own.start()
    gains = [
        pltpu.make_async_copy(a, b, s_loc.at[1 + i])
        for i, (a, b) in enumerate(((g1_hbm, g1_ref), (g2_hbm, g2_ref)))
    ]
    for g in gains:
        g.start()
    for i, w_hbm in enumerate((wq_hbm, wk_hbm, wv_hbm)):
        for src, dst, count in blocks:
            pltpu.make_async_copy(w_hbm.at[pl.ds(src, count)], ws.at[i, pl.ds(dst, count)], s_loc.at[3]).start()
    pltpu.make_async_copy(wo_hbm, ws.at[3], s_loc.at[3]).start()
    taps_own = pltpu.make_async_copy(cw_hbm, cw, s_loc.at[4])
    taps_own.start()
    first = jnp.minimum(tm, 1)
    cache_two = pltpu.make_async_copy(cache_hbm.at[first], cb.at[0, pl.ds(1, R)], s_loc.at[5])
    cache_one = pltpu.make_async_copy(cache_hbm.at[1], cb.at[1, pl.ds(1, R)], s_loc.at[6])
    pl.when(tm <= 1)(cache_two.start)
    pl.when(tm == 0)(cache_one.start)

    blank = jnp.zeros((W, C), BF16)
    for f in range(3):
        cb[f, 0] = blank
        cb[f, R + 1] = blank

    x_own.wait()
    for k in range(hr):
        a, b = xo[2 * k], xo[2 * k + 1]
        xg[z, k, c] = jnp.concatenate([a[:, :L], b[:, :L], a[:, L:], b[:, L:]], axis=-1)

    want = 1 + jnp.where(z > 0, 1, 0) + jnp.where(z < Z - 1, 1, 0)
    for hop in (1, 2):
        if N > hop:
            want = want + jnp.where(tm + hop < N, 1, 0)
    pl.semaphore_wait(barrier, want)

    def rightward(j, k):
        return send(xg.at[j, k, c], xg.at[j, k, c], s_right.at[k], r_z.at[j, k], dev(dz=z + 1))

    def leftward(j, k):
        return send(xg.at[j, k, c], xg.at[j, k, c], s_left.at[k], r_z.at[j, k], dev(dz=z - 1))

    def sideward(j, k, flow):
        return send(xg.at[j, k, c], xg.at[j, k, c], s_sib.at[flow, k], r_sib.at[j, k], dev(core=o))

    def outward(k):
        pl.when(z < Z - 1)(rightward(z, k).start)
        pl.when(z > 0)(leftward(z, k).start)

    outward(0)
    for k in range(hr):
        sideward(z, k, 0).start()

    gains[0].wait()
    gain_one = g1_ref[...].astype(F32).reshape(1, C)
    gain_one = jnp.concatenate([gain_one[:, at : at + count] for at, _, count in blocks], axis=-1)
    low_lanes = lax.broadcasted_iota(jnp.int32, (W, L), 1) < E

    def tokens(j, k):
        p, q = xg[j, k, 0].astype(F32), xg[j, k, 1].astype(F32)
        pt, qt = p[:, 2 * L :], q[:, 2 * L :]
        even = jnp.where(low_lanes, pt, pltpu.roll(qt, E, 1))
        odd = jnp.where(low_lanes, pltpu.roll(pt, E, 1), qt)
        return jnp.concatenate([
            jnp.concatenate([p[:, :L], q[:, :L], even], axis=-1),
            jnp.concatenate([p[:, L : 2 * L], q[:, L : 2 * L], odd], axis=-1),
        ], axis=0)

    def normed(wide):
        return normalized(wide, gain_one).astype(BF16)

    top[...] = jnp.full(top.shape, -1e30, F32)
    total[...] = jnp.zeros(total.shape, F32)
    acc[...] = jnp.zeros(acc.shape, F32)

    everything = pl.ds(0, hr * W)

    def attend(keys, at=everything):
        scores = lax.dot_general(qk[at, :], keys, (((1,), (1,)), ((), ())), preferred_element_type=F32)
        old = top[at, :]
        new = jnp.maximum(old, jnp.max(scores, axis=-1, keepdims=True))
        weight = jnp.exp2(scores - new)
        fade = jnp.exp2(old - new)
        top[at, :] = new
        total[at, :] = total[at, :] * fade + jnp.sum(weight, axis=-1, keepdims=True)
        acc[at, :] = acc[at, :] * fade + jnp.dot(weight.astype(BF16), keys, preferred_element_type=F32)

    for k in range(hr):
        sideward(z, k, 0).wait_recv()
    for k in range(1, hr):
        outward(k)
    pltpu.make_async_copy(ws, ws, s_loc.at[3]).wait()
    mine = tokens(z, c)
    xn[...] = jnp.concatenate(
        [mine[:, :L], mine[:, 2 * L : 2 * L + E], mine[:, L : 2 * L], mine[:, 2 * L + E :]], axis=-1
    ).astype(BF16)
    keys = normed(mine)
    query = jnp.dot(keys, ws[0], preferred_element_type=F32).astype(BF16)
    folded = lax.dot_general(query, ws[1], (((1,), (1,)), ((), ())), preferred_element_type=F32)
    qk[...] = (folded * (C ** (-0.5) * math.log2(math.e))).astype(BF16)
    attend(keys)
    attend(normed(tokens(z, o)))
    wvo[...] = jnp.dot(ws[2], ws[3], preferred_element_type=F32).astype(BF16)

    def piece(f, dw, start):
        rows = jnp.concatenate([cb[f, dh : dh + R].reshape(T, C) for dh in range(3)], axis=-1)
        kernel_rows = jnp.concatenate([cw[f, dh, dw] for dh in range(3)], axis=-1)
        value = lax.dot_general(rows, kernel_rows, (((1,), (1,)), ((), ())), preferred_element_type=F32)
        if start:
            parts[dw, pl.ds(8, T)] = value
        else:
            parts[dw, pl.ds(8, T)] += value

    def early(i):
        f, dw = divmod(i, 3)
        pl.when(tm <= 1 - f)(lambda: piece(f, dw, f == 0))

    taps_own.wait()
    pl.when(tm <= 1)(cache_two.wait)
    pl.when(tm == 0)(cache_one.wait)
    early(0)

    def cache_edge(f):
        row = jnp.where(c == 0, 0, R - 1)
        source = cache_hbm.at[first if f == 0 else 1, row]
        return send(source, hb.at[f, o], s_cache.at[f], r_halo.at[f, o], dev(dz=near))

    def cache_edges(act):
        pl.when(jnp.logical_and(has_near, tm <= 1))(lambda: act(cache_edge(0)))
        pl.when(jnp.logical_and(has_near, tm == 0))(lambda: act(cache_edge(1)))

    ahead = Z - 1 - z
    longer = jnp.maximum(z, ahead)
    sign = jnp.where(ahead >= z, 1, -1)
    edges_at = jnp.minimum(jnp.where(c == 0, ahead, z) + 1, Z - 1)
    slots = 5
    def step(d, carry):
        lo, hi = z - d, z + d
        has_lo, has_hi = lo >= 0, hi < Z

        for k in range(hr):

            @pl.when(has_lo)
            def _():
                rightward(lo, k).wait_recv()

                @pl.when(z < Z - 1)
                def _():
                    rightward(lo, k).wait_send()
                    rightward(lo, k).start()

                sideward(lo, k, 0).wait_send()
                sideward(lo, k, 0).start()

            @pl.when(has_hi)
            def _():
                leftward(hi, k).wait_recv()

                @pl.when(z > 0)
                def _():
                    leftward(hi, k).wait_send()
                    leftward(hi, k).start()

                pl.when(d > 1)(sideward(hi, k, 1).wait_send)
                sideward(hi, k, 1).start()

            if k == hr - 1:
                pl.when(d == edges_at)(lambda: cache_edges(lambda copy: copy.start()))

            for i in range(slots):
                if i % hr == k and i // hr + 1 < Z:
                    pl.when(d == i // hr + 1)(functools.partial(early, i + 1))

            def visit():
                j = z + jnp.where(d <= longer, sign * d, sign * (longer - d))
                sideward(j, k, 0).wait_recv()
                attend(normed(tokens(j, k)))

            if k < hr - 1:
                visit()
            else:
                pl.when(d < Z - 1)(visit)

        return carry

    lax.fori_loop(1, Z, step, 0)
    for i in range(slots):
        if i // hr + 1 >= Z:
            early(i + 1)

    last = jnp.where(longer == Z - 1, z + sign * (Z - 1), jnp.where(sign > 0, 0, Z - 1))
    sideward(last, hr - 1, 0).wait_recv()
    keys = normed(tokens(last, hr - 1))

    gains[1].wait()
    gain_two = g2_ref[...].astype(F32).reshape(1, C)

    def finish_rows(row, count):
        at = pl.ds(pl.multiple_of(row * W, W), count * W)
        attend(keys, at)
        mixed = (acc[at, :] * (1.0 / total[at, :])).astype(BF16)
        joined = xn[at, :].astype(F32) + jnp.dot(mixed, wvo[...], preferred_element_type=F32)
        joined = joined.astype(BF16).astype(F32)
        scaled = normalized(joined, gain_two)
        act = (scaled / (1.0 + jnp.exp(-scaled))).astype(BF16)
        cb[2, pl.ds(1 + c * hr + row, count)] = act.reshape(count, W, C)
        low, high = joined[:, :S].astype(BF16), joined[:, S:].astype(BF16)
        jo[pl.ds(c * hr + row, count)] = jnp.where(c == 0, low, high).reshape(count, W, S)
        jt[pl.ds(row, count)] = jnp.where(c == 0, high, low).reshape(count, W, S)

    edge = jnp.where(c == 0, 1, R)
    rest = jnp.where(c == 0, 2, 1 + hr)
    def along_tm(hop, part):
        row = cb.at[2, edge] if part == 0 else cb.at[2, pl.ds(rest, hr - 1)]
        there = cb.at[2 - hop, edge] if part == 0 else cb.at[2 - hop, pl.ds(rest, hr - 1)]
        return send(row, there, s_tm.at[hop - 1, part], r_tm.at[hop - 1, part], dev(frame=tm + hop))

    def edge_copy(f):
        src = cb.at[f, edge]
        return send(src, src, s_edge.at[2 - f], r_edge.at[2 - f], dev(core=o))

    def near_copy(hop):
        return send(
            cb.at[2, edge], hb.at[2 - hop, o], s_near.at[hop], r_halo.at[2 - hop, o],
            dev(dz=near, frame=tm + hop),
        )

    def near_copies(act):
        pl.when(has_near)(lambda: act(near_copy(0)))
        for hop in range(1, min(3, N)):
            pl.when(jnp.logical_and(jnp.logical_and(has_near, is_end), tm + hop < N))(
                functools.partial(lambda h: act(near_copy(h)), hop)
            )

    def near_pass(f):
        return send(cb.at[f, edge], hb.at[f, o], s_near.at[2 - f], r_halo.at[f, o], dev(dz=near))

    def rest_copy(f):
        src = cb.at[f, pl.ds(rest, hr - 1)]
        return send(src, src, s_rest.at[2 - f], r_rest.at[2 - f], dev(core=o))

    def edge_row(f):
        row = cb.at[f, jnp.where(c == 0, R, 1)]
        send(row, row, s_edge.at[2 - f], r_edge.at[2 - f], dev(core=o)).wait_recv()

    def rest_rows(f):
        rows = cb.at[f, pl.ds(jnp.where(c == 0, 1 + hr, 2), hr - 1)]
        send(rows, rows, s_rest.at[2 - f], r_rest.at[2 - f], dev(core=o)).wait_recv()

    def from_sibling(f):
        edge_row(f)
        rest_rows(f)

    def relay(f):
        row = hb.at[f, o]
        return send(row, row, s_half.at[f], r_halo.at[f, o], dev(core=o))

    def relay_halo(f):
        @pl.when(has_back)
        def _():
            relay(f).wait_recv()
            relay(f).start()

    def both_sides(visit):
        pl.when(z > 0)(lambda: visit(0))
        pl.when(z < Z - 1)(lambda: visit(1))

    for part in (0, 1):
        if part == 0:
            finish_rows(edge - 1 - c * hr, 1)
        else:
            finish_rows(rest - 1 - c * hr, hr - 1)
        for hop in (1, 2):
            if N > hop:
                pl.when(tm + hop < N)(along_tm(hop, part).start)
        if part == 0:
            edge_copy(2).start()
            near_copies(lambda copy: copy.start())
        else:
            rest_copy(2).start()

    joined_copy = send(jt, jo.at[pl.ds(c * hr, hr)], s_pair, r_pair, dev(core=o))
    joined_copy.start()

    def taps(f, start):
        for dw in range(3):
            piece(f, dw, start)

    def forwarded(f, part):
        along_tm(2 - f, part).wait_recv()
        if part == 0:
            edge_copy(f).start()
            pl.when(jnp.logical_and(has_near, inner))(near_pass(f).start)
        else:
            rest_copy(f).start()

    def product(f, dh, dw, at):
        return lax.dot_general(cb[f, at], cw[f, dh, dw], (((1,), (1,)), ((), ())), preferred_element_type=F32)

    def outer_taps(f):
        for dw in range(3):
            rows = jnp.concatenate([cb[f, 1], cb[f, R]], axis=0)
            both = lax.dot_general(rows, cw[f, 1, dw], (((1,), (1,)), ((), ())), preferred_element_type=F32)
            parts[dw, pl.ds(8, W)] += both[:W]
            parts[dw, pl.ds(8 + (R - 1) * W, W)] += both[W:]
            parts[dw, pl.ds(8 + W, W)] += product(f, 0, dw, 1)
            parts[dw, pl.ds(8 + (R - 2) * W, W)] += product(f, 2, dw, R)

    def row_taps(f, row):
        for dw in range(3):
            for dh in range(3):
                at = pl.ds(pl.multiple_of(8 + (row - dh) * W, 8), W)
                parts[dw, at] += lax.dot_general(
                    cb[f, row], cw[f, dh, dw], (((1,), (1,)), ((), ())), preferred_element_type=F32
                )

    def other_halo(f):
        row = hb.at[f, c]
        pl.when(has_near)(send(row, row, s_half.at[f], r_halo.at[f, c], dev(core=o)).wait_recv)

    def halo_taps(frames):
        for f in frames:
            other_halo(f)

        def visit(side):
            rows = jnp.concatenate([hb[f, side] for f in frames], axis=-1)
            for dw in range(3):
                kernel_rows = jnp.concatenate([cw[f, 2 * side, dw] for f in frames], axis=-1)
                parts[dw, pl.ds(8 + side * (T - W), W)] += lax.dot_general(
                    rows, kernel_rows, (((1,), (1,)), ((), ())), preferred_element_type=F32
                )

        both_sides(visit)

    def halos(frames):
        for f in frames:
            relay_halo(f)
        halo_taps(frames)

    from_sibling(2)
    if N > 2:
        pl.when(tm <= 1)(lambda: taps(2, False))
        pl.when(tm >= 2)(lambda: taps(2, True))
    else:
        taps(2, False)

    pl.when(tm == 0)(lambda: halos((0, 2, 1)))
    if N > 1:

        @pl.when(tm >= 1)
        def _():
            pl.when(is_end)(lambda: relay_halo(2))
            if N == 2:
                pl.when(is_end)(lambda: relay_halo(0))
            forwarded(1, 0)
            if N == 2:
                pl.when(is_end)(lambda: halo_taps((0, 2)))
            else:
                pl.when(is_end)(lambda: halo_taps((2,)))
            edge_row(1)
            outer_taps(1)
            forwarded(1, 1)
            late = (0, 2) if N == 2 else (2,)

            @pl.when(inner)
            def _():
                for f in late:
                    relay_halo(f)

            relay_halo(1)
            row_taps(1, jnp.where(c == 0, 2, R - 1))
            rest_rows(1)
            row_taps(1, jnp.where(c == 0, R - 1, 2))
            pl.when(is_end)(lambda: halo_taps((1,)))
            pl.when(inner)(lambda: halo_taps(late + (1,)))
    if N > 2:

        @pl.when(tm >= 2)
        def _():
            forwarded(0, 0)
            forwarded(0, 1)
            from_sibling(0)
            taps(0, False)

        pl.when(tm >= 1)(lambda: halos((0,)))

    there = jo.at[pl.ds(o * hr, hr)]
    send(jt, there, s_pair, r_pair, dev(core=o)).wait_recv()
    cell = lax.rem(lax.broadcasted_iota(jnp.int32, (T, S), 0), W)
    before = jnp.where(cell == 0, 0.0, parts[0, pl.ds(7, T)])
    after = jnp.where(cell == W - 1, 0.0, parts[2, pl.ds(9, T)])
    conv = before + parts[1, pl.ds(8, T)] + after
    out_ref[0] = (jo[...].reshape(T, S).astype(F32) + conv).astype(BF16).reshape(R, W, S)

    joined_copy.wait_send()
    for k in range(hr):
        pl.when(z < Z - 1)(rightward(z, k).wait_send)
        pl.when(z > 0)(leftward(z, k).wait_send)
        sideward(z, k, 0).wait_send()
        pl.when(z < Z - 1)(sideward(z, k, 1).wait_send)
    cache_edges(lambda copy: copy.wait_send())
    for f in range(3):
        pl.when(has_back)(relay(f).wait_send)
    near_copies(lambda copy: copy.wait_send())
    for part in (0, 1):
        for hop in (1, 2):
            if N > hop:
                pl.when(tm + hop < N)(along_tm(hop, part).wait_send)

    def spread_done(f):
        edge_copy(f).wait_send()
        rest_copy(f).wait_send()
        if f < 2:
            pl.when(jnp.logical_and(has_near, inner))(near_pass(f).wait_send)

    spread_done(2)
    if N > 1:
        pl.when(tm >= 1)(lambda: spread_done(1))
    if N > 2:
        pl.when(tm >= 2)(lambda: spread_done(0))


def solution(mesh):
    Z, N = mesh.shape["space"], mesh.shape["tm"]

    def body(frames_in, cache, gain_one, gain_two, w_query, w_key, w_value, w_out, conv_weight):
        _, R, W, S = frames_in.shape
        C = 2 * S
        hr, half, T = R // 2, R // 2 * W, R * W
        hops, sets = max(1, min(2, N - 1)), min(3, N)
        dma = pltpu.SemaphoreType.DMA
        hbm = pl.BlockSpec(memory_space=pltpu.HBM)
        vmem = pl.BlockSpec(memory_space=pltpu.VMEM)
        return pl.pallas_call(
            functools.partial(kernel, Z, N),
            out_shape=jax.ShapeDtypeStruct(frames_in.shape, BF16),
            in_specs=[hbm] * 9,
            out_specs=vmem,
            scratch_shapes=[
                pltpu.VMEM((R, W, S), BF16),
                pltpu.VMEM((Z, hr, 2, W, C), BF16),
                pltpu.VMEM((half, C), BF16),
                pltpu.VMEM((half, C), BF16),
                pltpu.VMEM((half, 1), F32),
                pltpu.VMEM((half, 1), F32),
                pltpu.VMEM((half, C), F32),
                pltpu.VMEM((3, R + 2, W, C), BF16),
                pltpu.VMEM((3, 2, W, C), BF16),
                pltpu.VMEM((hr, W, S), BF16),
                pltpu.VMEM((R, W, S), BF16),
                pltpu.VMEM((3, T + 16, S), F32),
                pltpu.VMEM((C,), BF16),
                pltpu.VMEM((C,), BF16),
                pltpu.VMEM((4, C, C), BF16),
                pltpu.VMEM((C, C), BF16),
                pltpu.VMEM((3, 3, 3, S, C), BF16),
                dma((7,)),
                dma,
                dma,
                dma((hr,)),
                dma((hr,)),
                dma((2, hr)),
                dma((Z, hr)),
                dma((Z, hr)),
                dma((2,)),
                dma((3, 2)),
                dma((sets,)),
                dma((sets,)),
                dma((sets,)),
                dma((sets,)),
                dma((sets,)),
                dma((hops, 2)),
                dma((hops, 2)),
                dma((3,)),
            ],
            compiler_params=pltpu.CompilerParams(
                collective_id=0, has_side_effects=True, vmem_limit_bytes=50 << 20
            ),
        )(*(pltpu.with_memory_space_constraint(a, pltpu.HBM) for a in (
            frames_in, cache, gain_one, gain_two,
            w_query, w_key, w_value, w_out, jnp.swapaxes(conv_weight, 3, 4),
        )))

    return jax.shard_map(
        body,
        mesh=mesh,
        in_specs=(
            P(("clips", "tm"), "space", None, "chan"),
            P("clips", "space", None, None),
            P(),
            P(),
            P(),
            P(),
            P(),
            P(),
            P(None, None, None, None, "chan"),
        ),
        out_specs=P(("clips", "tm"), "space", None, "chan"),
        check_vma=False,
    )
```

```python
import functools
import math

import jax
import jax.numpy as jnp
from jax import lax
from jax.experimental import pallas as pl
from jax.experimental.pallas import tpu as pltpu
from jax.sharding import PartitionSpec as P

F32 = jnp.float32
BF16 = jnp.bfloat16
MESH = pl.DeviceIdType.MESH


def normalized(wide, gain):
    factor = lax.rsqrt(jnp.mean(wide * wide, axis=-1, keepdims=True) + 1e-06)
    return wide * factor * gain


def kernel(
    Z, N,
    x_hbm, cache_hbm, g1_hbm, g2_hbm, wq_hbm, wk_hbm, wv_hbm, wo_hbm, cw_hbm,
    out_ref,
    xo, xg, xn, qk, top, total, acc, cb, hb, jt, jo, parts, g1_ref, g2_ref, ws, wvo, cw,
    s_loc, s_pair, r_pair, s_right, s_left, s_sib, r_z, r_sib,
    s_cache, r_halo, s_near, s_edge, s_rest, r_edge, r_rest, s_tm, r_tm, s_half,
):
    z = lax.axis_index("space")
    c = lax.axis_index("chan")
    tm = lax.axis_index("tm")
    o = 1 - c
    R, W, S = out_ref.shape[1:]
    C = 2 * S
    hr = R // 2
    T = R * W
    L = 128
    E = S - L
    blocks = ((0, 0, L), (S, L, L), (L, 2 * L, E), (S + L, 2 * L + E, E))

    def dev(dz=None, core=None, frame=None):
        return {
            "space": z if dz is None else dz,
            "chan": c if core is None else core,
            "tm": tm if frame is None else frame,
        }

    def send(src, dst, ssem, rsem, to):
        return pltpu.make_async_remote_copy(
            src_ref=src, dst_ref=dst, send_sem=ssem, recv_sem=rsem,
            device_id=to, device_id_type=MESH,
        )

    near, back = z + 2 * c - 1, z + 1 - 2 * c
    has_near = jnp.logical_and(near >= 0, near < Z)
    has_back = jnp.logical_and(back >= 0, back < Z)
    is_end = jnp.logical_or(z == 0, z == Z - 1)
    inner = jnp.logical_not(is_end)

    barrier = pltpu.get_barrier_semaphore()

    def greet(to):
        pl.semaphore_signal(barrier, inc=1, device_id=to, device_id_type=MESH)

    greet(dev(core=o))
    pl.when(z > 0)(lambda: greet(dev(dz=z - 1)))
    pl.when(z < Z - 1)(lambda: greet(dev(dz=z + 1)))
    for hop in (1, 2):
        if N > hop:
            pl.when(tm >= hop)(functools.partial(lambda h: greet(dev(frame=tm - h)), hop))

    x_own = pltpu.make_async_copy(x_hbm.at[0], xo, s_loc.at[0])
    x_own.start()
    gains = [
        pltpu.make_async_copy(a, b, s_loc.at[1 + i])
        for i, (a, b) in enumerate(((g1_hbm, g1_ref), (g2_hbm, g2_ref)))
    ]
    for g in gains:
        g.start()
    for i, w_hbm in enumerate((wq_hbm, wk_hbm, wv_hbm)):
        for src, dst, count in blocks:
            pltpu.make_async_copy(w_hbm.at[pl.ds(src, count)], ws.at[i, pl.ds(dst, count)], s_loc.at[3]).start()
    pltpu.make_async_copy(wo_hbm, ws.at[3], s_loc.at[3]).start()
    taps_own = pltpu.make_async_copy(cw_hbm, cw, s_loc.at[4])
    taps_own.start()
    first = jnp.minimum(tm, 1)
    cache_two = pltpu.make_async_copy(cache_hbm.at[first], cb.at[0, pl.ds(1, R)], s_loc.at[5])
    cache_one = pltpu.make_async_copy(cache_hbm.at[1], cb.at[1, pl.ds(1, R)], s_loc.at[6])
    pl.when(tm <= 1)(cache_two.start)
    pl.when(tm == 0)(cache_one.start)

    blank = jnp.zeros((W, C), BF16)
    for f in range(3):
        cb[f, 0] = blank
        cb[f, R + 1] = blank

    x_own.wait()
    for k in range(hr):
        a, b = xo[2 * k], xo[2 * k + 1]
        xg[z, k, c] = jnp.concatenate([a[:, :L], b[:, :L], a[:, L:], b[:, L:]], axis=-1)

    want = 1 + jnp.where(z > 0, 1, 0) + jnp.where(z < Z - 1, 1, 0)
    for hop in (1, 2):
        if N > hop:
            want = want + jnp.where(tm + hop < N, 1, 0)
    pl.semaphore_wait(barrier, want)

    def rightward(j, k):
        return send(xg.at[j, k, c], xg.at[j, k, c], s_right.at[k], r_z.at[j, k], dev(dz=z + 1))

    def leftward(j, k):
        return send(xg.at[j, k, c], xg.at[j, k, c], s_left.at[k], r_z.at[j, k], dev(dz=z - 1))

    def sideward(j, k, flow):
        return send(xg.at[j, k, c], xg.at[j, k, c], s_sib.at[flow, k], r_sib.at[j, k], dev(core=o))

    def outward(k):
        pl.when(z < Z - 1)(rightward(z, k).start)
        pl.when(z > 0)(leftward(z, k).start)

    outward(0)
    for k in range(hr):
        sideward(z, k, 0).start()

    gains[0].wait()
    gain_one = g1_ref[...].astype(F32).reshape(1, C)
    gain_one = jnp.concatenate([gain_one[:, at : at + count] for at, _, count in blocks], axis=-1)
    low_lanes = lax.broadcasted_iota(jnp.int32, (W, L), 1) < E

    def tokens(j, k):
        p, q = xg[j, k, 0].astype(F32), xg[j, k, 1].astype(F32)
        pt, qt = p[:, 2 * L :], q[:, 2 * L :]
        even = jnp.where(low_lanes, pt, pltpu.roll(qt, E, 1))
        odd = jnp.where(low_lanes, pltpu.roll(pt, E, 1), qt)
        return jnp.concatenate([
            jnp.concatenate([p[:, :L], q[:, :L], even], axis=-1),
            jnp.concatenate([p[:, L : 2 * L], q[:, L : 2 * L], odd], axis=-1),
        ], axis=0)

    def normed(wide):
        return normalized(wide, gain_one).astype(BF16)

    top[...] = jnp.full(top.shape, -1e30, F32)
    total[...] = jnp.zeros(total.shape, F32)
    acc[...] = jnp.zeros(acc.shape, F32)

    everything = pl.ds(0, hr * W)

    def attend(keys, at=everything):
        scores = lax.dot_general(qk[at, :], keys, (((1,), (1,)), ((), ())), preferred_element_type=F32)
        old = top[at, :]
        new = jnp.maximum(old, jnp.max(scores, axis=-1, keepdims=True))
        weight = jnp.exp2(scores - new)
        fade = jnp.exp2(old - new)
        top[at, :] = new
        total[at, :] = total[at, :] * fade + jnp.sum(weight, axis=-1, keepdims=True)
        acc[at, :] = acc[at, :] * fade + jnp.dot(weight.astype(BF16), keys, preferred_element_type=F32)

    for k in range(hr):
        sideward(z, k, 0).wait_recv()
    for k in range(1, hr):
        outward(k)
    pltpu.make_async_copy(ws, ws, s_loc.at[3]).wait()
    mine = tokens(z, c)
    xn[...] = jnp.concatenate(
        [mine[:, :L], mine[:, 2 * L : 2 * L + E], mine[:, L : 2 * L], mine[:, 2 * L + E :]], axis=-1
    ).astype(BF16)
    keys = normed(mine)
    query = jnp.dot(keys, ws[0], preferred_element_type=F32).astype(BF16)
    folded = lax.dot_general(query, ws[1], (((1,), (1,)), ((), ())), preferred_element_type=F32)
    qk[...] = (folded * (C ** (-0.5) * math.log2(math.e))).astype(BF16)
    attend(keys)
    attend(normed(tokens(z, o)))
    wvo[...] = jnp.dot(ws[2], ws[3], preferred_element_type=F32).astype(BF16)

    def piece(f, dw, start):
        rows = jnp.concatenate([cb[f, dh : dh + R].reshape(T, C) for dh in range(3)], axis=-1)
        kernel_rows = jnp.concatenate([cw[f, dh, dw] for dh in range(3)], axis=-1)
        value = lax.dot_general(rows, kernel_rows, (((1,), (1,)), ((), ())), preferred_element_type=F32)
        if start:
            parts[dw, pl.ds(8, T)] = value
        else:
            parts[dw, pl.ds(8, T)] += value

    def early(i):
        f, dw = divmod(i, 3)
        pl.when(tm <= 1 - f)(lambda: piece(f, dw, f == 0))

    taps_own.wait()
    pl.when(tm <= 1)(cache_two.wait)
    pl.when(tm == 0)(cache_one.wait)
    early(0)

    def cache_edge(f):
        row = jnp.where(c == 0, 0, R - 1)
        source = cache_hbm.at[first if f == 0 else 1, row]
        return send(source, hb.at[f, o], s_cache.at[f], r_halo.at[f, o], dev(dz=near))

    def cache_edges(act):
        pl.when(jnp.logical_and(has_near, tm <= 1))(lambda: act(cache_edge(0)))
        pl.when(jnp.logical_and(has_near, tm == 0))(lambda: act(cache_edge(1)))

    ahead = Z - 1 - z
    longer = jnp.maximum(z, ahead)
    sign = jnp.where(ahead >= z, 1, -1)
    edges_at = jnp.minimum(jnp.where(c == 0, ahead, z) + 1, Z - 1)
    slots = 5
    def step(d, carry):
        lo, hi = z - d, z + d
        has_lo, has_hi = lo >= 0, hi < Z

        for k in range(hr):

            @pl.when(has_lo)
            def _():
                rightward(lo, k).wait_recv()

                @pl.when(z < Z - 1)
                def _():
                    rightward(lo, k).wait_send()
                    rightward(lo, k).start()

                sideward(lo, k, 0).wait_send()
                sideward(lo, k, 0).start()

            @pl.when(has_hi)
            def _():
                leftward(hi, k).wait_recv()

                @pl.when(z > 0)
                def _():
                    leftward(hi, k).wait_send()
                    leftward(hi, k).start()

                pl.when(d > 1)(sideward(hi, k, 1).wait_send)
                sideward(hi, k, 1).start()

            if k == hr - 1:
                pl.when(d == edges_at)(lambda: cache_edges(lambda copy: copy.start()))

            for i in range(slots):
                if i % hr == k and i // hr + 1 < Z:
                    pl.when(d == i // hr + 1)(functools.partial(early, i + 1))

            def visit():
                j = z + jnp.where(d <= longer, sign * d, sign * (longer - d))
                sideward(j, k, 0).wait_recv()
                attend(normed(tokens(j, k)))

            if k < hr - 1:
                visit()
            else:
                pl.when(d < Z - 1)(visit)

        return carry

    lax.fori_loop(1, Z, step, 0)
    for i in range(slots):
        if i // hr + 1 >= Z:
            early(i + 1)

    last = jnp.where(longer == Z - 1, z + sign * (Z - 1), jnp.where(sign > 0, 0, Z - 1))
    sideward(last, hr - 1, 0).wait_recv()
    keys = normed(tokens(last, hr - 1))

    gains[1].wait()
    gain_two = g2_ref[...].astype(F32).reshape(1, C)

    def finish_rows(row, count):
        at = pl.ds(pl.multiple_of(row * W, W), count * W)
        attend(keys, at)
        mixed = (acc[at, :] * (1.0 / total[at, :])).astype(BF16)
        joined = xn[at, :].astype(F32) + jnp.dot(mixed, wvo[...], preferred_element_type=F32)
        joined = joined.astype(BF16).astype(F32)
        scaled = normalized(joined, gain_two)
        act = (scaled / (1.0 + jnp.exp(-scaled))).astype(BF16)
        cb[2, pl.ds(1 + c * hr + row, count)] = act.reshape(count, W, C)
        return joined

    def keep_joined(row, count, joined):
        low, high = joined[:, :S].astype(BF16), joined[:, S:].astype(BF16)
        jo[pl.ds(c * hr + row, count)] = jnp.where(c == 0, low, high).reshape(count, W, S)
        jt[pl.ds(row, count)] = jnp.where(c == 0, high, low).reshape(count, W, S)

    edge = jnp.where(c == 0, 1, R)
    rest = jnp.where(c == 0, 2, 1 + hr)
    def along_tm(hop, part):
        row = cb.at[2, edge] if part == 0 else cb.at[2, pl.ds(rest, hr - 1)]
        there = cb.at[2 - hop, edge] if part == 0 else cb.at[2 - hop, pl.ds(rest, hr - 1)]
        return send(row, there, s_tm.at[hop - 1, part], r_tm.at[hop - 1, part], dev(frame=tm + hop))

    def edge_copy(f):
        src = cb.at[f, edge]
        return send(src, src, s_edge.at[2 - f], r_edge.at[2 - f], dev(core=o))

    def near_copy(hop):
        return send(
            cb.at[2, edge], hb.at[2 - hop, o], s_near.at[hop], r_halo.at[2 - hop, o],
            dev(dz=near, frame=tm + hop),
        )

    def near_copies(act):
        pl.when(has_near)(lambda: act(near_copy(0)))
        for hop in range(1, min(3, N)):
            pl.when(jnp.logical_and(jnp.logical_and(has_near, is_end), tm + hop < N))(
                functools.partial(lambda h: act(near_copy(h)), hop)
            )

    def near_pass(f):
        return send(cb.at[f, edge], hb.at[f, o], s_near.at[2 - f], r_halo.at[f, o], dev(dz=near))

    def rest_copy(f):
        src = cb.at[f, pl.ds(rest, hr - 1)]
        return send(src, src, s_rest.at[2 - f], r_rest.at[2 - f], dev(core=o))

    def edge_row(f):
        row = cb.at[f, jnp.where(c == 0, R, 1)]
        send(row, row, s_edge.at[2 - f], r_edge.at[2 - f], dev(core=o)).wait_recv()

    def rest_rows(f):
        rows = cb.at[f, pl.ds(jnp.where(c == 0, 1 + hr, 2), hr - 1)]
        send(rows, rows, s_rest.at[2 - f], r_rest.at[2 - f], dev(core=o)).wait_recv()

    def from_sibling(f):
        edge_row(f)
        rest_rows(f)

    def relay(f):
        row = hb.at[f, o]
        return send(row, row, s_half.at[f], r_halo.at[f, o], dev(core=o))

    def relay_halo(f):
        @pl.when(has_back)
        def _():
            relay(f).wait_recv()
            relay(f).start()

    def both_sides(visit):
        pl.when(z > 0)(lambda: visit(0))
        pl.when(z < Z - 1)(lambda: visit(1))

    for part in (0, 1):
        row, count = (edge - 1 - c * hr, 1) if part == 0 else (rest - 1 - c * hr, hr - 1)
        joined = finish_rows(row, count)
        for hop in (1, 2):
            if N > hop:
                pl.when(tm + hop < N)(along_tm(hop, part).start)
        if part == 0:
            edge_copy(2).start()
            near_copies(lambda copy: copy.start())
        else:
            rest_copy(2).start()
        keep_joined(row, count, joined)

    joined_copy = send(jt, jo.at[pl.ds(c * hr, hr)], s_pair, r_pair, dev(core=o))
    joined_copy.start()

    def taps(f, start):
        for dw in range(3):
            piece(f, dw, start)

    def forwarded(f, part):
        along_tm(2 - f, part).wait_recv()
        if part == 0:
            edge_copy(f).start()
            pl.when(jnp.logical_and(has_near, inner))(near_pass(f).start)
        else:
            rest_copy(f).start()

    def product(f, dh, dw, at):
        return lax.dot_general(cb[f, at], cw[f, dh, dw], (((1,), (1,)), ((), ())), preferred_element_type=F32)

    def outer_taps(f):
        for dw in range(3):
            rows = jnp.concatenate([cb[f, 1], cb[f, R]], axis=0)
            both = lax.dot_general(rows, cw[f, 1, dw], (((1,), (1,)), ((), ())), preferred_element_type=F32)
            parts[dw, pl.ds(8, W)] += both[:W]
            parts[dw, pl.ds(8 + (R - 1) * W, W)] += both[W:]
            parts[dw, pl.ds(8 + W, W)] += product(f, 0, dw, 1)
            parts[dw, pl.ds(8 + (R - 2) * W, W)] += product(f, 2, dw, R)

    def row_taps(f, row):
        for dw in range(3):
            for dh in range(3):
                at = pl.ds(pl.multiple_of(8 + (row - dh) * W, 8), W)
                parts[dw, at] += lax.dot_general(
                    cb[f, row], cw[f, dh, dw], (((1,), (1,)), ((), ())), preferred_element_type=F32
                )

    def other_halo(f):
        row = hb.at[f, c]
        pl.when(has_near)(send(row, row, s_half.at[f], r_halo.at[f, c], dev(core=o)).wait_recv)

    def halo_taps(frames):
        for f in frames:
            other_halo(f)

        def visit(side):
            rows = jnp.concatenate([hb[f, side] for f in frames], axis=-1)
            for dw in range(3):
                kernel_rows = jnp.concatenate([cw[f, 2 * side, dw] for f in frames], axis=-1)
                parts[dw, pl.ds(8 + side * (T - W), W)] += lax.dot_general(
                    rows, kernel_rows, (((1,), (1,)), ((), ())), preferred_element_type=F32
                )

        both_sides(visit)

    def halos(frames):
        for f in frames:
            relay_halo(f)
        halo_taps(frames)

    from_sibling(2)
    if N > 2:
        pl.when(tm <= 1)(lambda: taps(2, False))
        pl.when(tm >= 2)(lambda: taps(2, True))
    else:
        taps(2, False)

    pl.when(tm == 0)(lambda: halos((0, 2, 1)))
    if N > 1:

        @pl.when(tm >= 1)
        def _():
            late = (0, 2) if N == 2 else (2,)

            def relays():
                for f in late:
                    relay_halo(f)

            pl.when(is_end)(relays)
            forwarded(1, 0)
            pl.when(is_end)(lambda: halo_taps(late))
            edge_row(1)
            outer_taps(1)
            pl.when(inner)(relays)
            relay_halo(1)
            pl.when(inner)(lambda: halo_taps(late))
            forwarded(1, 1)
            row_taps(1, jnp.where(c == 0, 2, R - 1))
            halo_taps((1,))
            rest_rows(1)
            row_taps(1, jnp.where(c == 0, R - 1, 2))
    if N > 2:

        @pl.when(tm >= 2)
        def _():
            forwarded(0, 0)
            forwarded(0, 1)
            from_sibling(0)
            taps(0, False)

        pl.when(tm >= 1)(lambda: halos((0,)))

    there = jo.at[pl.ds(o * hr, hr)]
    send(jt, there, s_pair, r_pair, dev(core=o)).wait_recv()
    cell = lax.rem(lax.broadcasted_iota(jnp.int32, (T, S), 0), W)
    before = jnp.where(cell == 0, 0.0, parts[0, pl.ds(7, T)])
    after = jnp.where(cell == W - 1, 0.0, parts[2, pl.ds(9, T)])
    conv = before + parts[1, pl.ds(8, T)] + after
    out_ref[0] = (jo[...].reshape(T, S).astype(F32) + conv).astype(BF16).reshape(R, W, S)

    joined_copy.wait_send()
    for k in range(hr):
        pl.when(z < Z - 1)(rightward(z, k).wait_send)
        pl.when(z > 0)(leftward(z, k).wait_send)
        sideward(z, k, 0).wait_send()
        pl.when(z < Z - 1)(sideward(z, k, 1).wait_send)
    cache_edges(lambda copy: copy.wait_send())
    for f in range(3):
        pl.when(has_back)(relay(f).wait_send)
    near_copies(lambda copy: copy.wait_send())
    for part in (0, 1):
        for hop in (1, 2):
            if N > hop:
                pl.when(tm + hop < N)(along_tm(hop, part).wait_send)

    def spread_done(f):
        edge_copy(f).wait_send()
        rest_copy(f).wait_send()
        if f < 2:
            pl.when(jnp.logical_and(has_near, inner))(near_pass(f).wait_send)

    spread_done(2)
    if N > 1:
        pl.when(tm >= 1)(lambda: spread_done(1))
    if N > 2:
        pl.when(tm >= 2)(lambda: spread_done(0))


def solution(mesh):
    Z, N = mesh.shape["space"], mesh.shape["tm"]

    def body(frames_in, cache, gain_one, gain_two, w_query, w_key, w_value, w_out, conv_weight):
        _, R, W, S = frames_in.shape
        C = 2 * S
        hr, half, T = R // 2, R // 2 * W, R * W
        hops, sets = max(1, min(2, N - 1)), min(3, N)
        dma = pltpu.SemaphoreType.DMA
        hbm = pl.BlockSpec(memory_space=pltpu.HBM)
        vmem = pl.BlockSpec(memory_space=pltpu.VMEM)
        return pl.pallas_call(
            functools.partial(kernel, Z, N),
            out_shape=jax.ShapeDtypeStruct(frames_in.shape, BF16),
            in_specs=[hbm] * 9,
            out_specs=vmem,
            scratch_shapes=[
                pltpu.VMEM((R, W, S), BF16),
                pltpu.VMEM((Z, hr, 2, W, C), BF16),
                pltpu.VMEM((half, C), BF16),
                pltpu.VMEM((half, C), BF16),
                pltpu.VMEM((half, 1), F32),
                pltpu.VMEM((half, 1), F32),
                pltpu.VMEM((half, C), F32),
                pltpu.VMEM((3, R + 2, W, C), BF16),
                pltpu.VMEM((3, 2, W, C), BF16),
                pltpu.VMEM((hr, W, S), BF16),
                pltpu.VMEM((R, W, S), BF16),
                pltpu.VMEM((3, T + 16, S), F32),
                pltpu.VMEM((C,), BF16),
                pltpu.VMEM((C,), BF16),
                pltpu.VMEM((4, C, C), BF16),
                pltpu.VMEM((C, C), BF16),
                pltpu.VMEM((3, 3, 3, S, C), BF16),
                dma((7,)),
                dma,
                dma,
                dma((hr,)),
                dma((hr,)),
                dma((2, hr)),
                dma((Z, hr)),
                dma((Z, hr)),
                dma((2,)),
                dma((3, 2)),
                dma((sets,)),
                dma((sets,)),
                dma((sets,)),
                dma((sets,)),
                dma((sets,)),
                dma((hops, 2)),
                dma((hops, 2)),
                dma((3,)),
            ],
            compiler_params=pltpu.CompilerParams(
                collective_id=0, has_side_effects=True, vmem_limit_bytes=50 << 20
            ),
        )(*(pltpu.with_memory_space_constraint(a, pltpu.HBM) for a in (
            frames_in, cache, gain_one, gain_two,
            w_query, w_key, w_value, w_out, jnp.swapaxes(conv_weight, 3, 4),
        )))

    return jax.shard_map(
        body,
        mesh=mesh,
        in_specs=(
            P(("clips", "tm"), "space", None, "chan"),
            P("clips", "space", None, None),
            P(),
            P(),
            P(),
            P(),
            P(),
            P(),
            P(None, None, None, None, "chan"),
        ),
        out_specs=P(("clips", "tm"), "space", None, "chan"),
        check_vma=False,
    )
```

```python
import functools
import math

import jax
import jax.numpy as jnp
from jax import lax
from jax.experimental import pallas as pl
from jax.experimental.pallas import tpu as pltpu
from jax.sharding import PartitionSpec as P

F32 = jnp.float32
BF16 = jnp.bfloat16
MESH = pl.DeviceIdType.MESH


def normalized(wide, gain):
    factor = lax.rsqrt(jnp.mean(wide * wide, axis=-1, keepdims=True) + 1e-06)
    return wide * factor * gain


def kernel(
    Z, N,
    x_hbm, cache_hbm, g1_hbm, g2_hbm, wq_hbm, wk_hbm, wv_hbm, wo_hbm, cw_hbm,
    out_ref,
    xo, xg, xn, qk, top, total, acc, cb, hb, jt, jo, parts, g1_ref, g2_ref, ws, wvo, cw,
    s_loc, s_pair, r_pair, s_right, s_left, s_sib, r_z, r_sib,
    s_cache, r_halo, s_near, s_edge, s_rest, r_edge, r_rest, s_tm, r_tm, s_half,
):
    z = lax.axis_index("space")
    c = lax.axis_index("chan")
    tm = lax.axis_index("tm")
    o = 1 - c
    R, W, S = out_ref.shape[1:]
    C = 2 * S
    hr = R // 2
    T = R * W
    L = 128
    E = S - L
    blocks = ((0, 0, L), (S, L, L), (L, 2 * L, E), (S + L, 2 * L + E, E))

    def dev(dz=None, core=None, frame=None):
        return {
            "space": z if dz is None else dz,
            "chan": c if core is None else core,
            "tm": tm if frame is None else frame,
        }

    def send(src, dst, ssem, rsem, to):
        return pltpu.make_async_remote_copy(
            src_ref=src, dst_ref=dst, send_sem=ssem, recv_sem=rsem,
            device_id=to, device_id_type=MESH,
        )

    near, back = z + 2 * c - 1, z + 1 - 2 * c
    has_near = jnp.logical_and(near >= 0, near < Z)
    has_back = jnp.logical_and(back >= 0, back < Z)
    is_end = jnp.logical_or(z == 0, z == Z - 1)
    inner = jnp.logical_not(is_end)

    barrier = pltpu.get_barrier_semaphore()

    def greet(to):
        pl.semaphore_signal(barrier, inc=1, device_id=to, device_id_type=MESH)

    greet(dev(core=o))
    pl.when(z > 0)(lambda: greet(dev(dz=z - 1)))
    pl.when(z < Z - 1)(lambda: greet(dev(dz=z + 1)))
    for hop in (1, 2):
        if N > hop:
            pl.when(tm >= hop)(functools.partial(lambda h: greet(dev(frame=tm - h)), hop))

    x_own = pltpu.make_async_copy(x_hbm.at[0], xo, s_loc.at[0])
    x_own.start()
    gains = [
        pltpu.make_async_copy(a, b, s_loc.at[1 + i])
        for i, (a, b) in enumerate(((g1_hbm, g1_ref), (g2_hbm, g2_ref)))
    ]
    for g in gains:
        g.start()
    for i, w_hbm in enumerate((wq_hbm, wk_hbm, wv_hbm)):
        for src, dst, count in blocks:
            pltpu.make_async_copy(w_hbm.at[pl.ds(src, count)], ws.at[i, pl.ds(dst, count)], s_loc.at[3]).start()
    pltpu.make_async_copy(wo_hbm, ws.at[3], s_loc.at[3]).start()
    taps_own = pltpu.make_async_copy(cw_hbm, cw, s_loc.at[4])
    taps_own.start()
    first = jnp.minimum(tm, 1)
    cache_two = pltpu.make_async_copy(cache_hbm.at[first], cb.at[0, pl.ds(1, R)], s_loc.at[5])
    cache_one = pltpu.make_async_copy(cache_hbm.at[1], cb.at[1, pl.ds(1, R)], s_loc.at[6])
    pl.when(tm <= 1)(cache_two.start)
    pl.when(tm == 0)(cache_one.start)

    blank = jnp.zeros((W, C), BF16)
    for f in range(3):
        cb[f, 0] = blank
        cb[f, R + 1] = blank

    x_own.wait()
    for k in range(hr):
        a, b = xo[2 * k], xo[2 * k + 1]
        xg[z, k, c] = jnp.concatenate([a[:, :L], b[:, :L], a[:, L:], b[:, L:]], axis=-1)

    want = 1 + jnp.where(z > 0, 1, 0) + jnp.where(z < Z - 1, 1, 0)
    for hop in (1, 2):
        if N > hop:
            want = want + jnp.where(tm + hop < N, 1, 0)
    pl.semaphore_wait(barrier, want)

    def rightward(j, k):
        return send(xg.at[j, k, c], xg.at[j, k, c], s_right.at[k], r_z.at[j, k], dev(dz=z + 1))

    def leftward(j, k):
        return send(xg.at[j, k, c], xg.at[j, k, c], s_left.at[k], r_z.at[j, k], dev(dz=z - 1))

    def sideward(j, k, flow):
        return send(xg.at[j, k, c], xg.at[j, k, c], s_sib.at[flow, k], r_sib.at[j, k], dev(core=o))

    def outward(k):
        pl.when(z < Z - 1)(rightward(z, k).start)
        pl.when(z > 0)(leftward(z, k).start)

    outward(0)
    for k in range(hr):
        sideward(z, k, 0).start()

    gains[0].wait()
    gain_one = g1_ref[...].astype(F32).reshape(1, C)
    gain_one = jnp.concatenate([gain_one[:, at : at + count] for at, _, count in blocks], axis=-1)
    low_lanes = lax.broadcasted_iota(jnp.int32, (W, L), 1) < E

    def tokens(j, k):
        p, q = xg[j, k, 0].astype(F32), xg[j, k, 1].astype(F32)
        pt, qt = p[:, 2 * L :], q[:, 2 * L :]
        even = jnp.where(low_lanes, pt, pltpu.roll(qt, E, 1))
        odd = jnp.where(low_lanes, pltpu.roll(pt, E, 1), qt)
        return jnp.concatenate([
            jnp.concatenate([p[:, :L], q[:, :L], even], axis=-1),
            jnp.concatenate([p[:, L : 2 * L], q[:, L : 2 * L], odd], axis=-1),
        ], axis=0)

    def normed(wide):
        return normalized(wide, gain_one).astype(BF16)

    top[...] = jnp.full(top.shape, -1e30, F32)
    total[...] = jnp.zeros(total.shape, F32)
    acc[...] = jnp.zeros(acc.shape, F32)

    everything = pl.ds(0, hr * W)

    def attend(keys, at=everything):
        scores = lax.dot_general(qk[at, :], keys, (((1,), (1,)), ((), ())), preferred_element_type=F32)
        old = top[at, :]
        new = jnp.maximum(old, jnp.max(scores, axis=-1, keepdims=True))
        weight = jnp.exp2(scores - new)
        fade = jnp.exp2(old - new)
        top[at, :] = new
        total[at, :] = total[at, :] * fade + jnp.sum(weight, axis=-1, keepdims=True)
        acc[at, :] = acc[at, :] * fade + jnp.dot(weight.astype(BF16), keys, preferred_element_type=F32)

    for k in range(hr):
        sideward(z, k, 0).wait_recv()
    for k in range(1, hr):
        outward(k)
    pltpu.make_async_copy(ws, ws, s_loc.at[3]).wait()
    mine = tokens(z, c)
    xn[...] = jnp.concatenate(
        [mine[:, :L], mine[:, 2 * L : 2 * L + E], mine[:, L : 2 * L], mine[:, 2 * L + E :]], axis=-1
    ).astype(BF16)
    keys = normed(mine)
    query = jnp.dot(keys, ws[0], preferred_element_type=F32).astype(BF16)
    folded = lax.dot_general(query, ws[1], (((1,), (1,)), ((), ())), preferred_element_type=F32)
    qk[...] = (folded * (C ** (-0.5) * math.log2(math.e))).astype(BF16)
    attend(keys)
    attend(normed(tokens(z, o)))
    wvo[...] = jnp.dot(ws[2], ws[3], preferred_element_type=F32).astype(BF16)

    def piece(f, dw, start):
        rows = jnp.concatenate([cb[f, dh : dh + R].reshape(T, C) for dh in range(3)], axis=-1)
        kernel_rows = jnp.concatenate([cw[f, dh, dw] for dh in range(3)], axis=-1)
        value = lax.dot_general(rows, kernel_rows, (((1,), (1,)), ((), ())), preferred_element_type=F32)
        if start:
            parts[dw, pl.ds(8, T)] = value
        else:
            parts[dw, pl.ds(8, T)] += value

    def early(i):
        f, dw = divmod(i, 3)
        there = tm <= 1 if f == 0 else jnp.logical_and(tm == 0, is_end)
        pl.when(there)(lambda: piece(f, dw, f == 0))

    taps_own.wait()
    pl.when(tm <= 1)(cache_two.wait)
    pl.when(tm == 0)(cache_one.wait)
    early(0)

    def cache_edge(f):
        row = jnp.where(c == 0, 0, R - 1)
        source = cache_hbm.at[first if f == 0 else 1, row]
        return send(source, hb.at[f, o], s_cache.at[f], r_halo.at[f, o], dev(dz=near))

    def cache_edges(act):
        pl.when(jnp.logical_and(has_near, tm <= 1))(lambda: act(cache_edge(0)))
        pl.when(jnp.logical_and(has_near, tm == 0))(lambda: act(cache_edge(1)))

    ahead = Z - 1 - z
    longer = jnp.maximum(z, ahead)
    sign = jnp.where(ahead >= z, 1, -1)
    shorter = Z - 1 - longer
    edges_at = jnp.where(c == 0, ahead, z) + 1
    slots = 5
    def step(d, carry):
        lo, hi = z - d, z + d
        has_lo, has_hi = lo >= 0, hi < Z

        for k in range(hr):

            @pl.when(has_lo)
            def _():
                rightward(lo, k).wait_recv()

                @pl.when(z < Z - 1)
                def _():
                    rightward(lo, k).wait_send()
                    rightward(lo, k).start()

                sideward(lo, k, 0).wait_send()
                sideward(lo, k, 0).start()

            @pl.when(has_hi)
            def _():
                leftward(hi, k).wait_recv()

                @pl.when(z > 0)
                def _():
                    leftward(hi, k).wait_send()
                    leftward(hi, k).start()

                pl.when(d > 1)(sideward(hi, k, 1).wait_send)
                sideward(hi, k, 1).start()

            if k == hr - 1:
                pl.when(d == edges_at)(lambda: cache_edges(lambda copy: copy.start()))

            for i in range(slots):
                if i % hr == k:
                    pl.when(d == i // hr + 1)(functools.partial(early, i + 1))

            @pl.when(jnp.logical_and(d > 1, d - 1 <= shorter))
            def _():
                j = z - sign * (d - 1)
                sideward(j, k, 0).wait_recv()
                attend(normed(tokens(j, k)))

            def visit():
                j = z + sign * d
                sideward(j, k, 0).wait_recv()
                attend(normed(tokens(j, k)))

            if k < hr - 1:
                visit()
            else:
                pl.when(d < longer)(visit)

        return carry

    lax.fori_loop(1, longer + 1, step, 0)

    last = z + sign * longer
    sideward(last, hr - 1, 0).wait_recv()
    keys = normed(tokens(last, hr - 1))

    gains[1].wait()
    gain_two = g2_ref[...].astype(F32).reshape(1, C)

    def finish_rows(row, count):
        at = pl.ds(pl.multiple_of(row * W, W), count * W)
        attend(keys, at)
        mixed = (acc[at, :] * (1.0 / total[at, :])).astype(BF16)
        joined = xn[at, :].astype(F32) + jnp.dot(mixed, wvo[...], preferred_element_type=F32)
        joined = joined.astype(BF16).astype(F32)
        scaled = normalized(joined, gain_two)
        act = (scaled / (1.0 + jnp.exp(-scaled))).astype(BF16)
        cb[2, pl.ds(1 + c * hr + row, count)] = act.reshape(count, W, C)
        return joined

    def keep_joined(row, count, joined):
        low, high = joined[:, :S].astype(BF16), joined[:, S:].astype(BF16)
        jo[pl.ds(c * hr + row, count)] = jnp.where(c == 0, low, high).reshape(count, W, S)
        jt[pl.ds(row, count)] = jnp.where(c == 0, high, low).reshape(count, W, S)

    edge = jnp.where(c == 0, 1, R)
    rest = jnp.where(c == 0, 2, 1 + hr)
    def along_tm(hop, part):
        row = cb.at[2, edge] if part == 0 else cb.at[2, pl.ds(rest, hr - 1)]
        there = cb.at[2 - hop, edge] if part == 0 else cb.at[2 - hop, pl.ds(rest, hr - 1)]
        return send(row, there, s_tm.at[hop - 1, part], r_tm.at[hop - 1, part], dev(frame=tm + hop))

    def edge_copy(f):
        src = cb.at[f, edge]
        return send(src, src, s_edge.at[2 - f], r_edge.at[2 - f], dev(core=o))

    def near_copy(hop):
        return send(
            cb.at[2, edge], hb.at[2 - hop, o], s_near.at[hop], r_halo.at[2 - hop, o],
            dev(dz=near, frame=tm + hop),
        )

    def near_copies(act):
        pl.when(has_near)(lambda: act(near_copy(0)))
        for hop in range(1, min(3, N)):
            pl.when(jnp.logical_and(jnp.logical_and(has_near, is_end), tm + hop < N))(
                functools.partial(lambda h: act(near_copy(h)), hop)
            )

    def near_pass(f):
        return send(cb.at[f, edge], hb.at[f, o], s_near.at[2 - f], r_halo.at[f, o], dev(dz=near))

    def rest_copy(f):
        src = cb.at[f, pl.ds(rest, hr - 1)]
        return send(src, src, s_rest.at[2 - f], r_rest.at[2 - f], dev(core=o))

    def edge_row(f):
        row = cb.at[f, jnp.where(c == 0, R, 1)]
        send(row, row, s_edge.at[2 - f], r_edge.at[2 - f], dev(core=o)).wait_recv()

    def rest_rows(f):
        rows = cb.at[f, pl.ds(jnp.where(c == 0, 1 + hr, 2), hr - 1)]
        send(rows, rows, s_rest.at[2 - f], r_rest.at[2 - f], dev(core=o)).wait_recv()

    def from_sibling(f):
        edge_row(f)
        rest_rows(f)

    def relay(f):
        row = hb.at[f, o]
        return send(row, row, s_half.at[f], r_halo.at[f, o], dev(core=o))

    def relay_halo(f):
        @pl.when(has_back)
        def _():
            relay(f).wait_recv()
            relay(f).start()

    def both_sides(visit):
        pl.when(z > 0)(lambda: visit(0))
        pl.when(z < Z - 1)(lambda: visit(1))

    for part in (0, 1):
        row, count = (edge - 1 - c * hr, 1) if part == 0 else (rest - 1 - c * hr, hr - 1)
        joined = finish_rows(row, count)
        for hop in (1, 2):
            if N > hop:
                pl.when(tm + hop < N)(along_tm(hop, part).start)
        if part == 0:
            edge_copy(2).start()
            near_copies(lambda copy: copy.start())
        else:
            rest_copy(2).start()
        keep_joined(row, count, joined)

    pl.when(edges_at > longer)(lambda: cache_edges(lambda copy: copy.start()))

    joined_copy = send(jt, jo.at[pl.ds(c * hr, hr)], s_pair, r_pair, dev(core=o))
    joined_copy.start()

    def taps(f, start):
        for dw in range(3):
            piece(f, dw, start)

    def forwarded(f, part):
        along_tm(2 - f, part).wait_recv()
        if part == 0:
            edge_copy(f).start()
            pl.when(jnp.logical_and(has_near, inner))(near_pass(f).start)
        else:
            rest_copy(f).start()

    def product(f, dh, dw, at):
        return lax.dot_general(cb[f, at], cw[f, dh, dw], (((1,), (1,)), ((), ())), preferred_element_type=F32)

    def outer_taps(f):
        for dw in range(3):
            rows = jnp.concatenate([cb[f, 1], cb[f, R]], axis=0)
            both = lax.dot_general(rows, cw[f, 1, dw], (((1,), (1,)), ((), ())), preferred_element_type=F32)
            parts[dw, pl.ds(8, W)] += both[:W]
            parts[dw, pl.ds(8 + (R - 1) * W, W)] += both[W:]
            parts[dw, pl.ds(8 + W, W)] += product(f, 0, dw, 1)
            parts[dw, pl.ds(8 + (R - 2) * W, W)] += product(f, 2, dw, R)

    def row_taps(f, row):
        for dw in range(3):
            for dh in range(3):
                at = pl.ds(pl.multiple_of(8 + (row - dh) * W, 8), W)
                parts[dw, at] += lax.dot_general(
                    cb[f, row], cw[f, dh, dw], (((1,), (1,)), ((), ())), preferred_element_type=F32
                )

    def other_halo(f):
        row = hb.at[f, c]
        pl.when(has_near)(send(row, row, s_half.at[f], r_halo.at[f, c], dev(core=o)).wait_recv)

    def halo_taps(frames):
        for f in frames:
            other_halo(f)

        def visit(side):
            rows = jnp.concatenate([hb[f, side] for f in frames], axis=-1)
            for dw in range(3):
                kernel_rows = jnp.concatenate([cw[f, 2 * side, dw] for f in frames], axis=-1)
                parts[dw, pl.ds(8 + side * (T - W), W)] += lax.dot_general(
                    rows, kernel_rows, (((1,), (1,)), ((), ())), preferred_element_type=F32
                )

        both_sides(visit)

    def halos(frames):
        for f in frames:
            relay_halo(f)
        halo_taps(frames)

    from_sibling(2)
    if N > 2:
        pl.when(tm <= 1)(lambda: taps(2, False))
        pl.when(tm >= 2)(lambda: taps(2, True))
    else:
        taps(2, False)

    pl.when(jnp.logical_and(tm == 0, inner))(lambda: taps(1, False))
    pl.when(tm == 0)(lambda: halos((0, 2, 1)))
    if N > 1:

        @pl.when(tm >= 1)
        def _():
            late = (0, 2) if N == 2 else (2,)

            def relays():
                for f in late:
                    relay_halo(f)

            pl.when(is_end)(relays)
            forwarded(1, 0)
            pl.when(is_end)(lambda: halo_taps(late))
            edge_row(1)
            outer_taps(1)
            pl.when(is_end)(lambda: relay_halo(1))
            forwarded(1, 1)
            row_taps(1, jnp.where(c == 0, 2, R - 1))
            pl.when(is_end)(lambda: halo_taps((1,)))
            rest_rows(1)
            row_taps(1, jnp.where(c == 0, R - 1, 2))

            @pl.when(inner)
            def _():
                relays()
                relay_halo(1)
                halo_taps(late + (1,))
    if N > 2:

        @pl.when(tm >= 2)
        def _():
            forwarded(0, 0)
            forwarded(0, 1)
            from_sibling(0)
            taps(0, False)

        pl.when(tm >= 1)(lambda: halos((0,)))

    there = jo.at[pl.ds(o * hr, hr)]
    send(jt, there, s_pair, r_pair, dev(core=o)).wait_recv()
    cell = lax.rem(lax.broadcasted_iota(jnp.int32, (T, S), 0), W)
    before = jnp.where(cell == 0, 0.0, parts[0, pl.ds(7, T)])
    after = jnp.where(cell == W - 1, 0.0, parts[2, pl.ds(9, T)])
    conv = before + parts[1, pl.ds(8, T)] + after
    out_ref[0] = (jo[...].reshape(T, S).astype(F32) + conv).astype(BF16).reshape(R, W, S)

    joined_copy.wait_send()
    for k in range(hr):
        pl.when(z < Z - 1)(rightward(z, k).wait_send)
        pl.when(z > 0)(leftward(z, k).wait_send)
        sideward(z, k, 0).wait_send()
        pl.when(z < Z - 1)(sideward(z, k, 1).wait_send)
    cache_edges(lambda copy: copy.wait_send())
    for f in range(3):
        pl.when(has_back)(relay(f).wait_send)
    near_copies(lambda copy: copy.wait_send())
    for part in (0, 1):
        for hop in (1, 2):
            if N > hop:
                pl.when(tm + hop < N)(along_tm(hop, part).wait_send)

    def spread_done(f):
        edge_copy(f).wait_send()
        rest_copy(f).wait_send()
        if f < 2:
            pl.when(jnp.logical_and(has_near, inner))(near_pass(f).wait_send)

    spread_done(2)
    if N > 1:
        pl.when(tm >= 1)(lambda: spread_done(1))
    if N > 2:
        pl.when(tm >= 2)(lambda: spread_done(0))


def solution(mesh):
    Z, N = mesh.shape["space"], mesh.shape["tm"]

    def body(frames_in, cache, gain_one, gain_two, w_query, w_key, w_value, w_out, conv_weight):
        _, R, W, S = frames_in.shape
        C = 2 * S
        hr, half, T = R // 2, R // 2 * W, R * W
        hops, sets = max(1, min(2, N - 1)), min(3, N)
        dma = pltpu.SemaphoreType.DMA
        hbm = pl.BlockSpec(memory_space=pltpu.HBM)
        vmem = pl.BlockSpec(memory_space=pltpu.VMEM)
        return pl.pallas_call(
            functools.partial(kernel, Z, N),
            out_shape=jax.ShapeDtypeStruct(frames_in.shape, BF16),
            in_specs=[hbm] * 9,
            out_specs=vmem,
            scratch_shapes=[
                pltpu.VMEM((R, W, S), BF16),
                pltpu.VMEM((Z, hr, 2, W, C), BF16),
                pltpu.VMEM((half, C), BF16),
                pltpu.VMEM((half, C), BF16),
                pltpu.VMEM((half, 1), F32),
                pltpu.VMEM((half, 1), F32),
                pltpu.VMEM((half, C), F32),
                pltpu.VMEM((3, R + 2, W, C), BF16),
                pltpu.VMEM((3, 2, W, C), BF16),
                pltpu.VMEM((hr, W, S), BF16),
                pltpu.VMEM((R, W, S), BF16),
                pltpu.VMEM((3, T + 16, S), F32),
                pltpu.VMEM((C,), BF16),
                pltpu.VMEM((C,), BF16),
                pltpu.VMEM((4, C, C), BF16),
                pltpu.VMEM((C, C), BF16),
                pltpu.VMEM((3, 3, 3, S, C), BF16),
                dma((7,)),
                dma,
                dma,
                dma((hr,)),
                dma((hr,)),
                dma((2, hr)),
                dma((Z, hr)),
                dma((Z, hr)),
                dma((2,)),
                dma((3, 2)),
                dma((sets,)),
                dma((sets,)),
                dma((sets,)),
                dma((sets,)),
                dma((sets,)),
                dma((hops, 2)),
                dma((hops, 2)),
                dma((3,)),
            ],
            compiler_params=pltpu.CompilerParams(
                collective_id=0, has_side_effects=True, vmem_limit_bytes=50 << 20
            ),
        )(*(pltpu.with_memory_space_constraint(a, pltpu.HBM) for a in (
            frames_in, cache, gain_one, gain_two,
            w_query, w_key, w_value, w_out, jnp.swapaxes(conv_weight, 3, 4),
        )))

    return jax.shard_map(
        body,
        mesh=mesh,
        in_specs=(
            P(("clips", "tm"), "space", None, "chan"),
            P("clips", "space", None, None),
            P(),
            P(),
            P(),
            P(),
            P(),
            P(),
            P(None, None, None, None, "chan"),
        ),
        out_specs=P(("clips", "tm"), "space", None, "chan"),
        check_vma=False,
    )
```

```python
import functools
import math

import jax
import jax.numpy as jnp
from jax import lax
from jax.experimental import pallas as pl
from jax.experimental.pallas import tpu as pltpu
from jax.sharding import PartitionSpec as P

F32 = jnp.float32
BF16 = jnp.bfloat16
MESH = pl.DeviceIdType.MESH


def normalized(wide, gain):
    factor = lax.rsqrt(jnp.mean(wide * wide, axis=-1, keepdims=True) + 1e-06)
    return wide * factor * gain


def kernel(
    Z, N,
    x_hbm, cache_hbm, g1_hbm, g2_hbm, wq_hbm, wk_hbm, wv_hbm, wo_hbm, cw_hbm,
    out_ref,
    xo, xg, xn, qk, top, total, acc, cb, hb, jt, jo, parts, g1_ref, g2_ref, ws, wvo, cw,
    s_loc, s_pair, r_pair, s_right, s_left, s_sib, r_z, r_sib,
    s_cache, r_halo, s_near, s_edge, s_rest, r_edge, r_rest, s_tm, r_tm, s_half,
):
    z = lax.axis_index("space")
    c = lax.axis_index("chan")
    tm = lax.axis_index("tm")
    o = 1 - c
    R, W, S = out_ref.shape[1:]
    C = 2 * S
    hr = R // 2
    T = R * W
    L = 128
    E = S - L
    blocks = ((0, 0, L), (S, L, L), (L, 2 * L, E), (S + L, 2 * L + E, E))

    def dev(dz=None, core=None, frame=None):
        return {
            "space": z if dz is None else dz,
            "chan": c if core is None else core,
            "tm": tm if frame is None else frame,
        }

    def send(src, dst, ssem, rsem, to):
        return pltpu.make_async_remote_copy(
            src_ref=src, dst_ref=dst, send_sem=ssem, recv_sem=rsem,
            device_id=to, device_id_type=MESH,
        )

    near, back = z + 2 * c - 1, z + 1 - 2 * c
    has_near = jnp.logical_and(near >= 0, near < Z)
    has_back = jnp.logical_and(back >= 0, back < Z)
    is_end = jnp.logical_or(z == 0, z == Z - 1)
    inner = jnp.logical_not(is_end)

    barrier = pltpu.get_barrier_semaphore()

    def greet(to):
        pl.semaphore_signal(barrier, inc=1, device_id=to, device_id_type=MESH)

    greet(dev(core=o))
    pl.when(z > 0)(lambda: greet(dev(dz=z - 1)))
    pl.when(z < Z - 1)(lambda: greet(dev(dz=z + 1)))
    for hop in (1, 2):
        if N > hop:
            pl.when(tm >= hop)(functools.partial(lambda h: greet(dev(frame=tm - h)), hop))

    x_own = pltpu.make_async_copy(x_hbm.at[0], xo, s_loc.at[0])
    x_own.start()
    gains = [
        pltpu.make_async_copy(a, b, s_loc.at[1 + i])
        for i, (a, b) in enumerate(((g1_hbm, g1_ref), (g2_hbm, g2_ref)))
    ]
    for g in gains:
        g.start()
    for i, w_hbm in enumerate((wq_hbm, wk_hbm, wv_hbm)):
        for src, dst, count in blocks:
            pltpu.make_async_copy(w_hbm.at[pl.ds(src, count)], ws.at[i, pl.ds(dst, count)], s_loc.at[3]).start()
    pltpu.make_async_copy(wo_hbm, ws.at[3], s_loc.at[3]).start()
    taps_own = pltpu.make_async_copy(cw_hbm, cw, s_loc.at[4])
    taps_own.start()
    first = jnp.minimum(tm, 1)
    cache_two = pltpu.make_async_copy(cache_hbm.at[first], cb.at[0, pl.ds(1, R)], s_loc.at[5])
    cache_one = pltpu.make_async_copy(cache_hbm.at[1], cb.at[1, pl.ds(1, R)], s_loc.at[6])
    pl.when(tm <= 1)(cache_two.start)
    pl.when(tm == 0)(cache_one.start)

    blank = jnp.zeros((W, C), BF16)
    for f in range(3):
        cb[f, 0] = blank
        cb[f, R + 1] = blank

    x_own.wait()
    for k in range(hr):
        a, b = xo[2 * k], xo[2 * k + 1]
        xg[z, k, c] = jnp.concatenate([a[:, :L], b[:, :L], a[:, L:], b[:, L:]], axis=-1)

    want = 1 + jnp.where(z > 0, 1, 0) + jnp.where(z < Z - 1, 1, 0)
    for hop in (1, 2):
        if N > hop:
            want = want + jnp.where(tm + hop < N, 1, 0)
    pl.semaphore_wait(barrier, want)

    def rightward(j, k):
        return send(xg.at[j, k, c], xg.at[j, k, c], s_right.at[k], r_z.at[j, k], dev(dz=z + 1))

    def leftward(j, k):
        return send(xg.at[j, k, c], xg.at[j, k, c], s_left.at[k], r_z.at[j, k], dev(dz=z - 1))

    def sideward(j, k, flow):
        return send(xg.at[j, k, c], xg.at[j, k, c], s_sib.at[flow, k], r_sib.at[j, k], dev(core=o))

    def outward(k):
        pl.when(z < Z - 1)(rightward(z, k).start)
        pl.when(z > 0)(leftward(z, k).start)

    outward(0)
    for k in range(hr):
        sideward(z, k, 0).start()

    gains[0].wait()
    gain_one = g1_ref[...].astype(F32).reshape(1, C)
    gain_one = jnp.concatenate([gain_one[:, at : at + count] for at, _, count in blocks], axis=-1)
    low_lanes = lax.broadcasted_iota(jnp.int32, (W, L), 1) < E

    def tokens(j, k):
        p, q = xg[j, k, 0].astype(F32), xg[j, k, 1].astype(F32)
        pt, qt = p[:, 2 * L :], q[:, 2 * L :]
        even = jnp.where(low_lanes, pt, pltpu.roll(qt, E, 1))
        odd = jnp.where(low_lanes, pltpu.roll(pt, E, 1), qt)
        return jnp.concatenate([
            jnp.concatenate([p[:, :L], q[:, :L], even], axis=-1),
            jnp.concatenate([p[:, L : 2 * L], q[:, L : 2 * L], odd], axis=-1),
        ], axis=0)

    def normed(wide):
        return normalized(wide, gain_one).astype(BF16)

    top[...] = jnp.full(top.shape, -1e30, F32)
    total[...] = jnp.zeros(total.shape, F32)
    acc[...] = jnp.zeros(acc.shape, F32)

    everything = pl.ds(0, hr * W)

    def attend(keys, at=everything):
        scores = lax.dot_general(qk[at, :], keys, (((1,), (1,)), ((), ())), preferred_element_type=F32)
        old = top[at, :]
        new = jnp.maximum(old, jnp.max(scores, axis=-1, keepdims=True))
        weight = jnp.exp2(scores - new)
        fade = jnp.exp2(old - new)
        top[at, :] = new
        total[at, :] = total[at, :] * fade + jnp.sum(weight, axis=-1, keepdims=True)
        acc[at, :] = acc[at, :] * fade + jnp.dot(weight.astype(BF16), keys, preferred_element_type=F32)

    for k in range(hr):
        sideward(z, k, 0).wait_recv()
    for k in range(1, hr):
        outward(k)
    pltpu.make_async_copy(ws, ws, s_loc.at[3]).wait()
    mine = tokens(z, c)
    xn[...] = jnp.concatenate(
        [mine[:, :L], mine[:, 2 * L : 2 * L + E], mine[:, L : 2 * L], mine[:, 2 * L + E :]], axis=-1
    ).astype(BF16)
    keys = normed(mine)
    query = jnp.dot(keys, ws[0], preferred_element_type=F32).astype(BF16)
    folded = lax.dot_general(query, ws[1], (((1,), (1,)), ((), ())), preferred_element_type=F32)
    qk[...] = (folded * (C ** (-0.5) * math.log2(math.e))).astype(BF16)
    attend(keys)
    attend(normed(tokens(z, o)))
    wvo[...] = jnp.dot(ws[2], ws[3], preferred_element_type=F32).astype(BF16)

    def piece(f, dw, start):
        rows = jnp.concatenate([cb[f, dh : dh + R].reshape(T, C) for dh in range(3)], axis=-1)
        kernel_rows = jnp.concatenate([cw[f, dh, dw] for dh in range(3)], axis=-1)
        value = lax.dot_general(rows, kernel_rows, (((1,), (1,)), ((), ())), preferred_element_type=F32)
        if start:
            parts[dw, pl.ds(8, T)] = value
        else:
            parts[dw, pl.ds(8, T)] += value

    def early(i):
        f, dw = divmod(i, 3)
        there = tm <= 1 if f == 0 else jnp.logical_and(tm == 0, is_end)
        pl.when(there)(lambda: piece(f, dw, f == 0))

    taps_own.wait()
    pl.when(tm <= 1)(cache_two.wait)
    pl.when(tm == 0)(cache_one.wait)
    early(0)

    def cache_edge(f):
        row = jnp.where(c == 0, 0, R - 1)
        source = cache_hbm.at[first if f == 0 else 1, row]
        return send(source, hb.at[f, o], s_cache.at[f], r_halo.at[f, o], dev(dz=near))

    def cache_edges(act):
        pl.when(jnp.logical_and(has_near, tm <= 1))(lambda: act(cache_edge(0)))
        pl.when(jnp.logical_and(has_near, tm == 0))(lambda: act(cache_edge(1)))

    ahead = Z - 1 - z
    longer = jnp.maximum(z, ahead)
    sign = jnp.where(ahead >= z, 1, -1)
    shorter = Z - 1 - longer
    edges_at = jnp.where(c == 0, ahead, z) + 1
    slots = 5
    def step(d, carry):
        lo, hi = z - d, z + d
        has_lo, has_hi = lo >= 0, hi < Z

        for k in range(hr):

            @pl.when(has_lo)
            def _():
                rightward(lo, k).wait_recv()

                @pl.when(z < Z - 1)
                def _():
                    rightward(lo, k).wait_send()
                    rightward(lo, k).start()

                sideward(lo, k, 0).wait_send()
                sideward(lo, k, 0).start()

            @pl.when(has_hi)
            def _():
                leftward(hi, k).wait_recv()

                @pl.when(z > 0)
                def _():
                    leftward(hi, k).wait_send()
                    leftward(hi, k).start()

                pl.when(d > 1)(sideward(hi, k, 1).wait_send)
                sideward(hi, k, 1).start()

            if k == hr - 1:
                pl.when(d == edges_at)(lambda: cache_edges(lambda copy: copy.start()))

            for i in range(slots):
                if i % hr == k:
                    pl.when(d == i // hr + 1)(functools.partial(early, i + 1))

            @pl.when(jnp.logical_and(d > 1, d - 1 <= shorter))
            def _():
                j = z - sign * (d - 1)
                sideward(j, k, 0).wait_recv()
                attend(normed(tokens(j, k)))

            def visit():
                j = z + sign * d
                sideward(j, k, 0).wait_recv()
                attend(normed(tokens(j, k)))

            if k < hr - 1:
                visit()
            else:
                pl.when(d < longer)(visit)

        return carry

    lax.fori_loop(1, longer + 1, step, 0)

    last = z + sign * longer
    sideward(last, hr - 1, 0).wait_recv()
    keys = normed(tokens(last, hr - 1))

    gains[1].wait()
    gain_two = g2_ref[...].astype(F32).reshape(1, C)

    def finish_rows(row, count):
        at = pl.ds(pl.multiple_of(row * W, W), count * W)
        attend(keys, at)
        mixed = (acc[at, :] * (1.0 / total[at, :])).astype(BF16)
        joined = xn[at, :].astype(F32) + jnp.dot(mixed, wvo[...], preferred_element_type=F32)
        joined = joined.astype(BF16).astype(F32)
        scaled = normalized(joined, gain_two)
        act = (scaled / (1.0 + jnp.exp(-scaled))).astype(BF16)
        cb[2, pl.ds(1 + c * hr + row, count)] = act.reshape(count, W, C)
        return joined

    def keep_joined(row, count, joined):
        low, high = joined[:, :S].astype(BF16), joined[:, S:].astype(BF16)
        jo[pl.ds(c * hr + row, count)] = jnp.where(c == 0, low, high).reshape(count, W, S)
        jt[pl.ds(row, count)] = jnp.where(c == 0, high, low).reshape(count, W, S)

    edge = jnp.where(c == 0, 1, R)
    rest = jnp.where(c == 0, 2, 1 + hr)
    other = jnp.where(c == 0, 1 + hr, 2)
    tail = W // 5
    head = W - tail
    spans = ((0, W), (0, head), (head, tail), (head, tail))
    def along_tm(hop, part):
        cells = pl.ds(*spans[part])
        src, dst = (cb.at[f, rest if part else edge, cells] for f in (2, 2 - hop))
        to = dev(frame=tm + hop, core=o if part == 3 else None)
        return send(src, dst, s_tm.at[hop - 1, part], r_tm.at[hop - 1, part], to)

    def from_tm(f, part):
        row = cb.at[f, (edge, rest, rest, other)[part], pl.ds(*spans[part])]
        send(row, row, s_tm.at[1 - f, part], r_tm.at[1 - f, part], dev(core=o)).wait_recv()

    def edge_copy(f):
        src = cb.at[f, edge]
        return send(src, src, s_edge.at[2 - f], r_edge.at[2 - f], dev(core=o))

    def near_copy(hop):
        return send(
            cb.at[2, edge], hb.at[2 - hop, o], s_near.at[hop], r_halo.at[2 - hop, o],
            dev(dz=near, frame=tm + hop),
        )

    def near_copies(act):
        pl.when(has_near)(lambda: act(near_copy(0)))
        for hop in range(1, min(3, N)):
            pl.when(jnp.logical_and(jnp.logical_and(has_near, is_end), tm + hop < N))(
                functools.partial(lambda h: act(near_copy(h)), hop)
            )

    def near_pass(f):
        return send(cb.at[f, edge], hb.at[f, o], s_near.at[2 - f], r_halo.at[f, o], dev(dz=near))

    def rest_copy(f):
        src = cb.at[f, rest, pl.ds(0, W if f == 2 else head)]
        return send(src, src, s_rest.at[2 - f], r_rest.at[2 - f], dev(core=o))

    def edge_row(f):
        row = cb.at[f, jnp.where(c == 0, R, 1)]
        send(row, row, s_edge.at[2 - f], r_edge.at[2 - f], dev(core=o)).wait_recv()

    def rest_row(f):
        row = cb.at[f, other, pl.ds(0, W if f == 2 else head)]
        send(row, row, s_rest.at[2 - f], r_rest.at[2 - f], dev(core=o)).wait_recv()

    def from_sibling(f):
        edge_row(f)
        rest_row(f)

    def relay(f):
        row = hb.at[f, o]
        return send(row, row, s_half.at[f], r_halo.at[f, o], dev(core=o))

    def relay_halo(f):
        @pl.when(has_back)
        def _():
            relay(f).wait_recv()
            relay(f).start()

    def both_sides(visit):
        pl.when(z > 0)(lambda: visit(0))
        pl.when(z < Z - 1)(lambda: visit(1))

    for part in (0, 1):
        row = (rest if part else edge) - 1 - c * hr
        joined = finish_rows(row, 1)
        for hop in (1, 2):
            if N > hop:
                for p in (1, 2, 3) if part else (0,):
                    pl.when(tm + hop < N)(along_tm(hop, p).start)
        if part == 0:
            edge_copy(2).start()
            near_copies(lambda copy: copy.start())
        else:
            rest_copy(2).start()
        keep_joined(row, 1, joined)

    pl.when(edges_at > longer)(lambda: cache_edges(lambda copy: copy.start()))

    joined_copy = send(jt, jo.at[pl.ds(c * hr, hr)], s_pair, r_pair, dev(core=o))
    joined_copy.start()

    def taps(f, start):
        for dw in range(3):
            piece(f, dw, start)

    def forwarded(f, part):
        from_tm(f, part)
        if part == 0:
            edge_copy(f).start()
            pl.when(jnp.logical_and(has_near, inner))(near_pass(f).start)
        else:
            rest_copy(f).start()

    def product(f, dh, dw, at):
        return lax.dot_general(cb[f, at], cw[f, dh, dw], (((1,), (1,)), ((), ())), preferred_element_type=F32)

    def outer_taps(f):
        for dw in range(3):
            rows = jnp.concatenate([cb[f, 1], cb[f, R]], axis=0)
            both = lax.dot_general(rows, cw[f, 1, dw], (((1,), (1,)), ((), ())), preferred_element_type=F32)
            parts[dw, pl.ds(8, W)] += both[:W]
            parts[dw, pl.ds(8 + (R - 1) * W, W)] += both[W:]
            parts[dw, pl.ds(8 + W, W)] += product(f, 0, dw, 1)
            parts[dw, pl.ds(8 + (R - 2) * W, W)] += product(f, 2, dw, R)

    def row_taps(f, pieces):
        rows = jnp.concatenate([cb[f, row, at : at + count] for row, at, count in pieces], axis=0)
        for dw in range(3):
            for dh in range(3):
                value = lax.dot_general(rows, cw[f, dh, dw], (((1,), (1,)), ((), ())), preferred_element_type=F32)
                start = 0
                for row, at, count in pieces:
                    place = pl.ds(pl.multiple_of(8 + (row - dh) * W + at, 8), count)
                    parts[dw, place] += value[start : start + count]
                    start += count

    def other_halo(f):
        row = hb.at[f, c]
        pl.when(has_near)(send(row, row, s_half.at[f], r_halo.at[f, c], dev(core=o)).wait_recv)

    def halo_taps(frames):
        for f in frames:
            other_halo(f)

        def visit(side):
            rows = jnp.concatenate([hb[f, side] for f in frames], axis=-1)
            for dw in range(3):
                kernel_rows = jnp.concatenate([cw[f, 2 * side, dw] for f in frames], axis=-1)
                parts[dw, pl.ds(8 + side * (T - W), W)] += lax.dot_general(
                    rows, kernel_rows, (((1,), (1,)), ((), ())), preferred_element_type=F32
                )

        both_sides(visit)

    def halos(frames):
        for f in frames:
            relay_halo(f)
        halo_taps(frames)

    late = (0, 2) if N == 2 else (2,)

    def relays():
        for f in late:
            relay_halo(f)

    pl.when(jnp.logical_and(tm >= 1, is_end))(relays)
    from_sibling(2)
    if N > 2:
        pl.when(tm <= 1)(lambda: taps(2, False))
        pl.when(tm >= 2)(lambda: taps(2, True))
    else:
        taps(2, False)

    there = jo.at[pl.ds(o * hr, hr)]
    send(jt, there, s_pair, r_pair, dev(core=o)).wait_recv()
    parts[1, pl.ds(8, T)] += jo[...].reshape(T, S).astype(F32)

    pl.when(jnp.logical_and(tm == 0, inner))(lambda: taps(1, False))
    pl.when(tm == 0)(lambda: halos((0, 2, 1)))
    if N > 1:

        @pl.when(tm >= 1)
        def _():
            pl.when(is_end)(lambda: relay_halo(1))
            forwarded(1, 0)
            pl.when(is_end)(lambda: halo_taps(late + (1,)))
            edge_row(1)
            outer_taps(1)
            forwarded(1, 1)
            row_taps(1, ((rest, 0, head),))
            from_tm(1, 2)
            from_tm(1, 3)
            rest_row(1)
            row_taps(1, ((rest, head, tail), (other, 0, W)))

            @pl.when(inner)
            def _():
                relays()
                relay_halo(1)
                halo_taps(late + (1,))
    if N > 2:

        @pl.when(tm >= 2)
        def _():
            forwarded(0, 0)
            forwarded(0, 1)
            from_tm(0, 2)
            from_tm(0, 3)
            from_sibling(0)
            taps(0, False)

        pl.when(tm >= 1)(lambda: halos((0,)))

    cell = lax.rem(lax.broadcasted_iota(jnp.int32, (T, S), 0), W)
    before = jnp.where(cell == 0, 0.0, parts[0, pl.ds(7, T)])
    after = jnp.where(cell == W - 1, 0.0, parts[2, pl.ds(9, T)])
    out_ref[0] = (before + parts[1, pl.ds(8, T)] + after).astype(BF16).reshape(R, W, S)

    joined_copy.wait_send()
    for k in range(hr):
        pl.when(z < Z - 1)(rightward(z, k).wait_send)
        pl.when(z > 0)(leftward(z, k).wait_send)
        sideward(z, k, 0).wait_send()
        pl.when(z < Z - 1)(sideward(z, k, 1).wait_send)
    cache_edges(lambda copy: copy.wait_send())
    for f in range(3):
        pl.when(has_back)(relay(f).wait_send)
    near_copies(lambda copy: copy.wait_send())
    for part in range(4):
        for hop in (1, 2):
            if N > hop:
                pl.when(tm + hop < N)(along_tm(hop, part).wait_send)

    def spread_done(f):
        edge_copy(f).wait_send()
        rest_copy(f).wait_send()
        if f < 2:
            pl.when(jnp.logical_and(has_near, inner))(near_pass(f).wait_send)

    spread_done(2)
    if N > 1:
        pl.when(tm >= 1)(lambda: spread_done(1))
    if N > 2:
        pl.when(tm >= 2)(lambda: spread_done(0))


def solution(mesh):
    Z, N = mesh.shape["space"], mesh.shape["tm"]

    def body(frames_in, cache, gain_one, gain_two, w_query, w_key, w_value, w_out, conv_weight):
        _, R, W, S = frames_in.shape
        C = 2 * S
        hr, half, T = R // 2, R // 2 * W, R * W
        hops, sets = max(1, min(2, N - 1)), min(3, N)
        dma = pltpu.SemaphoreType.DMA
        hbm = pl.BlockSpec(memory_space=pltpu.HBM)
        vmem = pl.BlockSpec(memory_space=pltpu.VMEM)
        return pl.pallas_call(
            functools.partial(kernel, Z, N),
            out_shape=jax.ShapeDtypeStruct(frames_in.shape, BF16),
            in_specs=[hbm] * 9,
            out_specs=vmem,
            scratch_shapes=[
                pltpu.VMEM((R, W, S), BF16),
                pltpu.VMEM((Z, hr, 2, W, C), BF16),
                pltpu.VMEM((half, C), BF16),
                pltpu.VMEM((half, C), BF16),
                pltpu.VMEM((half, 1), F32),
                pltpu.VMEM((half, 1), F32),
                pltpu.VMEM((half, C), F32),
                pltpu.VMEM((3, R + 2, W, C), BF16),
                pltpu.VMEM((3, 2, W, C), BF16),
                pltpu.VMEM((hr, W, S), BF16),
                pltpu.VMEM((R, W, S), BF16),
                pltpu.VMEM((3, T + 16, S), F32),
                pltpu.VMEM((C,), BF16),
                pltpu.VMEM((C,), BF16),
                pltpu.VMEM((4, C, C), BF16),
                pltpu.VMEM((C, C), BF16),
                pltpu.VMEM((3, 3, 3, S, C), BF16),
                dma((7,)),
                dma,
                dma,
                dma((hr,)),
                dma((hr,)),
                dma((2, hr)),
                dma((Z, hr)),
                dma((Z, hr)),
                dma((2,)),
                dma((3, 2)),
                dma((sets,)),
                dma((sets,)),
                dma((sets,)),
                dma((sets,)),
                dma((sets,)),
                dma((hops, 4)),
                dma((hops, 4)),
                dma((3,)),
            ],
            compiler_params=pltpu.CompilerParams(
                collective_id=0, has_side_effects=True, vmem_limit_bytes=50 << 20
            ),
        )(*(pltpu.with_memory_space_constraint(a, pltpu.HBM) for a in (
            frames_in, cache, gain_one, gain_two,
            w_query, w_key, w_value, w_out, jnp.swapaxes(conv_weight, 3, 4),
        )))

    return jax.shard_map(
        body,
        mesh=mesh,
        in_specs=(
            P(("clips", "tm"), "space", None, "chan"),
            P("clips", "space", None, None),
            P(),
            P(),
            P(),
            P(),
            P(),
            P(),
            P(None, None, None, None, "chan"),
        ),
        out_specs=P(("clips", "tm"), "space", None, "chan"),
        check_vma=False,
    )
```

```python
import functools
import math

import jax
import jax.numpy as jnp
from jax import lax
from jax.experimental import pallas as pl
from jax.experimental.pallas import tpu as pltpu
from jax.sharding import PartitionSpec as P

F32 = jnp.float32
BF16 = jnp.bfloat16
MESH = pl.DeviceIdType.MESH


def normalized(wide, gain):
    factor = lax.rsqrt(jnp.mean(wide * wide, axis=-1, keepdims=True) + 1e-06)
    return wide * factor * gain


def kernel(
    Z, N,
    x_hbm, cache_hbm, g1_hbm, g2_hbm, wq_hbm, wk_hbm, wv_hbm, wo_hbm, cw_hbm,
    out_ref,
    xo, xg, xn, qk, top, total, acc, cb, hb, jt, jo, parts, g1_ref, g2_ref, ws, wvo, cw,
    s_loc, s_pair, r_pair, s_right, s_left, s_sib, r_z, r_sib, s_last, r_last,
    s_cache, r_halo, s_near, s_edge, s_rest, r_edge, r_rest, s_tm, r_tm, s_half,
):
    z = lax.axis_index("space")
    c = lax.axis_index("chan")
    tm = lax.axis_index("tm")
    o = 1 - c
    R, W, S = out_ref.shape[1:]
    C = 2 * S
    hr = R // 2
    T = R * W
    tail = W // 5
    head = W - tail
    L = 128
    E = S - L
    blocks = ((0, 0, L), (S, L, L), (L, 2 * L, E), (S + L, 2 * L + E, E))

    def dev(dz=None, core=None, frame=None):
        return {
            "space": z if dz is None else dz,
            "chan": c if core is None else core,
            "tm": tm if frame is None else frame,
        }

    def send(src, dst, ssem, rsem, to):
        return pltpu.make_async_remote_copy(
            src_ref=src, dst_ref=dst, send_sem=ssem, recv_sem=rsem,
            device_id=to, device_id_type=MESH,
        )

    near, back = z + 2 * c - 1, z + 1 - 2 * c
    has_near = jnp.logical_and(near >= 0, near < Z)
    has_back = jnp.logical_and(back >= 0, back < Z)
    is_end = jnp.logical_or(z == 0, z == Z - 1)
    inner = jnp.logical_not(is_end)

    barrier = pltpu.get_barrier_semaphore()

    def greet(to):
        pl.semaphore_signal(barrier, inc=1, device_id=to, device_id_type=MESH)

    greet(dev(core=o))
    pl.when(z > 0)(lambda: greet(dev(dz=z - 1)))
    pl.when(z < Z - 1)(lambda: greet(dev(dz=z + 1)))
    for hop in (1, 2):
        if N > hop:
            pl.when(tm >= hop)(functools.partial(lambda h: greet(dev(frame=tm - h)), hop))

    x_own = pltpu.make_async_copy(x_hbm.at[0], xo, s_loc.at[0])
    x_own.start()
    gains = [
        pltpu.make_async_copy(a, b, s_loc.at[1 + i])
        for i, (a, b) in enumerate(((g1_hbm, g1_ref), (g2_hbm, g2_ref)))
    ]
    for g in gains:
        g.start()
    for i, w_hbm in enumerate((wq_hbm, wk_hbm, wv_hbm)):
        for src, dst, count in blocks:
            pltpu.make_async_copy(w_hbm.at[pl.ds(src, count)], ws.at[i, pl.ds(dst, count)], s_loc.at[3]).start()
    pltpu.make_async_copy(wo_hbm, ws.at[3], s_loc.at[3]).start()
    taps_own = pltpu.make_async_copy(cw_hbm, cw, s_loc.at[4])
    taps_own.start()
    first = jnp.minimum(tm, 1)
    cache_two = pltpu.make_async_copy(cache_hbm.at[first], cb.at[0, pl.ds(1, R)], s_loc.at[5])
    cache_one = pltpu.make_async_copy(cache_hbm.at[1], cb.at[1, pl.ds(1, R)], s_loc.at[6])
    pl.when(tm <= 1)(cache_two.start)
    pl.when(tm == 0)(cache_one.start)

    blank = jnp.zeros((W, C), BF16)
    for f in range(3):
        cb[f, 0] = blank
        cb[f, R + 1] = blank

    x_own.wait()
    for k in range(hr):
        a, b = xo[2 * k], xo[2 * k + 1]
        xg[z, k, c] = jnp.concatenate([a[:, :L], b[:, :L], a[:, L:], b[:, L:]], axis=-1)

    want = 1 + jnp.where(z > 0, 1, 0) + jnp.where(z < Z - 1, 1, 0)
    for hop in (1, 2):
        if N > hop:
            want = want + jnp.where(tm + hop < N, 1, 0)
    pl.semaphore_wait(barrier, want)

    def rightward(j, k, n=W):
        ref = xg.at[j, k, c, pl.ds(0, n)]
        return send(ref, ref, s_right.at[k], r_z.at[j, k], dev(dz=z + 1))

    def leftward(j, k, n=W):
        ref = xg.at[j, k, c, pl.ds(0, n)]
        return send(ref, ref, s_left.at[k], r_z.at[j, k], dev(dz=z - 1))

    def sideward(j, k, flow, n=W):
        ref = xg.at[j, k, c, pl.ds(0, n)]
        return send(ref, ref, s_sib.at[flow, k], r_sib.at[j, k], dev(core=o))

    def closing(j, kind, core, to):
        ref = xg.at[j, hr - 1, core, pl.ds(head, tail)]
        return send(ref, ref, s_last.at[kind], r_last.at[kind], dev(dz=to, core=o if kind else c))

    def outward(k):
        pl.when(z < Z - 1)(rightward(z, k).start)
        pl.when(z > 0)(leftward(z, k).start)

    outward(0)
    for k in range(hr):
        sideward(z, k, 0).start()

    gains[0].wait()
    gain_one = g1_ref[...].astype(F32).reshape(1, C)
    gain_one = jnp.concatenate([gain_one[:, at : at + count] for at, _, count in blocks], axis=-1)
    low_lanes = lax.broadcasted_iota(jnp.int32, (W, L), 1) < E

    def tokens(j, k):
        p, q = xg[j, k, 0].astype(F32), xg[j, k, 1].astype(F32)
        pt, qt = p[:, 2 * L :], q[:, 2 * L :]
        even = jnp.where(low_lanes, pt, pltpu.roll(qt, E, 1))
        odd = jnp.where(low_lanes, pltpu.roll(pt, E, 1), qt)
        return jnp.concatenate([
            jnp.concatenate([p[:, :L], q[:, :L], even], axis=-1),
            jnp.concatenate([p[:, L : 2 * L], q[:, L : 2 * L], odd], axis=-1),
        ], axis=0)

    def normed(wide):
        return normalized(wide, gain_one).astype(BF16)

    top[...] = jnp.full(top.shape, -1e30, F32)
    total[...] = jnp.zeros(total.shape, F32)
    acc[...] = jnp.zeros(acc.shape, F32)

    everything = pl.ds(0, hr * W)

    def attend(keys, at=everything):
        scores = lax.dot_general(qk[at, :], keys, (((1,), (1,)), ((), ())), preferred_element_type=F32)
        old = top[at, :]
        new = jnp.maximum(old, jnp.max(scores, axis=-1, keepdims=True))
        weight = jnp.exp2(scores - new)
        fade = jnp.exp2(old - new)
        top[at, :] = new
        total[at, :] = total[at, :] * fade + jnp.sum(weight, axis=-1, keepdims=True)
        acc[at, :] = acc[at, :] * fade + jnp.dot(weight.astype(BF16), keys, preferred_element_type=F32)

    for k in range(hr):
        sideward(z, k, 0).wait_recv()
    for k in range(1, hr):
        outward(k)
    pltpu.make_async_copy(ws, ws, s_loc.at[3]).wait()
    mine = tokens(z, c)
    xn[...] = jnp.concatenate(
        [mine[:, :L], mine[:, 2 * L : 2 * L + E], mine[:, L : 2 * L], mine[:, 2 * L + E :]], axis=-1
    ).astype(BF16)
    keys = normed(mine)
    query = jnp.dot(keys, ws[0], preferred_element_type=F32).astype(BF16)
    folded = lax.dot_general(query, ws[1], (((1,), (1,)), ((), ())), preferred_element_type=F32)
    qk[...] = (folded * (C ** (-0.5) * math.log2(math.e))).astype(BF16)
    attend(keys)
    attend(normed(tokens(z, o)))
    wvo[...] = jnp.dot(ws[2], ws[3], preferred_element_type=F32).astype(BF16)

    def piece(f, dw, start):
        rows = jnp.concatenate([cb[f, dh : dh + R].reshape(T, C) for dh in range(3)], axis=-1)
        kernel_rows = jnp.concatenate([cw[f, dh, dw] for dh in range(3)], axis=-1)
        value = lax.dot_general(rows, kernel_rows, (((1,), (1,)), ((), ())), preferred_element_type=F32)
        if start:
            parts[dw, pl.ds(8, T)] = value
        else:
            parts[dw, pl.ds(8, T)] += value

    def early(i):
        f, dw = divmod(i, 3)
        there = tm <= 1 if f == 0 else jnp.logical_and(tm == 0, is_end)
        pl.when(there)(lambda: piece(f, dw, f == 0))

    taps_own.wait()
    pl.when(tm <= 1)(cache_two.wait)
    pl.when(tm == 0)(cache_one.wait)
    early(0)

    def cache_edge(f):
        row = jnp.where(c == 0, 0, R - 1)
        source = cache_hbm.at[first if f == 0 else 1, row]
        return send(source, hb.at[f, o], s_cache.at[f], r_halo.at[f, o], dev(dz=near))

    def cache_edges(act):
        pl.when(jnp.logical_and(has_near, tm <= 1))(lambda: act(cache_edge(0)))
        pl.when(jnp.logical_and(has_near, tm == 0))(lambda: act(cache_edge(1)))

    ahead = Z - 1 - z
    longer = jnp.maximum(z, ahead)
    sign = jnp.where(ahead >= z, 1, -1)
    shorter = Z - 1 - longer
    edges_at = jnp.where(c == 0, ahead, z) + 1
    slots = 5

    def passing(j, k, d, ward, flow, onward, to, source):
        def give(n):
            ward(j, k).wait_send()
            ward(j, k, n).start()

        def share(n):
            if flow == 0:
                sideward(j, k, 0).wait_send()
            else:
                pl.when(d > 1)(sideward(j, k, 1).wait_send)
            sideward(j, k, flow, n).start()

        if k < hr - 1:
            ward(j, k).wait_recv()
            pl.when(onward)(lambda: give(W))
            share(W)
            return

        closes = jnp.logical_and(j == source, jnp.logical_not(onward))
        before = jnp.logical_and(j == source, jnp.logical_or(to == 0, to == Z - 1))

        @pl.when(closes)
        def _():
            ward(j, k, head).wait_recv()
            share(head)

        @pl.when(jnp.logical_not(closes))
        def _():
            ward(j, k).wait_recv()

            @pl.when(jnp.logical_and(onward, before))
            def _():
                give(head)
                for kind in (0, 1):
                    closing(j, kind, c, to).start()

            pl.when(jnp.logical_and(onward, jnp.logical_not(before)))(lambda: give(W))
            share(W)

    def step(d, carry):
        lo, hi = z - d, z + d

        for k in range(hr):
            pl.when(lo >= 0)(lambda: passing(lo, k, d, rightward, 0, z < Z - 1, z + 1, 0))
            pl.when(hi < Z)(lambda: passing(hi, k, d, leftward, 1, z > 0, z - 1, Z - 1))

            if k == hr - 1:
                pl.when(d == edges_at)(lambda: cache_edges(lambda copy: copy.start()))

            for i in range(slots):
                if i % hr == k:
                    pl.when(d == i // hr + 1)(functools.partial(early, i + 1))

            @pl.when(jnp.logical_and(d > 1, d - 1 <= shorter))
            def _():
                j = z - sign * (d - 1)
                sideward(j, k, 0).wait_recv()
                attend(normed(tokens(j, k)))

            def visit():
                j = z + sign * d
                sideward(j, k, 0).wait_recv()
                attend(normed(tokens(j, k)))

            if k < hr - 1:
                visit()
            else:
                pl.when(d < longer)(visit)

        return carry

    lax.fori_loop(1, longer + 1, step, 0)

    last = z + sign * longer
    pl.when(inner)(sideward(last, hr - 1, 0).wait_recv)

    @pl.when(is_end)
    def _():
        for kind in (0, 1):
            closing(last, kind, o if kind else c, z).wait_recv()
        sideward(last, hr - 1, 0, head).wait_recv()

    keys = normed(tokens(last, hr - 1))

    gains[1].wait()
    gain_two = g2_ref[...].astype(F32).reshape(1, C)

    def finish_rows(row, count):
        at = pl.ds(pl.multiple_of(row * W, W), count * W)
        attend(keys, at)
        mixed = (acc[at, :] * (1.0 / total[at, :])).astype(BF16)
        joined = xn[at, :].astype(F32) + jnp.dot(mixed, wvo[...], preferred_element_type=F32)
        joined = joined.astype(BF16).astype(F32)
        scaled = normalized(joined, gain_two)
        act = (scaled / (1.0 + jnp.exp(-scaled))).astype(BF16)
        cb[2, pl.ds(1 + c * hr + row, count)] = act.reshape(count, W, C)
        return joined

    def keep_joined(row, count, joined):
        low, high = joined[:, :S].astype(BF16), joined[:, S:].astype(BF16)
        jo[pl.ds(c * hr + row, count)] = jnp.where(c == 0, low, high).reshape(count, W, S)
        jt[pl.ds(row, count)] = jnp.where(c == 0, high, low).reshape(count, W, S)

    edge = jnp.where(c == 0, 1, R)
    rest = jnp.where(c == 0, 2, 1 + hr)
    other = jnp.where(c == 0, 1 + hr, 2)
    spans = ((0, W), (0, head), (head, tail), (head, tail))
    def along_tm(hop, part):
        cells = pl.ds(*spans[part])
        src, dst = (cb.at[f, rest if part else edge, cells] for f in (2, 2 - hop))
        to = dev(frame=tm + hop, core=o if part == 3 else None)
        return send(src, dst, s_tm.at[hop - 1, part], r_tm.at[hop - 1, part], to)

    def from_tm(f, part):
        row = cb.at[f, (edge, rest, rest, other)[part], pl.ds(*spans[part])]
        send(row, row, s_tm.at[1 - f, part], r_tm.at[1 - f, part], dev(core=o)).wait_recv()

    def edge_copy(f):
        src = cb.at[f, edge]
        return send(src, src, s_edge.at[2 - f], r_edge.at[2 - f], dev(core=o))

    def near_copy(hop):
        return send(
            cb.at[2, edge], hb.at[2 - hop, o], s_near.at[hop], r_halo.at[2 - hop, o],
            dev(dz=near, frame=tm + hop),
        )

    def near_copies(act):
        pl.when(has_near)(lambda: act(near_copy(0)))
        for hop in range(1, min(3, N)):
            pl.when(jnp.logical_and(jnp.logical_and(has_near, is_end), tm + hop < N))(
                functools.partial(lambda h: act(near_copy(h)), hop)
            )

    def near_pass(f):
        return send(cb.at[f, edge], hb.at[f, o], s_near.at[2 - f], r_halo.at[f, o], dev(dz=near))

    def rest_copy(f):
        src = cb.at[f, rest, pl.ds(0, W if f == 2 else head)]
        return send(src, src, s_rest.at[2 - f], r_rest.at[2 - f], dev(core=o))

    def edge_row(f):
        row = cb.at[f, jnp.where(c == 0, R, 1)]
        send(row, row, s_edge.at[2 - f], r_edge.at[2 - f], dev(core=o)).wait_recv()

    def rest_row(f):
        row = cb.at[f, other, pl.ds(0, W if f == 2 else head)]
        send(row, row, s_rest.at[2 - f], r_rest.at[2 - f], dev(core=o)).wait_recv()

    def from_sibling(f):
        edge_row(f)
        rest_row(f)

    def relay(f):
        row = hb.at[f, o]
        return send(row, row, s_half.at[f], r_halo.at[f, o], dev(core=o))

    def relay_halo(f):
        @pl.when(has_back)
        def _():
            relay(f).wait_recv()
            relay(f).start()

    def both_sides(visit):
        pl.when(z > 0)(lambda: visit(0))
        pl.when(z < Z - 1)(lambda: visit(1))

    for part in (0, 1):
        row = (rest if part else edge) - 1 - c * hr
        joined = finish_rows(row, 1)
        for hop in (1, 2):
            if N > hop:
                for p in (1, 2, 3) if part else (0,):
                    pl.when(tm + hop < N)(along_tm(hop, p).start)
        if part == 0:
            edge_copy(2).start()
            near_copies(lambda copy: copy.start())
        else:
            rest_copy(2).start()
        keep_joined(row, 1, joined)

    pl.when(edges_at > longer)(lambda: cache_edges(lambda copy: copy.start()))

    joined_copy = send(jt, jo.at[pl.ds(c * hr, hr)], s_pair, r_pair, dev(core=o))
    joined_copy.start()

    def taps(f, start):
        for dw in range(3):
            piece(f, dw, start)

    def forwarded(f, part):
        from_tm(f, part)
        if part == 0:
            edge_copy(f).start()
            pl.when(jnp.logical_and(has_near, inner))(near_pass(f).start)
        else:
            rest_copy(f).start()

    def product(f, dh, dw, at):
        return lax.dot_general(cb[f, at], cw[f, dh, dw], (((1,), (1,)), ((), ())), preferred_element_type=F32)

    def outer_taps(f):
        for dw in range(3):
            rows = jnp.concatenate([cb[f, 1], cb[f, R]], axis=0)
            both = lax.dot_general(rows, cw[f, 1, dw], (((1,), (1,)), ((), ())), preferred_element_type=F32)
            parts[dw, pl.ds(8, W)] += both[:W]
            parts[dw, pl.ds(8 + (R - 1) * W, W)] += both[W:]
            parts[dw, pl.ds(8 + W, W)] += product(f, 0, dw, 1)
            parts[dw, pl.ds(8 + (R - 2) * W, W)] += product(f, 2, dw, R)

    def row_taps(f, pieces):
        rows = jnp.concatenate([cb[f, row, at : at + count] for row, at, count in pieces], axis=0)
        for dw in range(3):
            for dh in range(3):
                value = lax.dot_general(rows, cw[f, dh, dw], (((1,), (1,)), ((), ())), preferred_element_type=F32)
                start = 0
                for row, at, count in pieces:
                    place = pl.ds(pl.multiple_of(8 + (row - dh) * W + at, 8), count)
                    parts[dw, place] += value[start : start + count]
                    start += count

    def other_halo(f):
        row = hb.at[f, c]
        pl.when(has_near)(send(row, row, s_half.at[f], r_halo.at[f, c], dev(core=o)).wait_recv)

    def halo_taps(frames):
        for f in frames:
            other_halo(f)

        def visit(side):
            rows = jnp.concatenate([hb[f, side] for f in frames], axis=-1)
            for dw in range(3):
                kernel_rows = jnp.concatenate([cw[f, 2 * side, dw] for f in frames], axis=-1)
                parts[dw, pl.ds(8 + side * (T - W), W)] += lax.dot_general(
                    rows, kernel_rows, (((1,), (1,)), ((), ())), preferred_element_type=F32
                )

        both_sides(visit)

    def halos(frames):
        for f in frames:
            relay_halo(f)
        halo_taps(frames)

    late = (0, 2) if N == 2 else (2,)

    def relays():
        for f in late:
            relay_halo(f)

    pl.when(jnp.logical_and(tm >= 1, is_end))(relays)
    from_sibling(2)
    if N > 2:
        pl.when(tm <= 1)(lambda: taps(2, False))
        pl.when(tm >= 2)(lambda: taps(2, True))
    else:
        taps(2, False)

    there = jo.at[pl.ds(o * hr, hr)]
    send(jt, there, s_pair, r_pair, dev(core=o)).wait_recv()
    parts[1, pl.ds(8, T)] += jo[...].reshape(T, S).astype(F32)

    pl.when(jnp.logical_and(tm == 0, inner))(lambda: taps(1, False))
    pl.when(tm == 0)(lambda: halos((0, 2, 1)))
    if N > 1:

        @pl.when(tm >= 1)
        def _():
            pl.when(jnp.logical_and(is_end, has_near))(lambda: halo_taps(late))
            forwarded(1, 0)
            pl.when(jnp.logical_and(is_end, has_back))(lambda: halo_taps(late))
            pl.when(is_end)(lambda: relay_halo(1))
            edge_row(1)
            outer_taps(1)
            pl.when(jnp.logical_and(is_end, has_near))(lambda: halo_taps((1,)))
            forwarded(1, 1)
            row_taps(1, ((rest, 0, head),))
            pl.when(jnp.logical_and(is_end, has_back))(lambda: halo_taps((1,)))
            from_tm(1, 2)
            from_tm(1, 3)
            rest_row(1)
            row_taps(1, ((rest, head, tail), (other, 0, W)))

            @pl.when(inner)
            def _():
                relays()
                relay_halo(1)
                halo_taps(late + (1,))
    if N > 2:

        @pl.when(tm >= 2)
        def _():
            forwarded(0, 0)
            forwarded(0, 1)
            from_tm(0, 2)
            from_tm(0, 3)
            from_sibling(0)
            taps(0, False)

        pl.when(tm >= 1)(lambda: halos((0,)))

    cell = lax.rem(lax.broadcasted_iota(jnp.int32, (T, S), 0), W)
    before = jnp.where(cell == 0, 0.0, parts[0, pl.ds(7, T)])
    after = jnp.where(cell == W - 1, 0.0, parts[2, pl.ds(9, T)])
    out_ref[0] = (before + parts[1, pl.ds(8, T)] + after).astype(BF16).reshape(R, W, S)

    joined_copy.wait_send()
    def drain(there, short, copy):
        pl.when(jnp.logical_and(there, short))(copy(head).wait_send)
        pl.when(jnp.logical_and(there, jnp.logical_not(short)))(copy(W).wait_send)

    for k in range(hr):
        at = z if k == hr - 1 else -1
        drain(z < Z - 1, at == Z - 2, lambda n: rightward(z, k, n))
        drain(z > 0, at == 1, lambda n: leftward(z, k, n))
        drain(True, at == Z - 1, lambda n: sideward(z, k, 0, n))
        drain(z < Z - 1, at == 0, lambda n: sideward(z, k, 1, n))

    @pl.when(jnp.logical_or(z == 1, z == Z - 2))
    def _():
        for kind in (0, 1):
            closing(z, kind, c, jnp.where(z == 1, 0, Z - 1)).wait_send()

    cache_edges(lambda copy: copy.wait_send())
    for f in range(3):
        pl.when(has_back)(relay(f).wait_send)
    near_copies(lambda copy: copy.wait_send())
    for part in range(4):
        for hop in (1, 2):
            if N > hop:
                pl.when(tm + hop < N)(along_tm(hop, part).wait_send)

    def spread_done(f):
        edge_copy(f).wait_send()
        rest_copy(f).wait_send()
        if f < 2:
            pl.when(jnp.logical_and(has_near, inner))(near_pass(f).wait_send)

    spread_done(2)
    if N > 1:
        pl.when(tm >= 1)(lambda: spread_done(1))
    if N > 2:
        pl.when(tm >= 2)(lambda: spread_done(0))


def solution(mesh):
    Z, N = mesh.shape["space"], mesh.shape["tm"]

    def body(frames_in, cache, gain_one, gain_two, w_query, w_key, w_value, w_out, conv_weight):
        _, R, W, S = frames_in.shape
        C = 2 * S
        hr, half, T = R // 2, R // 2 * W, R * W
        hops, sets = max(1, min(2, N - 1)), min(3, N)
        dma = pltpu.SemaphoreType.DMA
        hbm = pl.BlockSpec(memory_space=pltpu.HBM)
        vmem = pl.BlockSpec(memory_space=pltpu.VMEM)
        return pl.pallas_call(
            functools.partial(kernel, Z, N),
            out_shape=jax.ShapeDtypeStruct(frames_in.shape, BF16),
            in_specs=[hbm] * 9,
            out_specs=vmem,
            scratch_shapes=[
                pltpu.VMEM((R, W, S), BF16),
                pltpu.VMEM((Z, hr, 2, W, C), BF16),
                pltpu.VMEM((half, C), BF16),
                pltpu.VMEM((half, C), BF16),
                pltpu.VMEM((half, 1), F32),
                pltpu.VMEM((half, 1), F32),
                pltpu.VMEM((half, C), F32),
                pltpu.VMEM((3, R + 2, W, C), BF16),
                pltpu.VMEM((3, 2, W, C), BF16),
                pltpu.VMEM((hr, W, S), BF16),
                pltpu.VMEM((R, W, S), BF16),
                pltpu.VMEM((3, T + 16, S), F32),
                pltpu.VMEM((C,), BF16),
                pltpu.VMEM((C,), BF16),
                pltpu.VMEM((4, C, C), BF16),
                pltpu.VMEM((C, C), BF16),
                pltpu.VMEM((3, 3, 3, S, C), BF16),
                dma((7,)),
                dma,
                dma,
                dma((hr,)),
                dma((hr,)),
                dma((2, hr)),
                dma((Z, hr)),
                dma((Z, hr)),
                dma((2,)),
                dma((2,)),
                dma((2,)),
                dma((3, 2)),
                dma((sets,)),
                dma((sets,)),
                dma((sets,)),
                dma((sets,)),
                dma((sets,)),
                dma((hops, 4)),
                dma((hops, 4)),
                dma((3,)),
            ],
            compiler_params=pltpu.CompilerParams(
                collective_id=0, has_side_effects=True, vmem_limit_bytes=50 << 20
            ),
        )(*(pltpu.with_memory_space_constraint(a, pltpu.HBM) for a in (
            frames_in, cache, gain_one, gain_two,
            w_query, w_key, w_value, w_out, jnp.swapaxes(conv_weight, 3, 4),
        )))

    return jax.shard_map(
        body,
        mesh=mesh,
        in_specs=(
            P(("clips", "tm"), "space", None, "chan"),
            P("clips", "space", None, None),
            P(),
            P(),
            P(),
            P(),
            P(),
            P(),
            P(None, None, None, None, "chan"),
        ),
        out_specs=P(("clips", "tm"), "space", None, "chan"),
        check_vma=False,
    )
```

```python
import functools
import math

import jax
import jax.numpy as jnp
from jax import lax
from jax.experimental import pallas as pl
from jax.experimental.pallas import tpu as pltpu
from jax.sharding import PartitionSpec as P

F32 = jnp.float32
BF16 = jnp.bfloat16
MESH = pl.DeviceIdType.MESH


def normalized(wide, gain):
    factor = lax.rsqrt(jnp.mean(wide * wide, axis=-1, keepdims=True) + 1e-06)
    return wide * factor * gain


def kernel(
    Z, N,
    x_hbm, cache_hbm, g1_hbm, g2_hbm, wq_hbm, wk_hbm, wv_hbm, wo_hbm, cw_hbm,
    out_ref,
    xo, xg, xn, qk, top, total, acc, cb, hb, jt, jo, parts, g1_ref, g2_ref, ws, wvo, cw,
    s_loc, s_pair, r_pair, s_right, s_left, s_sib, r_z, r_sib, s_last, r_last,
    s_cache, r_halo, s_near, s_edge, s_rest, r_edge, r_rest, s_tm, r_tm, s_half,
):
    z = lax.axis_index("space")
    c = lax.axis_index("chan")
    tm = lax.axis_index("tm")
    o = 1 - c
    R, W, S = out_ref.shape[1:]
    C = 2 * S
    hr = R // 2
    T = R * W
    tail = 3 * W // 10
    head = W - tail
    L = 128
    E = S - L
    blocks = ((0, 0, L), (S, L, L), (L, 2 * L, E), (S + L, 2 * L + E, E))

    def dev(dz=None, core=None, frame=None):
        return {
            "space": z if dz is None else dz,
            "chan": c if core is None else core,
            "tm": tm if frame is None else frame,
        }

    def send(src, dst, ssem, rsem, to):
        return pltpu.make_async_remote_copy(
            src_ref=src, dst_ref=dst, send_sem=ssem, recv_sem=rsem,
            device_id=to, device_id_type=MESH,
        )

    near, back = z + 2 * c - 1, z + 1 - 2 * c
    has_near = jnp.logical_and(near >= 0, near < Z)
    has_back = jnp.logical_and(back >= 0, back < Z)
    is_end = jnp.logical_or(z == 0, z == Z - 1)
    inner = jnp.logical_not(is_end)

    barrier = pltpu.get_barrier_semaphore()

    def greet(to):
        pl.semaphore_signal(barrier, inc=1, device_id=to, device_id_type=MESH)

    greet(dev(core=o))
    pl.when(z > 0)(lambda: greet(dev(dz=z - 1)))
    pl.when(z < Z - 1)(lambda: greet(dev(dz=z + 1)))
    for hop in (1, 2):
        if N > hop:
            pl.when(tm >= hop)(functools.partial(lambda h: greet(dev(frame=tm - h)), hop))

    x_own = pltpu.make_async_copy(x_hbm.at[0], xo, s_loc.at[0])
    x_own.start()
    gains = [
        pltpu.make_async_copy(a, b, s_loc.at[1 + i])
        for i, (a, b) in enumerate(((g1_hbm, g1_ref), (g2_hbm, g2_ref)))
    ]
    for g in gains:
        g.start()
    for i, w_hbm in enumerate((wq_hbm, wk_hbm, wv_hbm)):
        for src, dst, count in blocks:
            pltpu.make_async_copy(w_hbm.at[pl.ds(src, count)], ws.at[i, pl.ds(dst, count)], s_loc.at[3]).start()
    pltpu.make_async_copy(wo_hbm, ws.at[3], s_loc.at[3]).start()
    taps_own = pltpu.make_async_copy(cw_hbm, cw, s_loc.at[4])
    taps_own.start()
    first = jnp.minimum(tm, 1)
    cache_two = pltpu.make_async_copy(cache_hbm.at[first], cb.at[0, pl.ds(1, R)], s_loc.at[5])
    cache_one = pltpu.make_async_copy(cache_hbm.at[1], cb.at[1, pl.ds(1, R)], s_loc.at[6])
    pl.when(tm <= 1)(cache_two.start)
    pl.when(tm == 0)(cache_one.start)

    blank = jnp.zeros((W, C), BF16)
    for f in range(3):
        cb[f, 0] = blank
        cb[f, R + 1] = blank

    x_own.wait()
    for k in range(hr):
        a, b = xo[2 * k], xo[2 * k + 1]
        xg[z, k, c] = jnp.concatenate([a[:, :L], b[:, :L], a[:, L:], b[:, L:]], axis=-1)

    want = 1 + jnp.where(z > 0, 1, 0) + jnp.where(z < Z - 1, 1, 0)
    for hop in (1, 2):
        if N > hop:
            want = want + jnp.where(tm + hop < N, 1, 0)
    pl.semaphore_wait(barrier, want)

    def rightward(j, k, n=W):
        ref = xg.at[j, k, c, pl.ds(0, n)]
        return send(ref, ref, s_right.at[k], r_z.at[j, k], dev(dz=z + 1))

    def leftward(j, k, n=W):
        ref = xg.at[j, k, c, pl.ds(0, n)]
        return send(ref, ref, s_left.at[k], r_z.at[j, k], dev(dz=z - 1))

    def sideward(j, k, flow, n=W):
        ref = xg.at[j, k, c, pl.ds(0, n)]
        return send(ref, ref, s_sib.at[flow, k], r_sib.at[j, k], dev(core=o))

    def closing(j, kind, core, to):
        ref = xg.at[j, hr - 1, core, pl.ds(head, tail)]
        return send(ref, ref, s_last.at[kind], r_last.at[kind], dev(dz=to, core=o if kind else c))

    def outward(k):
        pl.when(z < Z - 1)(rightward(z, k).start)
        pl.when(z > 0)(leftward(z, k).start)

    outward(0)
    for k in range(hr):
        sideward(z, k, 0).start()

    gains[0].wait()
    gain_one = g1_ref[...].astype(F32).reshape(1, C)
    gain_one = jnp.concatenate([gain_one[:, at : at + count] for at, _, count in blocks], axis=-1)
    low_lanes = lax.broadcasted_iota(jnp.int32, (W, L), 1) < E

    def tokens(j, k):
        p, q = xg[j, k, 0].astype(F32), xg[j, k, 1].astype(F32)
        pt, qt = p[:, 2 * L :], q[:, 2 * L :]
        even = jnp.where(low_lanes, pt, pltpu.roll(qt, E, 1))
        odd = jnp.where(low_lanes, pltpu.roll(pt, E, 1), qt)
        return jnp.concatenate([
            jnp.concatenate([p[:, :L], q[:, :L], even], axis=-1),
            jnp.concatenate([p[:, L : 2 * L], q[:, L : 2 * L], odd], axis=-1),
        ], axis=0)

    def normed(wide):
        return normalized(wide, gain_one).astype(BF16)

    top[...] = jnp.full(top.shape, -1e30, F32)
    total[...] = jnp.zeros(total.shape, F32)
    acc[...] = jnp.zeros(acc.shape, F32)

    everything = pl.ds(0, hr * W)

    def attend(keys, at=everything):
        scores = lax.dot_general(qk[at, :], keys, (((1,), (1,)), ((), ())), preferred_element_type=F32)
        old = top[at, :]
        new = jnp.maximum(old, jnp.max(scores, axis=-1, keepdims=True))
        weight = jnp.exp2(scores - new)
        fade = jnp.exp2(old - new)
        top[at, :] = new
        total[at, :] = total[at, :] * fade + jnp.sum(weight, axis=-1, keepdims=True)
        acc[at, :] = acc[at, :] * fade + jnp.dot(weight.astype(BF16), keys, preferred_element_type=F32)

    for k in range(hr):
        sideward(z, k, 0).wait_recv()
    for k in range(1, hr):
        outward(k)
    pltpu.make_async_copy(ws, ws, s_loc.at[3]).wait()
    mine = tokens(z, c)
    xn[...] = jnp.concatenate(
        [mine[:, :L], mine[:, 2 * L : 2 * L + E], mine[:, L : 2 * L], mine[:, 2 * L + E :]], axis=-1
    ).astype(BF16)
    keys = normed(mine)
    query = jnp.dot(keys, ws[0], preferred_element_type=F32).astype(BF16)
    folded = lax.dot_general(query, ws[1], (((1,), (1,)), ((), ())), preferred_element_type=F32)
    qk[...] = (folded * (C ** (-0.5) * math.log2(math.e))).astype(BF16)
    attend(keys)
    attend(normed(tokens(z, o)))
    wvo[...] = jnp.dot(ws[2], ws[3], preferred_element_type=F32).astype(BF16)

    def piece(f, dw, start):
        rows = jnp.concatenate([cb[f, dh : dh + R].reshape(T, C) for dh in range(3)], axis=-1)
        kernel_rows = jnp.concatenate([cw[f, dh, dw] for dh in range(3)], axis=-1)
        value = lax.dot_general(rows, kernel_rows, (((1,), (1,)), ((), ())), preferred_element_type=F32)
        if start:
            parts[dw, pl.ds(8, T)] = value
        else:
            parts[dw, pl.ds(8, T)] += value

    def early(i):
        f, dw = divmod(i, 3)
        there = tm <= 1 if f == 0 else jnp.logical_and(tm == 0, is_end)
        pl.when(there)(lambda: piece(f, dw, f == 0))

    taps_own.wait()
    pl.when(tm <= 1)(cache_two.wait)
    pl.when(tm == 0)(cache_one.wait)
    early(0)

    def cache_edge(f):
        row = jnp.where(c == 0, 0, R - 1)
        source = cache_hbm.at[first if f == 0 else 1, row]
        return send(source, hb.at[f, o], s_cache.at[f], r_halo.at[f, o], dev(dz=near))

    def cache_edges(act):
        pl.when(jnp.logical_and(has_near, tm <= 1))(lambda: act(cache_edge(0)))
        pl.when(jnp.logical_and(has_near, tm == 0))(lambda: act(cache_edge(1)))

    ahead = Z - 1 - z
    longer = jnp.maximum(z, ahead)
    sign = jnp.where(ahead >= z, 1, -1)
    shorter = Z - 1 - longer
    edges_at = jnp.where(c == 0, ahead, z) + 1
    slots = 5

    def passing(j, k, d, ward, flow, onward, to, source):
        def give(n):
            ward(j, k).wait_send()
            ward(j, k, n).start()

        def share(n):
            if flow == 0:
                sideward(j, k, 0).wait_send()
            else:
                pl.when(d > 1)(sideward(j, k, 1).wait_send)
            sideward(j, k, flow, n).start()

        if k < hr - 1:
            ward(j, k).wait_recv()
            pl.when(onward)(lambda: give(W))
            share(W)
            return

        closes = jnp.logical_and(j == source, jnp.logical_not(onward))
        before = jnp.logical_and(j == source, jnp.logical_or(to == 0, to == Z - 1))

        @pl.when(closes)
        def _():
            ward(j, k, head).wait_recv()
            share(head)

        @pl.when(jnp.logical_not(closes))
        def _():
            ward(j, k).wait_recv()

            @pl.when(jnp.logical_and(onward, before))
            def _():
                give(head)

            pl.when(jnp.logical_and(onward, jnp.logical_not(before)))(lambda: give(W))
            share(W)

    def step(d, carry):
        lo, hi = z - d, z + d

        for k in range(hr):
            pl.when(lo >= 0)(lambda: passing(lo, k, d, rightward, 0, z < Z - 1, z + 1, 0))
            pl.when(hi < Z)(lambda: passing(hi, k, d, leftward, 1, z > 0, z - 1, Z - 1))

            if k == hr - 1:
                pl.when(d == edges_at)(lambda: cache_edges(lambda copy: copy.start()))

            for i in range(slots):
                if i % hr == k:
                    pl.when(d == i // hr + 1)(functools.partial(early, i + 1))

            @pl.when(jnp.logical_and(d > 1, d - 1 <= shorter))
            def _():
                j = z - sign * (d - 1)
                sideward(j, k, 0).wait_recv()
                attend(normed(tokens(j, k)))

            def visit():
                j = z + sign * d
                sideward(j, k, 0).wait_recv()
                attend(normed(tokens(j, k)))

            if k < hr - 1:
                visit()
            else:
                pl.when(d < longer)(visit)

        return carry

    lax.fori_loop(1, longer + 1, step, 0)

    last = z + sign * longer

    def closings(act):
        @pl.when(jnp.logical_or(z == 1, z == Z - 2))
        def _():
            for kind in (0, 1):
                act(closing(z + sign * longer, kind, c, z - sign))

    closings(lambda copy: copy.start())
    pl.when(inner)(sideward(last, hr - 1, 0).wait_recv)

    @pl.when(is_end)
    def _():
        for kind in (0, 1):
            closing(last, kind, o if kind else c, z).wait_recv()
        sideward(last, hr - 1, 0, head).wait_recv()

    keys = normed(tokens(last, hr - 1))

    gains[1].wait()
    gain_two = g2_ref[...].astype(F32).reshape(1, C)

    def finish_rows(row, count):
        at = pl.ds(pl.multiple_of(row * W, W), count * W)
        attend(keys, at)
        mixed = (acc[at, :] * (1.0 / total[at, :])).astype(BF16)
        joined = xn[at, :].astype(F32) + jnp.dot(mixed, wvo[...], preferred_element_type=F32)
        joined = joined.astype(BF16).astype(F32)
        scaled = normalized(joined, gain_two)
        act = (scaled / (1.0 + jnp.exp(-scaled))).astype(BF16)
        cb[2, pl.ds(1 + c * hr + row, count)] = act.reshape(count, W, C)
        return joined

    def keep_joined(row, count, joined):
        low, high = joined[:, :S].astype(BF16), joined[:, S:].astype(BF16)
        jo[pl.ds(c * hr + row, count)] = jnp.where(c == 0, low, high).reshape(count, W, S)
        jt[pl.ds(row, count)] = jnp.where(c == 0, high, low).reshape(count, W, S)

    edge = jnp.where(c == 0, 1, R)
    rest = jnp.where(c == 0, 2, 1 + hr)
    other = jnp.where(c == 0, 1 + hr, 2)
    spans = ((0, W), (0, head), (head, tail), (head, tail))
    def along_tm(hop, part):
        cells = pl.ds(*spans[part])
        src, dst = (cb.at[f, rest if part else edge, cells] for f in (2, 2 - hop))
        to = dev(frame=tm + hop, core=o if part == 3 else None)
        return send(src, dst, s_tm.at[hop - 1, part], r_tm.at[hop - 1, part], to)

    def from_tm(f, part):
        row = cb.at[f, (edge, rest, rest, other)[part], pl.ds(*spans[part])]
        send(row, row, s_tm.at[1 - f, part], r_tm.at[1 - f, part], dev(core=o)).wait_recv()

    def edge_copy(f):
        src = cb.at[f, edge]
        return send(src, src, s_edge.at[2 - f], r_edge.at[2 - f], dev(core=o))

    def near_copy(hop):
        return send(
            cb.at[2, edge], hb.at[2 - hop, o], s_near.at[hop], r_halo.at[2 - hop, o],
            dev(dz=near, frame=tm + hop),
        )

    def near_copies(act):
        pl.when(has_near)(lambda: act(near_copy(0)))
        for hop in range(1, min(3, N)):
            pl.when(jnp.logical_and(jnp.logical_and(has_near, is_end), tm + hop < N))(
                functools.partial(lambda h: act(near_copy(h)), hop)
            )

    def near_pass(f):
        return send(cb.at[f, edge], hb.at[f, o], s_near.at[2 - f], r_halo.at[f, o], dev(dz=near))

    def rest_copy(f):
        src = cb.at[f, rest, pl.ds(0, W if f == 2 else head)]
        return send(src, src, s_rest.at[2 - f], r_rest.at[2 - f], dev(core=o))

    def edge_row(f):
        row = cb.at[f, jnp.where(c == 0, R, 1)]
        send(row, row, s_edge.at[2 - f], r_edge.at[2 - f], dev(core=o)).wait_recv()

    def rest_row(f):
        row = cb.at[f, other, pl.ds(0, W if f == 2 else head)]
        send(row, row, s_rest.at[2 - f], r_rest.at[2 - f], dev(core=o)).wait_recv()

    def from_sibling(f):
        edge_row(f)
        rest_row(f)

    def relay(f):
        row = hb.at[f, o]
        return send(row, row, s_half.at[f], r_halo.at[f, o], dev(core=o))

    def relay_halo(f):
        @pl.when(has_back)
        def _():
            relay(f).wait_recv()
            relay(f).start()

    def both_sides(visit):
        pl.when(z > 0)(lambda: visit(0))
        pl.when(z < Z - 1)(lambda: visit(1))

    for part in (0, 1):
        row = (rest if part else edge) - 1 - c * hr
        joined = finish_rows(row, 1)
        for hop in (1, 2):
            if N > hop:
                for p in (1, 2, 3) if part else (0,):
                    pl.when(tm + hop < N)(along_tm(hop, p).start)
        if part == 0:
            edge_copy(2).start()
            near_copies(lambda copy: copy.start())
        else:
            rest_copy(2).start()
        keep_joined(row, 1, joined)

    pl.when(edges_at > longer)(lambda: cache_edges(lambda copy: copy.start()))

    joined_copy = send(jt, jo.at[pl.ds(c * hr, hr)], s_pair, r_pair, dev(core=o))
    joined_copy.start()

    def taps(f, start):
        for dw in range(3):
            piece(f, dw, start)

    def forwarded(f, part):
        from_tm(f, part)
        if part == 0:
            edge_copy(f).start()
            pl.when(jnp.logical_and(has_near, inner))(near_pass(f).start)
        else:
            rest_copy(f).start()

    def product(f, dh, dw, at):
        return lax.dot_general(cb[f, at], cw[f, dh, dw], (((1,), (1,)), ((), ())), preferred_element_type=F32)

    def outer_taps(f):
        for dw in range(3):
            rows = jnp.concatenate([cb[f, 1], cb[f, R]], axis=0)
            both = lax.dot_general(rows, cw[f, 1, dw], (((1,), (1,)), ((), ())), preferred_element_type=F32)
            parts[dw, pl.ds(8, W)] += both[:W]
            parts[dw, pl.ds(8 + (R - 1) * W, W)] += both[W:]
            parts[dw, pl.ds(8 + W, W)] += product(f, 0, dw, 1)
            parts[dw, pl.ds(8 + (R - 2) * W, W)] += product(f, 2, dw, R)

    def row_taps(f, pieces):
        rows = jnp.concatenate([cb[f, row, at : at + count] for row, at, count in pieces], axis=0)
        for dw in range(3):
            for dh in range(3):
                value = lax.dot_general(rows, cw[f, dh, dw], (((1,), (1,)), ((), ())), preferred_element_type=F32)
                start = 0
                for row, at, count in pieces:
                    place = pl.ds(pl.multiple_of(8 + (row - dh) * W + at, 8), count)
                    parts[dw, place] += value[start : start + count]
                    start += count

    def other_halo(f):
        row = hb.at[f, c]
        pl.when(has_near)(send(row, row, s_half.at[f], r_halo.at[f, c], dev(core=o)).wait_recv)

    def halo_taps(frames):
        for f in frames:
            other_halo(f)

        def visit(side):
            rows = jnp.concatenate([hb[f, side] for f in frames], axis=-1)
            for dw in range(3):
                kernel_rows = jnp.concatenate([cw[f, 2 * side, dw] for f in frames], axis=-1)
                parts[dw, pl.ds(8 + side * (T - W), W)] += lax.dot_general(
                    rows, kernel_rows, (((1,), (1,)), ((), ())), preferred_element_type=F32
                )

        both_sides(visit)

    def halos(frames):
        for f in frames:
            relay_halo(f)
        halo_taps(frames)

    late = (0, 2) if N == 2 else (2,)

    def relays():
        for f in late:
            relay_halo(f)

    pl.when(jnp.logical_and(tm >= 1, is_end))(relays)
    from_sibling(2)
    if N > 2:
        pl.when(tm <= 1)(lambda: taps(2, False))
        pl.when(tm >= 2)(lambda: taps(2, True))
    else:
        taps(2, False)

    there = jo.at[pl.ds(o * hr, hr)]
    send(jt, there, s_pair, r_pair, dev(core=o)).wait_recv()
    parts[1, pl.ds(8, T)] += jo[...].reshape(T, S).astype(F32)

    pl.when(jnp.logical_and(tm == 0, inner))(lambda: taps(1, False))
    pl.when(tm == 0)(lambda: halos((0, 2, 1)))
    if N > 1:

        @pl.when(tm >= 1)
        def _():
            pl.when(jnp.logical_and(is_end, has_near))(lambda: halo_taps(late))
            forwarded(1, 0)
            pl.when(jnp.logical_and(is_end, has_back))(lambda: halo_taps(late))
            pl.when(is_end)(lambda: relay_halo(1))
            edge_row(1)
            outer_taps(1)
            pl.when(jnp.logical_and(is_end, has_near))(lambda: halo_taps((1,)))
            forwarded(1, 1)
            row_taps(1, ((rest, 0, head),))
            pl.when(jnp.logical_and(is_end, has_back))(lambda: halo_taps((1,)))
            from_tm(1, 2)
            from_tm(1, 3)
            rest_row(1)
            row_taps(1, ((rest, head, tail), (other, 0, W)))

            @pl.when(inner)
            def _():
                relays()
                relay_halo(1)
                halo_taps(late + (1,))
    if N > 2:

        @pl.when(tm >= 2)
        def _():
            forwarded(0, 0)
            forwarded(0, 1)
            from_tm(0, 2)
            from_tm(0, 3)
            from_sibling(0)
            taps(0, False)

        pl.when(tm >= 1)(lambda: halos((0,)))

    cell = lax.rem(lax.broadcasted_iota(jnp.int32, (T, S), 0), W)
    before = jnp.where(cell == 0, 0.0, parts[0, pl.ds(7, T)])
    after = jnp.where(cell == W - 1, 0.0, parts[2, pl.ds(9, T)])
    out_ref[0] = (before + parts[1, pl.ds(8, T)] + after).astype(BF16).reshape(R, W, S)

    joined_copy.wait_send()
    def drain(there, short, copy):
        pl.when(jnp.logical_and(there, short))(copy(head).wait_send)
        pl.when(jnp.logical_and(there, jnp.logical_not(short)))(copy(W).wait_send)

    for k in range(hr):
        at = z if k == hr - 1 else -1
        drain(z < Z - 1, at == Z - 2, lambda n: rightward(z, k, n))
        drain(z > 0, at == 1, lambda n: leftward(z, k, n))
        drain(True, at == Z - 1, lambda n: sideward(z, k, 0, n))
        drain(z < Z - 1, at == 0, lambda n: sideward(z, k, 1, n))

    closings(lambda copy: copy.wait_send())
    cache_edges(lambda copy: copy.wait_send())
    for f in range(3):
        pl.when(has_back)(relay(f).wait_send)
    near_copies(lambda copy: copy.wait_send())
    for part in range(4):
        for hop in (1, 2):
            if N > hop:
                pl.when(tm + hop < N)(along_tm(hop, part).wait_send)

    def spread_done(f):
        edge_copy(f).wait_send()
        rest_copy(f).wait_send()
        if f < 2:
            pl.when(jnp.logical_and(has_near, inner))(near_pass(f).wait_send)

    spread_done(2)
    if N > 1:
        pl.when(tm >= 1)(lambda: spread_done(1))
    if N > 2:
        pl.when(tm >= 2)(lambda: spread_done(0))


def solution(mesh):
    Z, N = mesh.shape["space"], mesh.shape["tm"]

    def body(frames_in, cache, gain_one, gain_two, w_query, w_key, w_value, w_out, conv_weight):
        _, R, W, S = frames_in.shape
        C = 2 * S
        hr, half, T = R // 2, R // 2 * W, R * W
        hops, sets = max(1, min(2, N - 1)), min(3, N)
        dma = pltpu.SemaphoreType.DMA
        hbm = pl.BlockSpec(memory_space=pltpu.HBM)
        vmem = pl.BlockSpec(memory_space=pltpu.VMEM)
        return pl.pallas_call(
            functools.partial(kernel, Z, N),
            out_shape=jax.ShapeDtypeStruct(frames_in.shape, BF16),
            in_specs=[hbm] * 9,
            out_specs=vmem,
            scratch_shapes=[
                pltpu.VMEM((R, W, S), BF16),
                pltpu.VMEM((Z, hr, 2, W, C), BF16),
                pltpu.VMEM((half, C), BF16),
                pltpu.VMEM((half, C), BF16),
                pltpu.VMEM((half, 1), F32),
                pltpu.VMEM((half, 1), F32),
                pltpu.VMEM((half, C), F32),
                pltpu.VMEM((3, R + 2, W, C), BF16),
                pltpu.VMEM((3, 2, W, C), BF16),
                pltpu.VMEM((hr, W, S), BF16),
                pltpu.VMEM((R, W, S), BF16),
                pltpu.VMEM((3, T + 16, S), F32),
                pltpu.VMEM((C,), BF16),
                pltpu.VMEM((C,), BF16),
                pltpu.VMEM((4, C, C), BF16),
                pltpu.VMEM((C, C), BF16),
                pltpu.VMEM((3, 3, 3, S, C), BF16),
                dma((7,)),
                dma,
                dma,
                dma((hr,)),
                dma((hr,)),
                dma((2, hr)),
                dma((Z, hr)),
                dma((Z, hr)),
                dma((2,)),
                dma((2,)),
                dma((2,)),
                dma((3, 2)),
                dma((sets,)),
                dma((sets,)),
                dma((sets,)),
                dma((sets,)),
                dma((sets,)),
                dma((hops, 4)),
                dma((hops, 4)),
                dma((3,)),
            ],
            compiler_params=pltpu.CompilerParams(
                collective_id=0, has_side_effects=True, vmem_limit_bytes=50 << 20
            ),
        )(*(pltpu.with_memory_space_constraint(a, pltpu.HBM) for a in (
            frames_in, cache, gain_one, gain_two,
            w_query, w_key, w_value, w_out, jnp.swapaxes(conv_weight, 3, 4),
        )))

    return jax.shard_map(
        body,
        mesh=mesh,
        in_specs=(
            P(("clips", "tm"), "space", None, "chan"),
            P("clips", "space", None, None),
            P(),
            P(),
            P(),
            P(),
            P(),
            P(),
            P(None, None, None, None, "chan"),
        ),
        out_specs=P(("clips", "tm"), "space", None, "chan"),
        check_vma=False,
    )
```

```python
import functools
import math

import jax
import jax.numpy as jnp
from jax import lax
from jax.experimental import pallas as pl
from jax.experimental.pallas import tpu as pltpu
from jax.sharding import PartitionSpec as P

F32 = jnp.float32
BF16 = jnp.bfloat16
MESH = pl.DeviceIdType.MESH


def normalized(wide, gain):
    factor = lax.rsqrt(jnp.mean(wide * wide, axis=-1, keepdims=True) + 1e-06)
    return wide * factor * gain


def kernel(
    Z, N,
    x_hbm, cache_hbm, g1_hbm, g2_hbm, wq_hbm, wk_hbm, wv_hbm, wo_hbm, cw_hbm,
    out_ref,
    xo, xg, xn, qk, top, total, acc, cb, hb, jt, jo, parts, g1_ref, g2_ref, ws, wvo, cw,
    s_loc, r_pair, s_right, s_left, s_sib, r_z, r_sib, s_last, r_last,
    s_cache, r_halo, s_near, s_edge, r_edge, r_rest, s_tm, r_tm,
):
    z = lax.axis_index("space")
    c = lax.axis_index("chan")
    tm = lax.axis_index("tm")
    o = 1 - c
    R, W, S = out_ref.shape[1:]
    C = 2 * S
    hr = R // 2
    T = R * W
    tail = 3 * W // 10
    head = W - tail
    L = 128
    E = S - L
    blocks = ((0, 0, L), (S, L, L), (L, 2 * L, E), (S + L, 2 * L + E, E))

    def dev(dz=None, core=None, frame=None):
        return {
            "space": z if dz is None else dz,
            "chan": c if core is None else core,
            "tm": tm if frame is None else frame,
        }

    def send(src, dst, ssem, rsem, to):
        return pltpu.make_async_remote_copy(
            src_ref=src, dst_ref=dst, send_sem=ssem, recv_sem=rsem,
            device_id=to, device_id_type=MESH,
        )

    near, back = z + 2 * c - 1, z + 1 - 2 * c
    has_near = jnp.logical_and(near >= 0, near < Z)
    has_back = jnp.logical_and(back >= 0, back < Z)
    is_end = jnp.logical_or(z == 0, z == Z - 1)
    inner = jnp.logical_not(is_end)

    barrier = pltpu.get_barrier_semaphore()

    def greet(to):
        pl.semaphore_signal(barrier, inc=1, device_id=to, device_id_type=MESH)

    greet(dev(core=o))
    pl.when(z > 0)(lambda: greet(dev(dz=z - 1)))
    pl.when(z < Z - 1)(lambda: greet(dev(dz=z + 1)))
    for hop in (1, 2):
        if N > hop:
            pl.when(tm >= hop)(functools.partial(lambda h: greet(dev(frame=tm - h)), hop))

    x_own = pltpu.make_async_copy(x_hbm.at[0], xo, s_loc.at[0])
    x_own.start()
    gains = [
        pltpu.make_async_copy(a, b, s_loc.at[1 + i])
        for i, (a, b) in enumerate(((g1_hbm, g1_ref), (g2_hbm, g2_ref)))
    ]
    for g in gains:
        g.start()
    for i, w_hbm in enumerate((wq_hbm, wk_hbm, wv_hbm)):
        for src, dst, count in blocks:
            pltpu.make_async_copy(w_hbm.at[pl.ds(src, count)], ws.at[i, pl.ds(dst, count)], s_loc.at[3]).start()
    pltpu.make_async_copy(wo_hbm, ws.at[3], s_loc.at[3]).start()
    taps_own = pltpu.make_async_copy(cw_hbm, cw, s_loc.at[4])
    taps_own.start()
    first = jnp.minimum(tm, 1)
    cache_two = pltpu.make_async_copy(cache_hbm.at[first], cb.at[0, pl.ds(1, R)], s_loc.at[5])
    cache_one = pltpu.make_async_copy(cache_hbm.at[1], cb.at[1, pl.ds(1, R)], s_loc.at[6])
    pl.when(tm <= 1)(cache_two.start)
    pl.when(tm == 0)(cache_one.start)

    blank = jnp.zeros((W, C), BF16)
    for f in range(3):
        cb[f, 0] = blank
        cb[f, R + 1] = blank

    x_own.wait()
    for k in range(hr):
        a, b = xo[2 * k], xo[2 * k + 1]
        xg[z, k, c] = jnp.concatenate([a[:, :L], b[:, :L], a[:, L:], b[:, L:]], axis=-1)

    want = 1 + jnp.where(z > 0, 1, 0) + jnp.where(z < Z - 1, 1, 0)
    for hop in (1, 2):
        if N > hop:
            want = want + jnp.where(tm + hop < N, 1, 0)
    pl.semaphore_wait(barrier, want)

    def rightward(j, k, n=W):
        ref = xg.at[j, k, c, pl.ds(0, n)]
        return send(ref, ref, s_right.at[k], r_z.at[j, k], dev(dz=z + 1))

    def leftward(j, k, n=W):
        ref = xg.at[j, k, c, pl.ds(0, n)]
        return send(ref, ref, s_left.at[k], r_z.at[j, k], dev(dz=z - 1))

    def sideward(j, k, flow, n=W):
        ref = xg.at[j, k, c, pl.ds(0, n)]
        return send(ref, ref, s_sib.at[flow, k], r_sib.at[j, k], dev(core=o))

    def closing(j, kind, core, to):
        ref = xg.at[j, hr - 1, core, pl.ds(head, tail)]
        return send(ref, ref, s_last.at[kind], r_last.at[kind], dev(dz=to, core=o if kind else c))

    def outward(k):
        pl.when(z < Z - 1)(rightward(z, k).start)
        pl.when(z > 0)(leftward(z, k).start)

    outward(0)
    for k in range(hr):
        sideward(z, k, 0).start()

    gains[0].wait()
    gain_one = g1_ref[...].astype(F32).reshape(1, C)
    gain_one = jnp.concatenate([gain_one[:, at : at + count] for at, _, count in blocks], axis=-1)
    low_lanes = lax.broadcasted_iota(jnp.int32, (W, L), 1) < E

    def tokens(j, k):
        p, q = xg[j, k, 0].astype(F32), xg[j, k, 1].astype(F32)
        pt, qt = p[:, 2 * L :], q[:, 2 * L :]
        even = jnp.where(low_lanes, pt, pltpu.roll(qt, E, 1))
        odd = jnp.where(low_lanes, pltpu.roll(pt, E, 1), qt)
        return jnp.concatenate([
            jnp.concatenate([p[:, :L], q[:, :L], even], axis=-1),
            jnp.concatenate([p[:, L : 2 * L], q[:, L : 2 * L], odd], axis=-1),
        ], axis=0)

    def normed(wide):
        return normalized(wide, gain_one).astype(BF16)

    top[...] = jnp.full(top.shape, -1e30, F32)
    total[...] = jnp.zeros(total.shape, F32)
    acc[...] = jnp.zeros(acc.shape, F32)

    everything = pl.ds(0, hr * W)

    def attend(keys, at=everything):
        scores = lax.dot_general(qk[at, :], keys, (((1,), (1,)), ((), ())), preferred_element_type=F32)
        old = top[at, :]
        new = jnp.maximum(old, jnp.max(scores, axis=-1, keepdims=True))
        weight = jnp.exp2(scores - new)
        fade = jnp.exp2(old - new)
        top[at, :] = new
        total[at, :] = total[at, :] * fade + jnp.sum(weight, axis=-1, keepdims=True)
        acc[at, :] = acc[at, :] * fade + jnp.dot(weight.astype(BF16), keys, preferred_element_type=F32)

    for k in range(hr):
        sideward(z, k, 0).wait_recv()
    for k in range(1, hr):
        outward(k)
    pltpu.make_async_copy(ws, ws, s_loc.at[3]).wait()
    mine = tokens(z, c)
    xn[...] = jnp.concatenate(
        [mine[:, :L], mine[:, 2 * L : 2 * L + E], mine[:, L : 2 * L], mine[:, 2 * L + E :]], axis=-1
    ).astype(BF16)
    keys = normed(mine)
    query = jnp.dot(keys, ws[0], preferred_element_type=F32).astype(BF16)
    folded = lax.dot_general(query, ws[1], (((1,), (1,)), ((), ())), preferred_element_type=F32)
    qk[...] = (folded * (C ** (-0.5) * math.log2(math.e))).astype(BF16)
    attend(keys)
    attend(normed(tokens(z, o)))
    wvo[...] = jnp.dot(ws[2], ws[3], preferred_element_type=F32).astype(BF16)

    def piece(f, dw, start):
        rows = jnp.concatenate([cb[f, dh : dh + R].reshape(T, C) for dh in range(3)], axis=-1)
        kernel_rows = jnp.concatenate([cw[f, dh, dw] for dh in range(3)], axis=-1)
        value = lax.dot_general(rows, kernel_rows, (((1,), (1,)), ((), ())), preferred_element_type=F32)
        if start:
            parts[dw, pl.ds(8, T)] = value
        else:
            parts[dw, pl.ds(8, T)] += value

    def early(i):
        f, dw = divmod(i, 3)
        there = tm <= 1 if f == 0 else jnp.logical_and(tm == 0, is_end)
        pl.when(there)(lambda: piece(f, dw, f == 0))

    taps_own.wait()
    pl.when(tm <= 1)(cache_two.wait)
    pl.when(tm == 0)(cache_one.wait)
    early(0)

    def cache_edge(f):
        row = jnp.where(c == 0, 0, R - 1)
        source = cache_hbm.at[first if f == 0 else 1, row]
        return send(source, hb.at[f, o], s_cache.at[f], r_halo.at[f, o], dev(dz=near))

    def cache_edges(act):
        pl.when(jnp.logical_and(has_near, tm <= 1))(lambda: act(cache_edge(0)))
        pl.when(jnp.logical_and(has_near, tm == 0))(lambda: act(cache_edge(1)))

    ahead = Z - 1 - z
    longer = jnp.maximum(z, ahead)
    sign = jnp.where(ahead >= z, 1, -1)
    shorter = Z - 1 - longer
    edges_at = jnp.where(c == 0, ahead, z) + 1
    slots = 5

    def passing(j, k, d, ward, flow, onward, to, source):
        def give(n):
            ward(j, k).wait_send()
            ward(j, k, n).start()

        def share(n):
            if flow == 0:
                sideward(j, k, 0).wait_send()
            else:
                pl.when(d > 1)(sideward(j, k, 1).wait_send)
            sideward(j, k, flow, n).start()

        if k < hr - 1:
            ward(j, k).wait_recv()
            pl.when(onward)(lambda: give(W))
            share(W)
            return

        closes = jnp.logical_and(j == source, jnp.logical_not(onward))
        before = jnp.logical_and(j == source, jnp.logical_or(to == 0, to == Z - 1))

        @pl.when(closes)
        def _():
            ward(j, k, head).wait_recv()
            share(head)

        @pl.when(jnp.logical_not(closes))
        def _():
            ward(j, k).wait_recv()

            @pl.when(jnp.logical_and(onward, before))
            def _():
                give(head)

            pl.when(jnp.logical_and(onward, jnp.logical_not(before)))(lambda: give(W))
            share(W)

    def step(d, carry):
        lo, hi = z - d, z + d

        for k in range(hr):
            pl.when(lo >= 0)(lambda: passing(lo, k, d, rightward, 0, z < Z - 1, z + 1, 0))
            pl.when(hi < Z)(lambda: passing(hi, k, d, leftward, 1, z > 0, z - 1, Z - 1))

            if k == hr - 1:
                pl.when(d == edges_at)(lambda: cache_edges(lambda copy: copy.start()))

            for i in range(slots):
                if i % hr == k:
                    pl.when(d == i // hr + 1)(functools.partial(early, i + 1))

            @pl.when(jnp.logical_and(d > 1, d - 1 <= shorter))
            def _():
                j = z - sign * (d - 1)
                sideward(j, k, 0).wait_recv()
                attend(normed(tokens(j, k)))

            def visit():
                j = z + sign * d
                sideward(j, k, 0).wait_recv()
                attend(normed(tokens(j, k)))

            if k < hr - 1:
                visit()
            else:
                pl.when(d < longer)(visit)

        return carry

    lax.fori_loop(1, longer + 1, step, 0)

    last = z + sign * longer

    def closings(act):
        @pl.when(jnp.logical_or(z == 1, z == Z - 2))
        def _():
            for kind in (0, 1):
                act(closing(z + sign * longer, kind, c, z - sign))

    closings(lambda copy: copy.start())
    pl.when(inner)(sideward(last, hr - 1, 0).wait_recv)

    @pl.when(is_end)
    def _():
        for kind in (0, 1):
            closing(last, kind, o if kind else c, z).wait_recv()
        sideward(last, hr - 1, 0, head).wait_recv()

    keys = normed(tokens(last, hr - 1))

    gains[1].wait()
    gain_two = g2_ref[...].astype(F32).reshape(1, C)

    def finish_rows(row, count):
        at = pl.ds(pl.multiple_of(row * W, W), count * W)
        attend(keys, at)
        mixed = (acc[at, :] * (1.0 / total[at, :])).astype(BF16)
        joined = xn[at, :].astype(F32) + jnp.dot(mixed, wvo[...], preferred_element_type=F32)
        joined = joined.astype(BF16).astype(F32)
        scaled = normalized(joined, gain_two)
        act = (scaled / (1.0 + jnp.exp(-scaled))).astype(BF16)
        cb[2, pl.ds(1 + c * hr + row, count)] = act.reshape(count, W, C)
        return joined

    def keep_joined(row, count, joined):
        low, high = joined[:, :S].astype(BF16), joined[:, S:].astype(BF16)
        jo[pl.ds(c * hr + row, count)] = jnp.where(c == 0, low, high).reshape(count, W, S)
        jt[pl.ds(row, count)] = jnp.where(c == 0, high, low).reshape(count, W, S)

    edge = jnp.where(c == 0, 1, R)
    rest = jnp.where(c == 0, 2, 1 + hr)
    other = jnp.where(c == 0, 1 + hr, 2)
    spans = ((0, W), (0, head), (head, tail), (head, tail))
    def drain(there, short, copy):
        pl.when(jnp.logical_and(there, short))(copy(head).wait_send)
        pl.when(jnp.logical_and(there, jnp.logical_not(short)))(copy(W).wait_send)

    def drain_gather():
        for k in range(hr):
            at = z if k == hr - 1 else -1
            drain(z < Z - 1, at == Z - 2, lambda n: rightward(z, k, n))
            drain(z > 0, at == 1, lambda n: leftward(z, k, n))
            drain(True, at == Z - 1, lambda n: sideward(z, k, 0, n))
            drain(z < Z - 1, at == 0, lambda n: sideward(z, k, 1, n))

    spare = [s_right.at[0], s_right.at[1], s_left.at[0], s_left.at[1], s_sib.at[0, 0], s_sib.at[0, 1], s_sib.at[1, 0]]

    def along_tm(hop, part):
        cells = pl.ds(*spans[part])
        src, dst = (cb.at[f, rest if part else edge, cells] for f in (2, 2 - hop))
        to = dev(frame=tm + hop, core=o if part == 3 else None)
        return send(src, dst, s_tm.at[hop - 1, part], r_tm.at[hop - 1, part], to)

    def from_tm(f, part):
        row = cb.at[f, (edge, rest, rest, other)[part], pl.ds(*spans[part])]
        send(row, row, s_tm.at[1 - f, part], r_tm.at[1 - f, part], dev(core=o)).wait_recv()

    def edge_copy(f):
        src = cb.at[f, edge]
        return send(src, src, s_edge.at[2 - f], r_edge.at[2 - f], dev(core=o))

    def near_copy(hop):
        return send(
            cb.at[2, edge], hb.at[2 - hop, o], s_near.at[hop], r_halo.at[2 - hop, o],
            dev(dz=near, frame=tm + hop),
        )

    def near_copies(act):
        pl.when(has_near)(lambda: act(near_copy(0)))
        for hop in range(1, min(3, N)):
            pl.when(jnp.logical_and(jnp.logical_and(has_near, is_end), tm + hop < N))(
                functools.partial(lambda h: act(near_copy(h)), hop)
            )

    def near_pass(f):
        return send(cb.at[f, edge], hb.at[f, o], s_near.at[2 - f], r_halo.at[f, o], dev(dz=near))

    def rest_copy(f):
        src = cb.at[f, rest, pl.ds(0, W if f == 2 else head)]
        return send(src, src, spare[2 - f], r_rest.at[2 - f], dev(core=o))

    def edge_row(f):
        row = cb.at[f, jnp.where(c == 0, R, 1)]
        send(row, row, s_edge.at[2 - f], r_edge.at[2 - f], dev(core=o)).wait_recv()

    def rest_row(f):
        row = cb.at[f, other, pl.ds(0, W if f == 2 else head)]
        send(row, row, spare[2 - f], r_rest.at[2 - f], dev(core=o)).wait_recv()

    def from_sibling(f):
        edge_row(f)
        rest_row(f)

    def relay(f):
        row = hb.at[f, o]
        return send(row, row, spare[3 + f], r_halo.at[f, o], dev(core=o))

    def relay_halo(f):
        @pl.when(has_back)
        def _():
            relay(f).wait_recv()
            relay(f).start()

    def both_sides(visit):
        pl.when(z > 0)(lambda: visit(0))
        pl.when(z < Z - 1)(lambda: visit(1))

    for part in (0, 1):
        if part:
            drain_gather()
        row = (rest if part else edge) - 1 - c * hr
        joined = finish_rows(row, 1)
        for hop in (1, 2):
            if N > hop:
                for p in (1, 2, 3) if part else (0,):
                    pl.when(tm + hop < N)(along_tm(hop, p).start)
        if part == 0:
            edge_copy(2).start()
            near_copies(lambda copy: copy.start())
        else:
            rest_copy(2).start()
        keep_joined(row, 1, joined)

    pl.when(edges_at > longer)(lambda: cache_edges(lambda copy: copy.start()))

    joined_copy = send(jt, jo.at[pl.ds(c * hr, hr)], spare[6], r_pair, dev(core=o))
    joined_copy.start()

    def taps(f, start):
        for dw in range(3):
            piece(f, dw, start)

    def forwarded(f, part):
        from_tm(f, part)
        if part == 0:
            edge_copy(f).start()
            pl.when(jnp.logical_and(has_near, inner))(near_pass(f).start)
        else:
            rest_copy(f).start()

    def product(f, dh, dw, at):
        return lax.dot_general(cb[f, at], cw[f, dh, dw], (((1,), (1,)), ((), ())), preferred_element_type=F32)

    def outer_taps(f):
        for dw in range(3):
            rows = jnp.concatenate([cb[f, 1], cb[f, R]], axis=0)
            both = lax.dot_general(rows, cw[f, 1, dw], (((1,), (1,)), ((), ())), preferred_element_type=F32)
            parts[dw, pl.ds(8, W)] += both[:W]
            parts[dw, pl.ds(8 + (R - 1) * W, W)] += both[W:]
            parts[dw, pl.ds(8 + W, W)] += product(f, 0, dw, 1)
            parts[dw, pl.ds(8 + (R - 2) * W, W)] += product(f, 2, dw, R)

    def row_taps(f, pieces):
        rows = jnp.concatenate([cb[f, row, at : at + count] for row, at, count in pieces], axis=0)
        for dw in range(3):
            for dh in range(3):
                value = lax.dot_general(rows, cw[f, dh, dw], (((1,), (1,)), ((), ())), preferred_element_type=F32)
                start = 0
                for row, at, count in pieces:
                    place = pl.ds(pl.multiple_of(8 + (row - dh) * W + at, 8), count)
                    parts[dw, place] += value[start : start + count]
                    start += count

    def other_halo(f):
        row = hb.at[f, c]
        pl.when(has_near)(send(row, row, spare[3 + f], r_halo.at[f, c], dev(core=o)).wait_recv)

    def halo_taps(frames):
        for f in frames:
            other_halo(f)

        def visit(side):
            rows = jnp.concatenate([hb[f, side] for f in frames], axis=-1)
            for dw in range(3):
                kernel_rows = jnp.concatenate([cw[f, 2 * side, dw] for f in frames], axis=-1)
                parts[dw, pl.ds(8 + side * (T - W), W)] += lax.dot_general(
                    rows, kernel_rows, (((1,), (1,)), ((), ())), preferred_element_type=F32
                )

        both_sides(visit)

    def halos(frames):
        for f in frames:
            relay_halo(f)
        halo_taps(frames)

    late = (0, 2) if N == 2 else (2,)

    def relays():
        for f in late:
            relay_halo(f)

    pl.when(jnp.logical_and(tm >= 1, is_end))(relays)
    from_sibling(2)
    if N > 2:
        pl.when(tm <= 1)(lambda: taps(2, False))
        pl.when(tm >= 2)(lambda: taps(2, True))
    else:
        taps(2, False)

    there = jo.at[pl.ds(o * hr, hr)]
    send(jt, there, spare[6], r_pair, dev(core=o)).wait_recv()
    parts[1, pl.ds(8, T)] += jo[...].reshape(T, S).astype(F32)

    pl.when(jnp.logical_and(tm == 0, inner))(lambda: taps(1, False))
    pl.when(tm == 0)(lambda: halos((0, 2, 1)))
    if N > 1:

        @pl.when(tm >= 1)
        def _():
            pl.when(jnp.logical_and(is_end, has_near))(lambda: halo_taps(late))
            forwarded(1, 0)
            pl.when(jnp.logical_and(is_end, has_back))(lambda: halo_taps(late))
            pl.when(is_end)(lambda: relay_halo(1))
            edge_row(1)
            outer_taps(1)
            pl.when(jnp.logical_and(is_end, has_near))(lambda: halo_taps((1,)))
            forwarded(1, 1)
            row_taps(1, ((rest, 0, head),))
            pl.when(jnp.logical_and(is_end, has_back))(lambda: halo_taps((1,)))
            from_tm(1, 2)
            from_tm(1, 3)
            rest_row(1)
            row_taps(1, ((rest, head, tail), (other, 0, W)))

            @pl.when(inner)
            def _():
                relays()
                relay_halo(1)
                halo_taps(late + (1,))
    if N > 2:

        @pl.when(tm >= 2)
        def _():
            forwarded(0, 0)
            forwarded(0, 1)
            from_tm(0, 2)
            from_tm(0, 3)
            from_sibling(0)
            taps(0, False)

        pl.when(tm >= 1)(lambda: halos((0,)))

    cell = lax.rem(lax.broadcasted_iota(jnp.int32, (T, S), 0), W)
    before = jnp.where(cell == 0, 0.0, parts[0, pl.ds(7, T)])
    after = jnp.where(cell == W - 1, 0.0, parts[2, pl.ds(9, T)])
    out_ref[0] = (before + parts[1, pl.ds(8, T)] + after).astype(BF16).reshape(R, W, S)

    joined_copy.wait_send()
    closings(lambda copy: copy.wait_send())
    cache_edges(lambda copy: copy.wait_send())
    for f in range(3):
        pl.when(has_back)(relay(f).wait_send)
    near_copies(lambda copy: copy.wait_send())
    for part in range(4):
        for hop in (1, 2):
            if N > hop:
                pl.when(tm + hop < N)(along_tm(hop, part).wait_send)

    def spread_done(f):
        edge_copy(f).wait_send()
        rest_copy(f).wait_send()
        if f < 2:
            pl.when(jnp.logical_and(has_near, inner))(near_pass(f).wait_send)

    spread_done(2)
    if N > 1:
        pl.when(tm >= 1)(lambda: spread_done(1))
    if N > 2:
        pl.when(tm >= 2)(lambda: spread_done(0))


def solution(mesh):
    Z, N = mesh.shape["space"], mesh.shape["tm"]

    def body(frames_in, cache, gain_one, gain_two, w_query, w_key, w_value, w_out, conv_weight):
        _, R, W, S = frames_in.shape
        C = 2 * S
        hr, half, T = R // 2, R // 2 * W, R * W
        hops, sets = max(1, min(2, N - 1)), min(3, N)
        dma = pltpu.SemaphoreType.DMA
        hbm = pl.BlockSpec(memory_space=pltpu.HBM)
        vmem = pl.BlockSpec(memory_space=pltpu.VMEM)
        return pl.pallas_call(
            functools.partial(kernel, Z, N),
            out_shape=jax.ShapeDtypeStruct(frames_in.shape, BF16),
            in_specs=[hbm] * 9,
            out_specs=vmem,
            scratch_shapes=[
                pltpu.VMEM((R, W, S), BF16),
                pltpu.VMEM((Z, hr, 2, W, C), BF16),
                pltpu.VMEM((half, C), BF16),
                pltpu.VMEM((half, C), BF16),
                pltpu.VMEM((half, 1), F32),
                pltpu.VMEM((half, 1), F32),
                pltpu.VMEM((half, C), F32),
                pltpu.VMEM((3, R + 2, W, C), BF16),
                pltpu.VMEM((3, 2, W, C), BF16),
                pltpu.VMEM((hr, W, S), BF16),
                pltpu.VMEM((R, W, S), BF16),
                pltpu.VMEM((3, T + 16, S), F32),
                pltpu.VMEM((C,), BF16),
                pltpu.VMEM((C,), BF16),
                pltpu.VMEM((4, C, C), BF16),
                pltpu.VMEM((C, C), BF16),
                pltpu.VMEM((3, 3, 3, S, C), BF16),
                dma((7,)),
                dma,
                dma((hr,)),
                dma((hr,)),
                dma((2, hr)),
                dma((Z, hr)),
                dma((Z, hr)),
                dma((2,)),
                dma((2,)),
                dma((2,)),
                dma((3, 2)),
                dma((sets,)),
                dma((sets,)),
                dma((sets,)),
                dma((sets,)),
                dma((hops, 4)),
                dma((hops, 4)),
            ],
            compiler_params=pltpu.CompilerParams(
                collective_id=0, has_side_effects=True, vmem_limit_bytes=50 << 20
            ),
        )(*(pltpu.with_memory_space_constraint(a, pltpu.HBM) for a in (
            frames_in, cache, gain_one, gain_two,
            w_query, w_key, w_value, w_out, jnp.swapaxes(conv_weight, 3, 4),
        )))

    return jax.shard_map(
        body,
        mesh=mesh,
        in_specs=(
            P(("clips", "tm"), "space", None, "chan"),
            P("clips", "space", None, None),
            P(),
            P(),
            P(),
            P(),
            P(),
            P(),
            P(None, None, None, None, "chan"),
        ),
        out_specs=P(("clips", "tm"), "space", None, "chan"),
        check_vma=False,
    )
```

```python
import functools
import math

import jax
import jax.numpy as jnp
from jax import lax
from jax.experimental import pallas as pl
from jax.experimental.pallas import tpu as pltpu
from jax.sharding import PartitionSpec as P

F32 = jnp.float32
BF16 = jnp.bfloat16
MESH = pl.DeviceIdType.MESH


def normalized(wide, gain):
    factor = lax.rsqrt(jnp.mean(wide * wide, axis=-1, keepdims=True) + 1e-06)
    return wide * factor * gain


def kernel(
    Z, N,
    x_hbm, cache_hbm, g1_hbm, g2_hbm, wq_hbm, wk_hbm, wv_hbm, wo_hbm, cw_hbm,
    out_ref,
    xo, xg, xn, qk, top, total, acc, cb, hb, jt, jo, parts, g1_ref, g2_ref, ws, wvo, cw,
    s_loc, r_pair, s_right, s_left, s_sib, r_z, r_sib, s_last, r_last,
    s_cache, r_halo, s_near, s_edge, r_edge, r_rest, s_tm, r_tm,
):
    z = lax.axis_index("space")
    c = lax.axis_index("chan")
    tm = lax.axis_index("tm")
    o = 1 - c
    R, W, S = out_ref.shape[1:]
    C = 2 * S
    hr = R // 2
    T = R * W
    last_tail = 3 * W // 10
    last_head = W - last_tail
    L = 128
    E = S - L
    blocks = ((0, 0, L), (S, L, L), (L, 2 * L, E), (S + L, 2 * L + E, E))

    def dev(dz=None, core=None, frame=None):
        return {
            "space": z if dz is None else dz,
            "chan": c if core is None else core,
            "tm": tm if frame is None else frame,
        }

    def send(src, dst, ssem, rsem, to):
        return pltpu.make_async_remote_copy(
            src_ref=src, dst_ref=dst, send_sem=ssem, recv_sem=rsem,
            device_id=to, device_id_type=MESH,
        )

    near, back = z + 2 * c - 1, z + 1 - 2 * c
    has_near = jnp.logical_and(near >= 0, near < Z)
    has_back = jnp.logical_and(back >= 0, back < Z)
    is_end = jnp.logical_or(z == 0, z == Z - 1)
    inner = jnp.logical_not(is_end)

    barrier = pltpu.get_barrier_semaphore()

    def greet(to):
        pl.semaphore_signal(barrier, inc=1, device_id=to, device_id_type=MESH)

    greet(dev(core=o))
    pl.when(z > 0)(lambda: greet(dev(dz=z - 1)))
    pl.when(z < Z - 1)(lambda: greet(dev(dz=z + 1)))
    for hop in (1, 2):
        if N > hop:
            pl.when(tm >= hop)(functools.partial(lambda h: greet(dev(frame=tm - h)), hop))

    x_own = pltpu.make_async_copy(x_hbm.at[0], xo, s_loc.at[0])
    x_own.start()
    gains = [
        pltpu.make_async_copy(a, b, s_loc.at[1 + i])
        for i, (a, b) in enumerate(((g1_hbm, g1_ref), (g2_hbm, g2_ref)))
    ]
    for g in gains:
        g.start()
    for i, w_hbm in enumerate((wq_hbm, wk_hbm, wv_hbm)):
        for src, dst, count in blocks:
            pltpu.make_async_copy(w_hbm.at[pl.ds(src, count)], ws.at[i, pl.ds(dst, count)], s_loc.at[3]).start()
    pltpu.make_async_copy(wo_hbm, ws.at[3], s_loc.at[3]).start()
    taps_own = pltpu.make_async_copy(cw_hbm, cw, s_loc.at[4])
    taps_own.start()
    first = jnp.minimum(tm, 1)
    cache_two = pltpu.make_async_copy(cache_hbm.at[first], cb.at[0, pl.ds(1, R)], s_loc.at[5])
    cache_one = pltpu.make_async_copy(cache_hbm.at[1], cb.at[1, pl.ds(1, R)], s_loc.at[6])
    pl.when(tm <= 1)(cache_two.start)
    pl.when(tm == 0)(cache_one.start)

    blank = jnp.zeros((W, C), BF16)
    for f in range(3):
        cb[f, 0] = blank
        cb[f, R + 1] = blank

    x_own.wait()
    for k in range(hr):
        a, b = xo[2 * k], xo[2 * k + 1]
        xg[z, k, c] = jnp.concatenate([a[:, :L], b[:, :L], a[:, L:], b[:, L:]], axis=-1)

    want = 1 + jnp.where(z > 0, 1, 0) + jnp.where(z < Z - 1, 1, 0)
    for hop in (1, 2):
        if N > hop:
            want = want + jnp.where(tm + hop < N, 1, 0)
    pl.semaphore_wait(barrier, want)

    def rightward(j, k, n=W):
        ref = xg.at[j, k, c, pl.ds(0, n)]
        return send(ref, ref, s_right.at[k], r_z.at[j, k], dev(dz=z + 1))

    def leftward(j, k, n=W):
        ref = xg.at[j, k, c, pl.ds(0, n)]
        return send(ref, ref, s_left.at[k], r_z.at[j, k], dev(dz=z - 1))

    def sideward(j, k, flow, n=W):
        ref = xg.at[j, k, c, pl.ds(0, n)]
        return send(ref, ref, s_sib.at[flow, k], r_sib.at[j, k], dev(core=o))

    def closing(j, kind, core, to):
        ref = xg.at[j, hr - 1, core, pl.ds(last_head, last_tail)]
        return send(ref, ref, s_last.at[kind], r_last.at[kind], dev(dz=to, core=o if kind else c))

    def outward(k):
        pl.when(z < Z - 1)(rightward(z, k).start)
        pl.when(z > 0)(leftward(z, k).start)

    outward(0)
    for k in range(hr):
        sideward(z, k, 0).start()

    gains[0].wait()
    gain_one = g1_ref[...].astype(F32).reshape(1, C)
    gain_one = jnp.concatenate([gain_one[:, at : at + count] for at, _, count in blocks], axis=-1)
    low_lanes = lax.broadcasted_iota(jnp.int32, (W, L), 1) < E

    def tokens(j, k):
        p, q = xg[j, k, 0].astype(F32), xg[j, k, 1].astype(F32)
        pt, qt = p[:, 2 * L :], q[:, 2 * L :]
        even = jnp.where(low_lanes, pt, pltpu.roll(qt, E, 1))
        odd = jnp.where(low_lanes, pltpu.roll(pt, E, 1), qt)
        return jnp.concatenate([
            jnp.concatenate([p[:, :L], q[:, :L], even], axis=-1),
            jnp.concatenate([p[:, L : 2 * L], q[:, L : 2 * L], odd], axis=-1),
        ], axis=0)

    def normed(wide):
        return normalized(wide, gain_one).astype(BF16)

    top[...] = jnp.full(top.shape, -1e30, F32)
    total[...] = jnp.zeros(total.shape, F32)
    acc[...] = jnp.zeros(acc.shape, F32)

    everything = pl.ds(0, hr * W)

    def attend(keys, at=everything):
        scores = lax.dot_general(qk[at, :], keys, (((1,), (1,)), ((), ())), preferred_element_type=F32)
        old = top[at, :]
        new = jnp.maximum(old, jnp.max(scores, axis=-1, keepdims=True))
        weight = jnp.exp2(scores - new)
        fade = jnp.exp2(old - new)
        top[at, :] = new
        total[at, :] = total[at, :] * fade + jnp.sum(weight, axis=-1, keepdims=True)
        acc[at, :] = acc[at, :] * fade + jnp.dot(weight.astype(BF16), keys, preferred_element_type=F32)

    for k in range(hr):
        sideward(z, k, 0).wait_recv()
    for k in range(1, hr):
        outward(k)
    pltpu.make_async_copy(ws, ws, s_loc.at[3]).wait()
    mine = tokens(z, c)
    xn[...] = jnp.concatenate(
        [mine[:, :L], mine[:, 2 * L : 2 * L + E], mine[:, L : 2 * L], mine[:, 2 * L + E :]], axis=-1
    ).astype(BF16)
    keys = normed(mine)
    query = jnp.dot(keys, ws[0], preferred_element_type=F32).astype(BF16)
    folded = lax.dot_general(query, ws[1], (((1,), (1,)), ((), ())), preferred_element_type=F32)
    qk[...] = (folded * (C ** (-0.5) * math.log2(math.e))).astype(BF16)
    attend(keys)
    attend(normed(tokens(z, o)))
    wvo[...] = jnp.dot(ws[2], ws[3], preferred_element_type=F32).astype(BF16)

    def piece(f, dw, start):
        rows = jnp.concatenate([cb[f, dh : dh + R].reshape(T, C) for dh in range(3)], axis=-1)
        kernel_rows = jnp.concatenate([cw[f, dh, dw] for dh in range(3)], axis=-1)
        value = lax.dot_general(rows, kernel_rows, (((1,), (1,)), ((), ())), preferred_element_type=F32)
        if start:
            parts[dw, pl.ds(8, T)] = value
        else:
            parts[dw, pl.ds(8, T)] += value

    def early(i):
        f, dw = divmod(i, 3)
        there = tm <= 1 if f == 0 else jnp.logical_and(tm == 0, is_end)
        pl.when(there)(lambda: piece(f, dw, f == 0))

    taps_own.wait()
    pl.when(tm <= 1)(cache_two.wait)
    pl.when(tm == 0)(cache_one.wait)
    early(0)

    def cache_edge(f):
        row = jnp.where(c == 0, 0, R - 1)
        source = cache_hbm.at[first if f == 0 else 1, row]
        return send(source, hb.at[f, o], s_cache.at[f], r_halo.at[f, o], dev(dz=near))

    def cache_edges(act):
        pl.when(jnp.logical_and(has_near, tm <= 1))(lambda: act(cache_edge(0)))
        pl.when(jnp.logical_and(has_near, tm == 0))(lambda: act(cache_edge(1)))

    ahead = Z - 1 - z
    longer = jnp.maximum(z, ahead)
    sign = jnp.where(ahead >= z, 1, -1)
    shorter = Z - 1 - longer
    edges_at = jnp.where(c == 0, ahead, z) + 1
    slots = 5

    def passing(j, k, d, ward, flow, onward, to, source):
        def give(n):
            ward(j, k).wait_send()
            ward(j, k, n).start()

        def share(n):
            if flow == 0:
                sideward(j, k, 0).wait_send()
            else:
                pl.when(d > 1)(sideward(j, k, 1).wait_send)
            sideward(j, k, flow, n).start()

        if k < hr - 1:
            ward(j, k).wait_recv()
            pl.when(onward)(lambda: give(W))
            share(W)
            return

        closes = jnp.logical_and(j == source, jnp.logical_not(onward))
        before = jnp.logical_and(j == source, jnp.logical_or(to == 0, to == Z - 1))

        @pl.when(closes)
        def _():
            ward(j, k, last_head).wait_recv()
            share(last_head)

        @pl.when(jnp.logical_not(closes))
        def _():
            ward(j, k).wait_recv()

            @pl.when(jnp.logical_and(onward, before))
            def _():
                give(last_head)

            pl.when(jnp.logical_and(onward, jnp.logical_not(before)))(lambda: give(W))
            share(W)

    def step(d, carry):
        lo, hi = z - d, z + d

        for k in range(hr):
            pl.when(lo >= 0)(lambda: passing(lo, k, d, rightward, 0, z < Z - 1, z + 1, 0))
            pl.when(hi < Z)(lambda: passing(hi, k, d, leftward, 1, z > 0, z - 1, Z - 1))

            if k == hr - 1:
                pl.when(d == edges_at)(lambda: cache_edges(lambda copy: copy.start()))

            for i in range(slots):
                if i % hr == k:
                    pl.when(d == i // hr + 1)(functools.partial(early, i + 1))

            @pl.when(jnp.logical_and(d > 1, d - 1 <= shorter))
            def _():
                j = z - sign * (d - 1)
                sideward(j, k, 0).wait_recv()
                attend(normed(tokens(j, k)))

            def visit():
                j = z + sign * d
                sideward(j, k, 0).wait_recv()
                attend(normed(tokens(j, k)))

            if k < hr - 1:
                visit()
            else:
                pl.when(d < longer)(visit)

        return carry

    lax.fori_loop(1, longer + 1, step, 0)

    last = z + sign * longer

    def closings(act):
        @pl.when(jnp.logical_or(z == 1, z == Z - 2))
        def _():
            for kind in (0, 1):
                act(closing(z + sign * longer, kind, c, z - sign))

    closings(lambda copy: copy.start())
    pl.when(inner)(sideward(last, hr - 1, 0).wait_recv)

    @pl.when(is_end)
    def _():
        for kind in (0, 1):
            closing(last, kind, o if kind else c, z).wait_recv()
        sideward(last, hr - 1, 0, last_head).wait_recv()

    keys = normed(tokens(last, hr - 1))

    gains[1].wait()
    gain_two = g2_ref[...].astype(F32).reshape(1, C)

    def finish_rows(row, count):
        at = pl.ds(pl.multiple_of(row * W, W), count * W)
        attend(keys, at)
        mixed = (acc[at, :] * (1.0 / total[at, :])).astype(BF16)
        joined = xn[at, :].astype(F32) + jnp.dot(mixed, wvo[...], preferred_element_type=F32)
        joined = joined.astype(BF16).astype(F32)
        scaled = normalized(joined, gain_two)
        act = (scaled / (1.0 + jnp.exp(-scaled))).astype(BF16)
        cb[2, pl.ds(1 + c * hr + row, count)] = act.reshape(count, W, C)
        return joined

    def keep_joined(row, count, joined):
        low, high = joined[:, :S].astype(BF16), joined[:, S:].astype(BF16)
        jo[pl.ds(c * hr + row, count)] = jnp.where(c == 0, low, high).reshape(count, W, S)
        jt[pl.ds(row, count)] = jnp.where(c == 0, high, low).reshape(count, W, S)

    edge = jnp.where(c == 0, 1, R)
    rest = jnp.where(c == 0, 2, 1 + hr)
    other = jnp.where(c == 0, 1 + hr, 2)
    tail = W // 5
    head = W - tail
    spans = ((0, W), (0, head), (head, tail), (head, tail))
    def drain(there, short, copy):
        pl.when(jnp.logical_and(there, short))(copy(last_head).wait_send)
        pl.when(jnp.logical_and(there, jnp.logical_not(short)))(copy(W).wait_send)

    def drain_gather():
        for k in range(hr):
            at = z if k == hr - 1 else -1
            drain(z < Z - 1, at == Z - 2, lambda n: rightward(z, k, n))
            drain(z > 0, at == 1, lambda n: leftward(z, k, n))
            drain(True, at == Z - 1, lambda n: sideward(z, k, 0, n))
            drain(z < Z - 1, at == 0, lambda n: sideward(z, k, 1, n))

    spare = [s_right.at[0], s_right.at[1], s_left.at[0], s_left.at[1], s_sib.at[0, 0], s_sib.at[0, 1], s_sib.at[1, 0]]

    def along_tm(hop, part):
        cells = pl.ds(*spans[part])
        src, dst = (cb.at[f, rest if part else edge, cells] for f in (2, 2 - hop))
        to = dev(frame=tm + hop, core=o if part == 3 else None)
        return send(src, dst, s_tm.at[hop - 1, part], r_tm.at[hop - 1, part], to)

    def from_tm(f, part):
        row = cb.at[f, (edge, rest, rest, other)[part], pl.ds(*spans[part])]
        send(row, row, s_tm.at[1 - f, part], r_tm.at[1 - f, part], dev(core=o)).wait_recv()

    def edge_copy(f):
        src = cb.at[f, edge]
        return send(src, src, s_edge.at[2 - f], r_edge.at[2 - f], dev(core=o))

    def near_copy(hop):
        return send(
            cb.at[2, edge], hb.at[2 - hop, o], s_near.at[hop], r_halo.at[2 - hop, o],
            dev(dz=near, frame=tm + hop),
        )

    def near_copies(act):
        pl.when(has_near)(lambda: act(near_copy(0)))
        for hop in range(1, min(3, N)):
            pl.when(jnp.logical_and(jnp.logical_and(has_near, is_end), tm + hop < N))(
                functools.partial(lambda h: act(near_copy(h)), hop)
            )

    def near_pass(f):
        return send(cb.at[f, edge], hb.at[f, o], s_near.at[2 - f], r_halo.at[f, o], dev(dz=near))

    def rest_copy(f):
        src = cb.at[f, rest, pl.ds(0, W if f == 2 else head)]
        return send(src, src, spare[2 - f], r_rest.at[2 - f], dev(core=o))

    def edge_row(f):
        row = cb.at[f, jnp.where(c == 0, R, 1)]
        send(row, row, s_edge.at[2 - f], r_edge.at[2 - f], dev(core=o)).wait_recv()

    def rest_row(f):
        row = cb.at[f, other, pl.ds(0, W if f == 2 else head)]
        send(row, row, spare[2 - f], r_rest.at[2 - f], dev(core=o)).wait_recv()

    def from_sibling(f):
        edge_row(f)
        rest_row(f)

    def relay(f):
        row = hb.at[f, o]
        return send(row, row, spare[3 + f], r_halo.at[f, o], dev(core=o))

    def relay_halo(f):
        @pl.when(has_back)
        def _():
            relay(f).wait_recv()
            relay(f).start()

    def both_sides(visit):
        pl.when(z > 0)(lambda: visit(0))
        pl.when(z < Z - 1)(lambda: visit(1))

    for part in (0, 1):
        if part:
            drain_gather()
        row = (rest if part else edge) - 1 - c * hr
        joined = finish_rows(row, 1)
        for hop in (1, 2):
            if N > hop:
                for p in (1, 2, 3) if part else (0,):
                    pl.when(tm + hop < N)(along_tm(hop, p).start)
        if part == 0:
            edge_copy(2).start()
            near_copies(lambda copy: copy.start())
        else:
            rest_copy(2).start()
        keep_joined(row, 1, joined)

    pl.when(edges_at > longer)(lambda: cache_edges(lambda copy: copy.start()))

    joined_copy = send(jt, jo.at[pl.ds(c * hr, hr)], spare[6], r_pair, dev(core=o))
    joined_copy.start()

    def taps(f, start):
        for dw in range(3):
            piece(f, dw, start)

    def forwarded(f, part):
        from_tm(f, part)
        if part == 0:
            edge_copy(f).start()
            pl.when(jnp.logical_and(has_near, inner))(near_pass(f).start)
        else:
            rest_copy(f).start()

    def product(f, dh, dw, at):
        return lax.dot_general(cb[f, at], cw[f, dh, dw], (((1,), (1,)), ((), ())), preferred_element_type=F32)

    def outer_taps(f):
        for dw in range(3):
            rows = jnp.concatenate([cb[f, 1], cb[f, R]], axis=0)
            both = lax.dot_general(rows, cw[f, 1, dw], (((1,), (1,)), ((), ())), preferred_element_type=F32)
            parts[dw, pl.ds(8, W)] += both[:W]
            parts[dw, pl.ds(8 + (R - 1) * W, W)] += both[W:]
            parts[dw, pl.ds(8 + W, W)] += product(f, 0, dw, 1)
            parts[dw, pl.ds(8 + (R - 2) * W, W)] += product(f, 2, dw, R)

    def row_taps(f, pieces):
        rows = jnp.concatenate([cb[f, row, at : at + count] for row, at, count in pieces], axis=0)
        for dw in range(3):
            for dh in range(3):
                value = lax.dot_general(rows, cw[f, dh, dw], (((1,), (1,)), ((), ())), preferred_element_type=F32)
                start = 0
                for row, at, count in pieces:
                    place = pl.ds(pl.multiple_of(8 + (row - dh) * W + at, 8), count)
                    parts[dw, place] += value[start : start + count]
                    start += count

    def other_halo(f):
        row = hb.at[f, c]
        pl.when(has_near)(send(row, row, spare[3 + f], r_halo.at[f, c], dev(core=o)).wait_recv)

    def halo_taps(frames):
        for f in frames:
            other_halo(f)

        def visit(side):
            rows = jnp.concatenate([hb[f, side] for f in frames], axis=-1)
            for dw in range(3):
                kernel_rows = jnp.concatenate([cw[f, 2 * side, dw] for f in frames], axis=-1)
                parts[dw, pl.ds(8 + side * (T - W), W)] += lax.dot_general(
                    rows, kernel_rows, (((1,), (1,)), ((), ())), preferred_element_type=F32
                )

        both_sides(visit)

    def halos(frames):
        for f in frames:
            relay_halo(f)
        halo_taps(frames)

    late = (0, 2) if N == 2 else (2,)

    def relays():
        for f in late:
            relay_halo(f)

    pl.when(jnp.logical_and(tm >= 1, is_end))(relays)
    from_sibling(2)
    if N > 2:
        pl.when(tm <= 1)(lambda: taps(2, False))
        pl.when(tm >= 2)(lambda: taps(2, True))
    else:
        taps(2, False)

    there = jo.at[pl.ds(o * hr, hr)]
    send(jt, there, spare[6], r_pair, dev(core=o)).wait_recv()
    parts[1, pl.ds(8, T)] += jo[...].reshape(T, S).astype(F32)

    pl.when(jnp.logical_and(tm == 0, inner))(lambda: taps(1, False))
    pl.when(tm == 0)(lambda: halos((0, 2, 1)))
    if N > 1:

        @pl.when(tm >= 1)
        def _():
            pl.when(jnp.logical_and(is_end, has_near))(lambda: halo_taps(late))
            forwarded(1, 0)
            pl.when(jnp.logical_and(is_end, has_back))(lambda: halo_taps(late))
            pl.when(is_end)(lambda: relay_halo(1))
            edge_row(1)
            outer_taps(1)
            pl.when(jnp.logical_and(is_end, has_near))(lambda: halo_taps((1,)))
            forwarded(1, 1)
            row_taps(1, ((rest, 0, head),))
            pl.when(jnp.logical_and(is_end, has_back))(lambda: halo_taps((1,)))
            from_tm(1, 2)
            from_tm(1, 3)
            rest_row(1)
            row_taps(1, ((rest, head, tail), (other, 0, W)))

            @pl.when(inner)
            def _():
                relays()
                relay_halo(1)
                halo_taps(late + (1,))
    if N > 2:

        @pl.when(tm >= 2)
        def _():
            forwarded(0, 0)
            forwarded(0, 1)
            from_tm(0, 2)
            from_tm(0, 3)
            from_sibling(0)
            taps(0, False)

        pl.when(tm >= 1)(lambda: halos((0,)))

    cell = lax.rem(lax.broadcasted_iota(jnp.int32, (T, S), 0), W)
    before = jnp.where(cell == 0, 0.0, parts[0, pl.ds(7, T)])
    after = jnp.where(cell == W - 1, 0.0, parts[2, pl.ds(9, T)])
    out_ref[0] = (before + parts[1, pl.ds(8, T)] + after).astype(BF16).reshape(R, W, S)

    joined_copy.wait_send()
    closings(lambda copy: copy.wait_send())
    cache_edges(lambda copy: copy.wait_send())
    for f in range(3):
        pl.when(has_back)(relay(f).wait_send)
    near_copies(lambda copy: copy.wait_send())
    for part in range(4):
        for hop in (1, 2):
            if N > hop:
                pl.when(tm + hop < N)(along_tm(hop, part).wait_send)

    def spread_done(f):
        edge_copy(f).wait_send()
        rest_copy(f).wait_send()
        if f < 2:
            pl.when(jnp.logical_and(has_near, inner))(near_pass(f).wait_send)

    spread_done(2)
    if N > 1:
        pl.when(tm >= 1)(lambda: spread_done(1))
    if N > 2:
        pl.when(tm >= 2)(lambda: spread_done(0))


def solution(mesh):
    Z, N = mesh.shape["space"], mesh.shape["tm"]

    def body(frames_in, cache, gain_one, gain_two, w_query, w_key, w_value, w_out, conv_weight):
        _, R, W, S = frames_in.shape
        C = 2 * S
        hr, half, T = R // 2, R // 2 * W, R * W
        hops, sets = max(1, min(2, N - 1)), min(3, N)
        dma = pltpu.SemaphoreType.DMA
        hbm = pl.BlockSpec(memory_space=pltpu.HBM)
        vmem = pl.BlockSpec(memory_space=pltpu.VMEM)
        return pl.pallas_call(
            functools.partial(kernel, Z, N),
            out_shape=jax.ShapeDtypeStruct(frames_in.shape, BF16),
            in_specs=[hbm] * 9,
            out_specs=vmem,
            scratch_shapes=[
                pltpu.VMEM((R, W, S), BF16),
                pltpu.VMEM((Z, hr, 2, W, C), BF16),
                pltpu.VMEM((half, C), BF16),
                pltpu.VMEM((half, C), BF16),
                pltpu.VMEM((half, 1), F32),
                pltpu.VMEM((half, 1), F32),
                pltpu.VMEM((half, C), F32),
                pltpu.VMEM((3, R + 2, W, C), BF16),
                pltpu.VMEM((3, 2, W, C), BF16),
                pltpu.VMEM((hr, W, S), BF16),
                pltpu.VMEM((R, W, S), BF16),
                pltpu.VMEM((3, T + 16, S), F32),
                pltpu.VMEM((C,), BF16),
                pltpu.VMEM((C,), BF16),
                pltpu.VMEM((4, C, C), BF16),
                pltpu.VMEM((C, C), BF16),
                pltpu.VMEM((3, 3, 3, S, C), BF16),
                dma((7,)),
                dma,
                dma((hr,)),
                dma((hr,)),
                dma((2, hr)),
                dma((Z, hr)),
                dma((Z, hr)),
                dma((2,)),
                dma((2,)),
                dma((2,)),
                dma((3, 2)),
                dma((sets,)),
                dma((sets,)),
                dma((sets,)),
                dma((sets,)),
                dma((hops, 4)),
                dma((hops, 4)),
            ],
            compiler_params=pltpu.CompilerParams(
                collective_id=0, has_side_effects=True, vmem_limit_bytes=50 << 20
            ),
        )(*(pltpu.with_memory_space_constraint(a, pltpu.HBM) for a in (
            frames_in, cache, gain_one, gain_two,
            w_query, w_key, w_value, w_out, jnp.swapaxes(conv_weight, 3, 4),
        )))

    return jax.shard_map(
        body,
        mesh=mesh,
        in_specs=(
            P(("clips", "tm"), "space", None, "chan"),
            P("clips", "space", None, None),
            P(),
            P(),
            P(),
            P(),
            P(),
            P(),
            P(None, None, None, None, "chan"),
        ),
        out_specs=P(("clips", "tm"), "space", None, "chan"),
        check_vma=False,
    )
```
